32 devices in a mesh: gx: 8 (over y, x, core), gy: 4 (over z).
Axes of the slice: x: 2, y: 2, z: 4, core: 2. Of those that a mesh axis runs over, the one named last changes fastest.
Arguments:
- state: float32 [54, 64, 4096], P(None, 'gx', 'gy'), may hold values from 0.05 to 3, as said below
- diffusivity: float32 [54], replicated, may hold values from 0.02 to 0.1
- log_prefactor: float32 [325], replicated, may hold values from -1 to 1
- activation: float32 [325], replicated, may hold values from 0.5 to 4
- heat: float32 [325], replicated, may hold values from 0.005 to 0.05
- reactants: float32 [650, 53], replicated, may hold values from 0 to 1, as said below
- products: float32 [53, 325], replicated, may hold values from 0 to 2, as said below
- substeps: int32 [64, 32], P('gx', 'gy'), may hold values from 1 to 4
- flame: int32 [64, 32], P('gx', 'gy'), may hold values from 0 to 1, as said below
Outputs:
- next_state: float32 [54, 64, 4096], P(None, 'gx', 'gy')
The draws below stay inside these ranges and needn't reach their ends.
Inputs may be any that keep to these rules, and one draw needn't show every extreme that they name: `state`: component 0 is the temperature, from 1 to 3; the other components are concentrations from 0.05 to 2. `reactants`: each row is one-hot: it names one species. `products`: column r is the sum of two one-hot columns, the two products of reaction r. `flame`: within the 8 x (8) entries that one device holds, at most 4 are 1. In every draw there is one index along the first mesh axis where every device holds exactly 4; elsewhere a device holds 4 with probability 1/4 and otherwise 0 to 2.
All inputs are finite; a program needn't handle non-finite values.
Results may differ from the reference program's by a relative error of at most 0.0001.
Values sent between devices are 32-bit elements; how exact they have to be, the bound alone decides.
No kernel may reach another device: no remote copies, remote signals or barrier semaphores. Data moves between devices by JAX's collectives and lax.ppermute only.
A program may use at most 128 MiB of HBM per device.

```python
import math
import jax
import jax.numpy as jnp
from jax import lax

SP = 53
RX = 325
COMP = 54
X_DEV = 8
Y_DEV = 32
NZ = 32
BLOCK = 128
MAXSUB = 4
NX = 64
NY = 128
NBY = 32


def draw_state(key, part):
    shape = (SP + 1, NX, NY * NZ)
    uniform = jax.random.uniform(key, shape, jnp.float32)
    first_row = jnp.arange(SP + 1) == 0
    lower = jnp.where(first_row, 1.0, 0.05)[:, None, None]
    upper = jnp.where(first_row, 3.0, 2.0)[:, None, None]
    return jnp.exp(jnp.log(lower) + (jnp.log(upper) - jnp.log(lower)) * uniform)


def draw_reactants(key, part):
    chosen = jax.random.randint(jax.random.fold_in(key, 11), (2 * RX,), 0, SP)
    return (chosen[:, None] == jnp.arange(SP)[None, :]).astype(jnp.float32)


def draw_products(key, part):
    chosen = jax.random.randint(jax.random.fold_in(key, 23), (2, RX), 0, SP)
    species = jnp.arange(SP)[:, None]
    return (species == chosen[0][None, :]).astype(jnp.float32) + (species == chosen[1][None, :]).astype(jnp.float32)


def draw_flame(key, part):
    columns = NX // X_DEV
    rows = NY // Y_DEV
    row_blocks = Y_DEV * NZ // BLOCK
    per_device = X_DEV * row_blocks
    most = rows
    keys = jax.random.split(jax.random.fold_in(key, 37), 4)
    heavy = jax.random.randint(keys[0], (columns, rows), 0, 4) == 0
    light = jnp.minimum(jax.random.randint(keys[1], (columns, rows), 0, 3), most)
    counted = jnp.where(heavy, most, light)
    full_column = jax.random.randint(keys[2], (), 0, columns)
    counted = jnp.where(jnp.arange(columns)[:, None] == full_column, most, counted)
    block_ratings = jax.random.randint(keys[3], (columns, rows, per_device), 0, 65536) * per_device + jnp.arange(per_device)
    ranks = jnp.argsort(jnp.argsort(block_ratings, axis=-1), axis=-1)
    burning = (ranks < counted[..., None]).astype(jnp.int32)
    burning = burning.reshape(columns, rows, X_DEV, row_blocks)
    return jnp.transpose(burning, (0, 2, 1, 3)).reshape(NX, rows * row_blocks)


def place_ends(entries, stream_key, low, high):
    index_at = [jax.random.randint(jax.random.fold_in(stream_key, axis), (), 0, length) for axis, length in enumerate(entries.shape)]
    widest = entries.shape.index(max(entries.shape))
    next_to = index_at[:widest] + [(index_at[widest] + 1) % entries.shape[widest]] + index_at[widest + 1:]
    return entries.at[tuple(index_at)].set(low).at[tuple(next_to)].set(high)


def setup_inputs(seed: int = 0) -> dict:
    key_of = jax.random.split(jax.random.key(seed), 10)
    return {
        "state": draw_state(jax.random.fold_in(key_of[9], 71), 0),
        "diffusivity": jnp.clip(jnp.exp(jax.random.uniform(key_of[1], (COMP,), jnp.float32, math.log(0.02), math.log(0.1))), 0.02, 0.1),
        "log_prefactor": jnp.clip(jax.random.uniform(key_of[2], (RX,), jnp.float32, -1.0, 1.0), -1.0, 1.0),
        "activation": jnp.clip(jnp.exp(jax.random.uniform(key_of[3], (RX,), jnp.float32, math.log(0.5), math.log(4.0))), 0.5, 4.0),
        "heat": jnp.clip(jnp.exp(jax.random.uniform(key_of[4], (RX,), jnp.float32, math.log(0.005), math.log(0.05))), 0.005, 0.05),
        "reactants": draw_reactants(jax.random.fold_in(key_of[9], 71), 0),
        "products": draw_products(jax.random.fold_in(key_of[9], 71), 0),
        "substeps": place_ends(jax.random.randint(key_of[7], (NX, NBY), 1, MAXSUB + 1), jax.random.fold_in(key_of[7], 1), 1, MAXSUB).astype(jnp.int32),
        "flame": draw_flame(jax.random.fold_in(key_of[9], 71), 0),
    }


near_weight = 4.0 / 3.0
far_weight = 1.0 / 12.0
centre_weight = 7.5


def along_z(field, offset, zposition):
    if offset > 0:
        return jnp.where(zposition < NZ - offset, jnp.roll(field, -offset, -1), jnp.roll(field, NZ - offset, -1))
    reach = -offset
    return jnp.where(zposition >= reach, jnp.roll(field, reach, -1), jnp.roll(field, reach - NZ, -1))


def laplacian(field, zposition):
    nearest = jnp.roll(field, 1, 0) + jnp.roll(field, -1, 0)
    nearest = nearest + jnp.roll(field, NZ, 1) + jnp.roll(field, -NZ, 1)
    nearest = nearest + along_z(field, 1, zposition) + along_z(field, -1, zposition)
    farther = jnp.roll(field, 2, 0) + jnp.roll(field, -2, 0)
    farther = farther + jnp.roll(field, 2 * NZ, 1) + jnp.roll(field, -2 * NZ, 1)
    farther = farther + along_z(field, 2, zposition) + along_z(field, -2, zposition)
    return near_weight * nearest - far_weight * farther - centre_weight * field


def react_step(thermal, amounts, step_size, log_prefactor, activation, heat, reactants, products):
    exact_result = lax.Precision.HIGHEST
    nreact = log_prefactor.shape[0]
    speeds = jnp.exp(log_prefactor[:, None] - activation[:, None] / thermal[..., None, :])
    picked = jnp.einsum('qs,...sn->...qn', reactants, amounts, precision=exact_result)
    first_side = picked[..., :nreact, :]
    second_side = picked[..., nreact:, :]
    progress = speeds * first_side * second_side
    produced = jnp.einsum('sr,...rn->...sn', products, progress, precision=exact_result)
    partner = jnp.concatenate([speeds * second_side, speeds * first_side], axis=-2)
    consumed = jnp.einsum('qs,...qn->...sn', reactants, partner, precision=exact_result)
    widened = step_size[..., None, :]
    new_amounts = (amounts + widened * produced) / (1.0 + widened * consumed)
    new_thermal = thermal + step_size * jnp.einsum('r,...rn->...n', heat, progress, precision=exact_result)
    return new_thermal, new_amounts


def reference(state, diffusivity, log_prefactor, activation, heat, reactants, products, substeps, flame):
    components, planes, row_cells = state.shape
    zposition = jnp.arange(row_cells) % NZ
    transport = lax.map(lambda field: laplacian(field, zposition), state) * diffusivity[:, None, None]
    live = (flame * substeps).reshape(-1).astype(jnp.int32)
    block_list = state.reshape(components, -1, BLOCK)

    def per_block(inputs):
        position, count = inputs
        block = lax.dynamic_index_in_dim(block_list, position, 1, keepdims=False)
        step_size = jnp.reshape(1.0 / jnp.maximum(count, 1).astype(jnp.float32), (1,))

        def advance(substep, carry):
            return react_step(carry[0], carry[1], step_size, log_prefactor, activation, heat, reactants, products)

        thermal, amounts = lax.fori_loop(0, count, advance, (block[0], block[1:]))
        return jnp.concatenate([thermal[None], amounts], 0)

    reacted = lax.map(per_block, (jnp.arange(live.shape[0], dtype=jnp.int32), live))
    reacted = jnp.transpose(reacted, (1, 0, 2)).reshape(components, planes, row_cells)
    return reacted + transport
```

```python
import functools

import jax
import jax.numpy as jnp
from jax import lax
from jax.experimental import pallas as pl
from jax.experimental.pallas import tpu as pltpu
from jax.sharding import PartitionSpec as P

NZ = 32
LANES = 128
near_weight = 4.0 / 3.0
far_weight = 1.0 / 12.0
centre_weight = 7.5
LOG2E = 1.4426950408889634
GROUP = 4
FIRST_CHUNK = 34
PIECE = 64

VMEM = pltpu.VMEM
SMEM = pltpu.SMEM


def params(mib):
    return pltpu.CompilerParams(vmem_limit_bytes=mib << 20)


def high_side(parity_flip):
    odd = lax.rem(lax.axis_index("gx"), 2)
    return odd if not parity_flip else 1 - odd


def pack_kernel(comps, planes, tiles, split, s_ref, a0_ref, a1_ref, b_ref, lo_ref, hi_ref):
    rows = planes * tiles
    far_side = high_side(False)
    lane = lax.broadcasted_iota(jnp.int32, (planes, LANES), 1)

    def plane(c, x):
        return s_ref[pl.ds(c * rows + x, tiles, stride=planes), :]

    off_a = far_side * (planes - 2)
    off_b = (1 - far_side) * (planes - 2)
    for c in range(comps):
        for p in range(2):
            if c < split:
                a0_ref[c, p] = plane(c, off_a + p)
            else:
                a1_ref[c - split, p] = plane(c, off_a + p)
    for c in range(comps):
        for p in range(2):
            b_ref[c, p] = plane(c, off_b + p)
    for k in range(comps // 2):
        even, odd = 2 * k * rows, (2 * k + 1) * rows
        last = (tiles - 1) * planes
        first_even = s_ref[even : even + planes, :]
        first_odd = s_ref[odd : odd + planes, :]
        last_even = s_ref[even + last : even + last + planes, :]
        last_odd = s_ref[odd + last : odd + last + planes, :]
        lo_ref[k] = jnp.where(lane < 64, first_even, pltpu.roll(first_odd, 64, 1))
        hi_ref[k] = jnp.where(lane < 64, pltpu.roll(last_even, 64, 1), last_odd)


def split3(value):
    high = value.astype(jnp.bfloat16)
    rest = value - high.astype(jnp.float32)
    middle = rest.astype(jnp.bfloat16)
    low = (rest - middle.astype(jnp.float32)).astype(jnp.bfloat16)
    return high, middle, low


def main_kernel(
    comps,
    planes,
    tiles,
    nreact,
    s_ref,
    d_ref,
    lp_ref,
    act_ref,
    heat_ref,
    rt_ref,
    pr_ref,
    sub_ref,
    flame_ref,
    o_ref,
    q_ref,
    p_ref,
    w1_ref,
    w2_ref,
    a_ref,
    t_ref,
    st_ref,
    pos_ref,
    cnt_ref,
):
    rows = planes * tiles
    species = comps - 1
    block_rows = planes * tiles

    count = jnp.int32(0)
    for x in range(planes):
        for b in range(tiles):
            n = flame_ref[x, b] * sub_ref[x, b]
            pos_ref[count] = b * planes + x
            cnt_ref[count] = n
            count = count + (n > 0).astype(jnp.int32)

    shape = (tiles, planes, LANES)
    lane = lax.broadcasted_iota(jnp.int32, shape, 2)
    z = lax.rem(lane, NZ)
    x = lax.broadcasted_iota(jnp.int32, shape, 1)
    zero = jnp.zeros((1, planes, LANES), jnp.float32)

    def component(c, carry):
        start = pl.multiple_of(c * rows, rows)
        v = s_ref[pl.ds(start, rows), :].reshape(shape)

        def lanes(shift):
            return pltpu.roll(v, shift, 2)

        def up(a):
            return jnp.concatenate([zero, a[:-1]], 0)

        def down(a):
            return jnp.concatenate([a[1:], zero], 0)

        r32, r64, r96 = lanes(32), lanes(64), lanes(96)
        near = jnp.where(lane < 32, up(r32), r32) + jnp.where(lane < 96, r96, down(r96))
        far = r64 + jnp.where(lane < 64, up(r64), down(r64))
        near = near + jnp.where(z < NZ - 1, lanes(LANES - 1), lanes(NZ - 1))
        near = near + jnp.where(z > 0, lanes(1), lanes(LANES - NZ + 1))
        far = far + jnp.where(z < NZ - 2, lanes(LANES - 2), lanes(NZ - 2))
        far = far + jnp.where(z > 1, lanes(2), lanes(LANES - NZ + 2))
        near = near + jnp.where(x > 0, pltpu.roll(v, 1, 1), 0.0)
        near = near + jnp.where(x < planes - 1, pltpu.roll(v, planes - 1, 1), 0.0)
        far = far + jnp.where(x > 1, pltpu.roll(v, 2, 1), 0.0)
        far = far + jnp.where(x < planes - 2, pltpu.roll(v, planes - 2, 1), 0.0)
        out = v + d_ref[c] * (near_weight * near - far_weight * far - centre_weight * v)
        o_ref[pl.ds(start, rows), :] = out.reshape(rows, LANES)
        return carry

    lax.fori_loop(0, comps, component, 0)

    @pl.when(count > 0)
    def _():
        padded = q_ref.shape[1]
        wide = w1_ref.shape[0]
        q_ref[...] = jnp.zeros_like(q_ref)
        p_ref[...] = jnp.zeros_like(p_ref)
        q_ref[0:species, 0:nreact] = rt_ref[:, 0:nreact] + rt_ref[:, nreact : 2 * nreact]
        p_ref[0:species, 0:nreact] = pr_ref[...]
        p_ref[PIECE : PIECE + species, 0:nreact] = q_ref[0:species, 0:nreact]
        for i, piece in enumerate(split3(act_ref[...] * (-LOG2E))):
            q_ref[species + i : species + i + 1, 0:nreact] = piece.astype(jnp.float32)
        for i, piece in enumerate(split3(lp_ref[...] * LOG2E)):
            q_ref[species + 3 + i : species + 4 + i, 0:nreact] = piece.astype(jnp.float32)
        for i, piece in enumerate(split3(heat_ref[...])):
            p_ref[species + i : species + i + 1, 0:nreact] = piece.astype(jnp.float32)
        q = q_ref[...]
        w1 = jnp.transpose(jnp.concatenate([q, q, q], 0))
        w1_ref[...] = w1[0:wide].astype(jnp.bfloat16)
        w = p_ref[...].astype(jnp.bfloat16)
        head, rest = w[:, :256], w[:, 256:padded]
        w2_ref[...] = jnp.concatenate([head, head, rest, rest], 1)

        a_ref[...] = jnp.ones_like(a_ref)
        arow = lax.broadcasted_iota(jnp.int32, a_ref.shape, 0)

        def group(g, carry):
            most = jnp.int32(0)
            pieces = []
            for i in range(GROUP):
                slot = g * GROUP + i
                here = jnp.where(slot < count, slot, 0)
                at = pos_ref[here]
                n = jnp.where(slot < count, cnt_ref[here], 0)
                most = jnp.maximum(most, n)
                cols = slice(i * LANES, (i + 1) * LANES)
                a_ref[0:species, cols] = s_ref[pl.ds(block_rows + at, species, stride=rows), :]
                t_ref[:, cols] = s_ref[pl.ds(at, 1), :]
                pieces.append(jnp.full((1, LANES), n, jnp.int32))
            counts = jnp.concatenate(pieces, 1)
            st_ref[...] = 1.0 / jnp.maximum(counts, 1).astype(jnp.float32)

            def substep(k, inner):
                step = jnp.where(counts > k, st_ref[...], 0.0)
                amounts = a_ref[...]
                thermal = t_ref[...]
                inverse = 1.0 / thermal
                terms = jnp.where(
                    arow < species,
                    jnp.log2(amounts),
                    jnp.where(
                        arow < species + 3, inverse, jnp.where(arow < species + 6, 1.0, 0.0)
                    ),
                )
                rhs = jnp.concatenate(split3(terms), 0)
                exponent = jnp.dot(w1_ref[...], rhs, preferred_element_type=jnp.float32)
                progress = jnp.exp2(exponent)
                high = progress.astype(jnp.bfloat16)
                low = (progress - high.astype(jnp.float32)).astype(jnp.bfloat16)
                gap = 2 * LANES - wide + LANES
                rhs = jnp.concatenate(
                    [high[:256], low[:256], high[256:], high[:gap], low[256:], low[:gap]], 0
                )
                out = jnp.dot(w2_ref[...], rhs, preferred_element_type=jnp.float32)
                produced = out[:PIECE]
                loss = out[PIECE:]
                warm = out[species : species + 1] + (
                    out[species + 1 : species + 2] + out[species + 2 : species + 3]
                )
                a_ref[...] = (amounts + step * produced) * (amounts / (amounts + step * loss))
                t_ref[...] = thermal + step * warm
                return inner

            lax.fori_loop(0, most, substep, 0)

            for i in range(GROUP):
                slot = g * GROUP + i

                @pl.when(slot < count)
                def _(i=i, slot=slot):
                    at = pos_ref[slot]
                    cols = slice(i * LANES, (i + 1) * LANES)
                    where = pl.ds(block_rows + at, species, stride=rows)
                    o_ref[where, :] = o_ref[where, :] + (a_ref[0:species, cols] - s_ref[where, :])
                    top = pl.ds(at, 1)
                    o_ref[top, :] = o_ref[top, :] + (t_ref[:, cols] - s_ref[top, :])

            return carry

        lax.fori_loop(0, (count + (GROUP - 1)) // GROUP, group, 0)


def edge_kernel(
    planes, tiles, begin, size, part_ref, d_ref, ha_ref, hb_ref, zl_ref, zh_ref, *rest
):
    out_hbm, work, sem = rest[-3:]
    rows = planes * tiles
    lane = lax.broadcasted_iota(jnp.int32, (planes, LANES), 1)
    side_a = high_side(False)
    side_b = 1 - side_a
    copies = []
    step = 2
    quarter = max(step, (size // 4) // step * step)

    def add_plane(c, base, h_ref, index, side):
        weight = d_ref[c]
        near = h_ref[index, 1 - side]
        far = h_ref[index, side]
        first = pl.ds(base + side * (planes - 1), tiles, stride=planes)
        second = pl.ds(base + 1 + side * (planes - 3), tiles, stride=planes)
        work[first, :] = work[first, :] + weight * (near_weight * near - far_weight * far)
        work[second, :] = work[second, :] - weight * (far_weight * near)

    done = 0
    for i in range(0, size, step):
        for j in range(step):
            c = begin + i + j
            base = (i + j) * rows
            work[base : base + rows, :] = part_ref[c * rows : (c + 1) * rows, :]
            add_plane(c, base, ha_ref, i + j, side_a)
            add_plane(c, base, hb_ref, c, side_b)
        k = (begin + i) // 2
        low = zl_ref[k]
        high = zh_ref[k]
        low = near_weight * jnp.where(lane % 64 < NZ, pltpu.roll(low, LANES - NZ, 1), 0.0) - (
            far_weight * low
        )
        high = near_weight * jnp.where(lane % 64 >= NZ, pltpu.roll(high, NZ, 1), 0.0) - (
            far_weight * high
        )
        last = (tiles - 1) * planes
        for j in range(step):
            base = (i + j) * rows
            weight = d_ref[begin + i + j]
            mine_low = low if j == 0 else pltpu.roll(low, 64, 1)
            mine_high = high if j == 1 else pltpu.roll(high, 64, 1)
            top = slice(base, base + planes)
            work[top, :] = work[top, :] + jnp.where(lane < 64, weight * mine_low, 0.0)
            end = slice(base + last, base + last + planes)
            work[end, :] = work[end, :] + jnp.where(lane >= 64, weight * mine_high, 0.0)
        now = i + step
        if now - done >= quarter or now == size:
            copy = pltpu.make_async_copy(
                work.at[pl.ds(done * rows, (now - done) * rows), :],
                out_hbm.at[pl.ds((begin + done) * rows, (now - done) * rows), :],
                sem.at[len(copies)],
            )
            copy.start()
            copies.append(copy)
            done = now
    for copy in copies:
        copy.wait()


def per_device(
    state, diffusivity, log_prefactor, activation, heat, reactants, products, substeps, flame
):
    comps, planes, cells = state.shape
    tiles = cells // LANES
    rows = planes * tiles
    nreact = log_prefactor.shape[0]
    split = FIRST_CHUNK
    gx, gy = lax.axis_size("gx"), lax.axis_size("gy")
    f32 = jnp.float32
    flat = (
        state.reshape(comps, planes, tiles, LANES)
        .transpose(0, 2, 1, 3)
        .reshape(comps * rows, LANES)
    )
    vmem = pl.BlockSpec(memory_space=VMEM)
    smem = pl.BlockSpec(memory_space=SMEM)
    anywhere = pl.BlockSpec(memory_space=pl.ANY)

    sds = jax.ShapeDtypeStruct
    a0, a1, b, lo, hi = pl.pallas_call(
        functools.partial(pack_kernel, comps, planes, tiles, split),
        out_shape=(
            sds((split, 2, tiles, LANES), f32),
            sds((comps - split, 2, tiles, LANES), f32),
            sds((comps, 2, tiles, LANES), f32),
            sds((comps // 2, planes, LANES), f32),
            sds((comps // 2, planes, LANES), f32),
        ),
        in_specs=[vmem],
        out_specs=[vmem] * 5,
        compiler_params=params(16),
        name="pack",
    )(flat)

    outer = [(i, (i + 1) % gx) for i in range(1, gx, 2)]
    outer = outer + [(t, s) for s, t in outer]
    inner = [(i, i + 1) for i in range(0, gx, 2)]
    inner = inner + [(t, s) for s, t in inner]
    forward = [(i, (i + 1) % gy) for i in range(gy)]
    backward = [(t, s) for s, t in forward]
    ha0 = lax.ppermute(a0, "gx", outer)
    ha1 = lax.ppermute(a1, "gx", outer)
    hb = lax.ppermute(b, "gx", inner)
    zl = lax.ppermute(hi, "gy", forward)
    zh = lax.ppermute(lo, "gy", backward)

    padded = pl.cdiv(nreact, LANES) * LANES
    wide = pl.cdiv(nreact, 16) * 16
    part = pl.pallas_call(
        functools.partial(main_kernel, comps, planes, tiles, nreact),
        out_shape=sds((comps * rows, LANES), f32),
        in_specs=[vmem, smem, vmem, vmem, vmem, vmem, vmem, smem, smem],
        out_specs=vmem,
        scratch_shapes=[
            VMEM((PIECE, padded), f32),
            VMEM((2 * PIECE, padded), f32),
            VMEM((wide, 3 * PIECE), jnp.bfloat16),
            VMEM((2 * PIECE, 2 * padded), jnp.bfloat16),
            VMEM((PIECE, GROUP * LANES), f32),
            VMEM((1, GROUP * LANES), f32),
            VMEM((1, GROUP * LANES), f32),
            SMEM((rows + 1,), jnp.int32),
            SMEM((rows + 1,), jnp.int32),
        ],
        compiler_params=params(24),
        cost_estimate=pl.CostEstimate(
            flops=2_000_000_000, bytes_accessed=16_000_000, transcendentals=1_000_000
        ),
        name="main",
    )(
        flat,
        diffusivity,
        log_prefactor.reshape(1, nreact),
        activation.reshape(1, nreact),
        heat.reshape(1, nreact),
        reactants.T,
        products,
        substeps,
        flame,
    )

    def edges(begin, size, halo, previous):
        extra = [] if previous is None else [previous]
        return pl.pallas_call(
            functools.partial(edge_kernel, planes, tiles, begin, size),
            out_shape=sds((comps * rows, LANES), f32),
            in_specs=[vmem, smem, vmem, vmem, vmem, vmem] + [anywhere] * len(extra),
            out_specs=anywhere,
            scratch_shapes=[VMEM((size * rows, LANES), f32), pltpu.SemaphoreType.DMA((8,))],
            input_output_aliases={6: 0} if extra else {},
            compiler_params=params(16),
            cost_estimate=pl.CostEstimate(
                flops=1_000_000, bytes_accessed=3_000_000, transcendentals=0
            ),
            name="edges",
        )(part, diffusivity, halo, hb, zl, zh, *extra)

    out = edges(0, split, ha0, None)
    out = edges(split, comps - split, ha1, out)
    return (
        out.reshape(comps, tiles, planes, LANES).transpose(0, 2, 1, 3).reshape(comps, planes, cells)
    )


def solution(mesh):
    in_specs = (P(None, "gx", "gy"), P(), P(), P(), P(), P(), P(), P("gx", "gy"), P("gx", "gy"))
    out_specs = P(None, "gx", "gy")
    return jax.shard_map(
        per_device, mesh=mesh, in_specs=in_specs, out_specs=out_specs, check_vma=False
    )
```

```python
import functools

import jax
import jax.numpy as jnp
import numpy as np
from jax import lax
from jax.experimental import pallas as pl
from jax.experimental.pallas import tpu as pltpu
from jax.sharding import PartitionSpec as P

NZ = 32
LANES = 128
near_weight = 4.0 / 3.0
far_weight = 1.0 / 12.0
LOG2E = 1.4426950408889634
GROUP = 4
FIRST_CHUNK = 34
PIECE = 64

VMEM = pltpu.VMEM
SMEM = pltpu.SMEM


def params(mib):
    return pltpu.CompilerParams(vmem_limit_bytes=mib << 20)


def high_side(parity_flip):
    odd = lax.rem(lax.axis_index("gx"), 2)
    return odd if not parity_flip else 1 - odd


def pack_kernel(comps, planes, tiles, split, s_ref, a0_ref, a1_ref, b_ref, lo_ref, hi_ref):
    rows = planes * tiles
    far_side = high_side(False)
    lane = lax.broadcasted_iota(jnp.int32, (planes, LANES), 1)

    def plane(c, x):
        return s_ref[pl.ds(c * rows + x, tiles, stride=planes), :]

    off_a = far_side * (planes - 2)
    off_b = (1 - far_side) * (planes - 2)
    for c in range(comps):
        for p in range(2):
            if c < split:
                a0_ref[c, p] = plane(c, off_a + p)
            else:
                a1_ref[c - split, p] = plane(c, off_a + p)
    for c in range(comps):
        for p in range(2):
            b_ref[c, p] = plane(c, off_b + p)
    for k in range(comps // 2):
        even, odd = 2 * k * rows, (2 * k + 1) * rows
        last = (tiles - 1) * planes
        first_even = s_ref[even : even + planes, :]
        first_odd = s_ref[odd : odd + planes, :]
        last_even = s_ref[even + last : even + last + planes, :]
        last_odd = s_ref[odd + last : odd + last + planes, :]
        lo_ref[k] = jnp.where(lane < 64, first_even, pltpu.roll(first_odd, 64, 1))
        hi_ref[k] = jnp.where(lane < 64, pltpu.roll(last_even, 64, 1), last_odd)


def split3(value):
    high = value.astype(jnp.bfloat16)
    rest = value - high.astype(jnp.float32)
    middle = rest.astype(jnp.bfloat16)
    low = (rest - middle.astype(jnp.float32)).astype(jnp.bfloat16)
    return high, middle, low


def main_kernel(
    comps,
    planes,
    tiles,
    nreact,
    s_ref,
    d_ref,
    shift_ref,
    lp_hbm,
    act_hbm,
    heat_hbm,
    rt_hbm,
    pr_hbm,
    sub_ref,
    flame_ref,
    o_ref,
    lp_ref,
    act_ref,
    heat_ref,
    rt_ref,
    pr_ref,
    q_ref,
    p_ref,
    w1_ref,
    w2_ref,
    a_ref,
    t_ref,
    st_ref,
    pos_ref,
    sem,
):
    rows = planes * tiles
    species = comps - 1
    block_rows = planes * tiles
    loads = [
        pltpu.make_async_copy(source, target, sem.at[i])
        for i, (source, target) in enumerate(
            (
                (lp_hbm, lp_ref),
                (act_hbm, act_ref),
                (heat_hbm, heat_ref),
                (rt_hbm, rt_ref),
                (pr_hbm, pr_ref),
            )
        )
    ]
    for load in loads:
        load.start()

    count = jnp.int32(0)
    for x in range(planes):
        for b in range(tiles):
            pos_ref[count] = b * planes + x
            count = count + flame_ref[x, b]

    many = max(n for n in range(1, 7) if comps % n == 0)
    shape = (many, tiles, planes, LANES)
    lane = lax.broadcasted_iota(jnp.int32, (1, 1, planes, LANES), 3)
    x = lax.broadcasted_iota(jnp.int32, (1, 1, planes, LANES), 2)
    zero = jnp.zeros((many, 1, planes, LANES), jnp.float32)
    near, far = near_weight * 12.0, -far_weight * 12.0
    up1 = jnp.where(x > 0, near, 0.0)
    down1 = jnp.where(x < planes - 1, near, 0.0)
    up2 = jnp.where(x > 1, far, 0.0)
    down2 = jnp.where(x < planes - 2, far, 0.0)
    shifts = shift_ref[...]

    def components(i, carry):
        start = pl.multiple_of(i * many * rows, many * rows)
        flat = s_ref[pl.ds(start, many * rows), :]
        high = flat.astype(jnp.bfloat16)
        low = (flat - high.astype(jnp.float32)).astype(jnp.bfloat16)
        both = jnp.concatenate([high, low], 1)
        out = jnp.dot(both, shifts, preferred_element_type=jnp.float32)
        v = flat.reshape(shape)
        own = out[:, :LANES].reshape(shape)
        cross = out[:, LANES:].reshape(shape)
        before = jnp.concatenate([zero, cross[:, :-1]], 1)
        after = jnp.concatenate([cross[:, 1:], zero], 1)
        own = own + jnp.where(lane < 64, before, after)
        own = own + (pltpu.roll(v, 1, 2) * up1 + pltpu.roll(v, planes - 1, 2) * down1)
        own = own + (pltpu.roll(v, 2, 2) * up2 + pltpu.roll(v, planes - 2, 2) * down2)
        for j in range(many):
            where = pl.ds(pl.multiple_of(start + j * rows, rows), rows)
            scale = d_ref[i * many + j] * (1.0 / 12.0)
            o_ref[where, :] = (v[j] + scale * own[j]).reshape(rows, LANES)
        return carry

    lax.fori_loop(0, comps // many, components, 0)
    for load in loads:
        load.wait()

    @pl.when(count > 0)
    def _():
        padded = q_ref.shape[1]
        wide = w1_ref.shape[0]
        q_ref[...] = jnp.zeros_like(q_ref)
        p_ref[...] = jnp.zeros_like(p_ref)
        q_ref[0:species, 0:nreact] = rt_ref[:, 0:nreact] + rt_ref[:, nreact : 2 * nreact]
        p_ref[0:species, 0:nreact] = pr_ref[...]
        p_ref[PIECE : PIECE + species, 0:nreact] = q_ref[0:species, 0:nreact]
        for i, piece in enumerate(split3(act_ref[...].reshape(1, nreact) * (-LOG2E))):
            q_ref[species + i : species + i + 1, 0:nreact] = piece.astype(jnp.float32)
        for i, piece in enumerate(split3(lp_ref[...].reshape(1, nreact) * LOG2E)):
            q_ref[species + 3 + i : species + 4 + i, 0:nreact] = piece.astype(jnp.float32)
        for i, piece in enumerate(split3(heat_ref[...].reshape(1, nreact))):
            p_ref[species + i : species + i + 1, 0:nreact] = piece.astype(jnp.float32)
        q = q_ref[...]
        w1 = jnp.transpose(jnp.concatenate([q, q, q], 0))
        w1_ref[...] = w1[0:wide].astype(jnp.bfloat16)
        w = p_ref[...].astype(jnp.bfloat16)
        head, rest = w[:, :256], w[:, 256:padded]
        w2_ref[...] = jnp.concatenate([head, head, rest, rest], 1)

        a_ref[...] = jnp.ones_like(a_ref)
        arow = lax.broadcasted_iota(jnp.int32, a_ref.shape, 0)

        def group(g, carry):
            most = jnp.int32(0)
            pieces = []
            for i in range(GROUP):
                slot = g * GROUP + i
                here = jnp.where(slot < count, slot, 0)
                at = pos_ref[here]
                n = jnp.where(
                    slot < count, sub_ref[lax.rem(at, planes), lax.div(at, planes)], 0
                )
                most = jnp.maximum(most, n)
                cols = slice(i * LANES, (i + 1) * LANES)
                a_ref[0:species, cols] = s_ref[pl.ds(block_rows + at, species, stride=rows), :]
                t_ref[:, cols] = s_ref[pl.ds(at, 1), :]
                pieces.append(jnp.full((1, LANES), n, jnp.int32))
            counts = jnp.concatenate(pieces, 1)
            st_ref[...] = 1.0 / jnp.maximum(counts, 1).astype(jnp.float32)

            def substep(k, inner):
                step = jnp.where(counts > k, st_ref[...], 0.0)
                amounts = a_ref[...]
                thermal = t_ref[...]
                inverse = 1.0 / thermal
                terms = jnp.where(
                    arow < species,
                    jnp.log2(amounts),
                    jnp.where(
                        arow < species + 3, inverse, jnp.where(arow < species + 6, 1.0, 0.0)
                    ),
                )
                rhs = jnp.concatenate(split3(terms), 0)
                exponent = jnp.dot(w1_ref[...], rhs, preferred_element_type=jnp.float32)
                progress = jnp.exp2(exponent)
                high = progress.astype(jnp.bfloat16)
                low = (progress - high.astype(jnp.float32)).astype(jnp.bfloat16)
                gap = 2 * LANES - wide + LANES
                rhs = jnp.concatenate(
                    [high[:256], low[:256], high[256:], high[:gap], low[256:], low[:gap]], 0
                )
                out = jnp.dot(w2_ref[...], rhs, preferred_element_type=jnp.float32)
                produced = out[:PIECE]
                loss = out[PIECE:]
                warm = out[species : species + 1] + (
                    out[species + 1 : species + 2] + out[species + 2 : species + 3]
                )
                a_ref[...] = (amounts + step * produced) * (amounts / (amounts + step * loss))
                t_ref[...] = thermal + step * warm
                return inner

            lax.fori_loop(0, most, substep, 0)

            for i in range(GROUP):
                slot = g * GROUP + i

                @pl.when(slot < count)
                def _(i=i, slot=slot):
                    at = pos_ref[slot]
                    cols = slice(i * LANES, (i + 1) * LANES)
                    where = pl.ds(block_rows + at, species, stride=rows)
                    o_ref[where, :] = o_ref[where, :] + (a_ref[0:species, cols] - s_ref[where, :])
                    top = pl.ds(at, 1)
                    o_ref[top, :] = o_ref[top, :] + (t_ref[:, cols] - s_ref[top, :])

            return carry

        lax.fori_loop(0, (count + (GROUP - 1)) // GROUP, group, 0)


def add_plane(planes, tiles, work, weight, c, h_ref, index, side):
    rows = planes * tiles
    near = h_ref[index, 1 - side]
    far = h_ref[index, side]
    first = pl.ds(c * rows + side * (planes - 1), tiles, stride=planes)
    second = pl.ds(c * rows + 1 + side * (planes - 3), tiles, stride=planes)
    work[first, :] = work[first, :] + weight * (near_weight * near - far_weight * far)
    work[second, :] = work[second, :] - weight * (far_weight * near)


def send_out(rows, begin, end, work, out_hbm, sem):
    where = pl.ds(begin * rows, (end - begin) * rows)
    copy = pltpu.make_async_copy(work.at[where, :], out_hbm.at[where, :], sem)
    copy.start()
    return copy


def inner_edges_kernel(
    comps, planes, tiles, split, part_ref, d_ref, ha_ref, hb_ref, zl_ref, zh_ref, work, out, sem
):
    rows = planes * tiles
    lane = lax.broadcasted_iota(jnp.int32, (planes, LANES), 1)
    side_a = high_side(False)
    side_b = 1 - side_a
    last = (tiles - 1) * planes
    copies = []
    done = 0
    for k in range(comps // 2):
        low = zl_ref[k]
        high = zh_ref[k]
        low = near_weight * jnp.where(lane % 64 < NZ, pltpu.roll(low, LANES - NZ, 1), 0.0) - (
            far_weight * low
        )
        high = near_weight * jnp.where(lane % 64 >= NZ, pltpu.roll(high, NZ, 1), 0.0) - (
            far_weight * high
        )
        other_low = pltpu.roll(low, 64, 1)
        other_high = pltpu.roll(high, 64, 1)
        for j in range(2):
            c = 2 * k + j
            weight = d_ref[c]
            mine_low = low if j == 0 else other_low
            mine_high = high if j == 1 else other_high
            top = slice(c * rows, c * rows + planes)
            work[top, :] = work[top, :] + jnp.where(lane < 64, weight * mine_low, 0.0)
            end = slice(c * rows + last, c * rows + last + planes)
            work[end, :] = work[end, :] + jnp.where(lane >= 64, weight * mine_high, 0.0)
            add_plane(planes, tiles, work, weight, c, hb_ref, c, side_b)
            if c < split:
                add_plane(planes, tiles, work, weight, c, ha_ref, c, side_a)
        now = 2 * k + 2
        if now <= split and (now - done >= 10 or now == split):
            copies.append(send_out(rows, done, now, work, out, sem.at[len(copies)]))
            done = now
    for copy in copies:
        copy.wait()


def outer_edges_kernel(comps, planes, tiles, split, part_ref, d_ref, ha_ref, prev, work, out, sem):
    rows = planes * tiles
    side = high_side(False)
    copies = []
    done = split
    for c in range(split, comps):
        add_plane(planes, tiles, work, d_ref[c], c, ha_ref, c - split, side)
        now = c + 1
        if now - done >= 5 or now == comps:
            copies.append(send_out(rows, done, now, work, out, sem.at[len(copies)]))
            done = now
    for copy in copies:
        copy.wait()


def shift_matrix():
    source = np.arange(LANES)[:, None]
    target = np.arange(LANES)[None, :]
    weights = {1: 16.0, 2: -1.0}
    ys, yt, zs, zt = source // NZ, target // NZ, source % NZ, target % NZ
    rows = LANES // NZ
    own = np.where(source == target, -90.0, 0.0)
    cross = np.zeros_like(own)
    for distance, weight in weights.items():
        turn = (zt - zs) % NZ
        own += np.where((ys == yt) & ((turn == distance) | (turn == NZ - distance)), weight, 0.0)
        own += np.where((zs == zt) & (abs(yt - ys) == distance), weight, 0.0)
        to_next = (target < 64) & (zs == zt) & (yt + rows - ys == distance)
        to_previous = (target >= 64) & (zs == zt) & (ys + rows - yt == distance)
        cross += np.where(to_next | to_previous, weight, 0.0)
    one = np.concatenate([own, cross], 1)
    return jnp.asarray(np.concatenate([one, one], 0), jnp.bfloat16)


def per_device(
    state, diffusivity, log_prefactor, activation, heat, reactants, products, substeps, flame
):
    comps, planes, cells = state.shape
    tiles = cells // LANES
    rows = planes * tiles
    nreact = log_prefactor.shape[0]
    split = FIRST_CHUNK
    gx, gy = lax.axis_size("gx"), lax.axis_size("gy")
    f32 = jnp.float32
    flat = (
        state.reshape(comps, planes, tiles, LANES)
        .transpose(0, 2, 1, 3)
        .reshape(comps * rows, LANES)
    )
    vmem = pl.BlockSpec(memory_space=VMEM)
    smem = pl.BlockSpec(memory_space=SMEM)
    anywhere = pl.BlockSpec(memory_space=pl.ANY)

    sds = jax.ShapeDtypeStruct
    a0, a1, b, lo, hi = pl.pallas_call(
        functools.partial(pack_kernel, comps, planes, tiles, split),
        out_shape=(
            sds((split, 2, tiles, LANES), f32),
            sds((comps - split, 2, tiles, LANES), f32),
            sds((comps, 2, tiles, LANES), f32),
            sds((comps // 2, planes, LANES), f32),
            sds((comps // 2, planes, LANES), f32),
        ),
        in_specs=[vmem],
        out_specs=[vmem] * 5,
        compiler_params=params(16),
        name="pack",
    )(flat)

    outer = [(i, (i + 1) % gx) for i in range(1, gx, 2)]
    outer = outer + [(t, s) for s, t in outer]
    inner = [(i, i + 1) for i in range(0, gx, 2)]
    inner = inner + [(t, s) for s, t in inner]
    forward = [(i, (i + 1) % gy) for i in range(gy)]
    backward = [(t, s) for s, t in forward]
    ha0 = lax.ppermute(a0, "gx", outer)
    ha1 = lax.ppermute(a1, "gx", outer)
    hb = lax.ppermute(b, "gx", inner)
    zl = lax.ppermute(hi, "gy", forward)
    zh = lax.ppermute(lo, "gy", backward)

    padded = pl.cdiv(nreact, LANES) * LANES
    wide = pl.cdiv(nreact, 16) * 16
    part = pl.pallas_call(
        functools.partial(main_kernel, comps, planes, tiles, nreact),
        out_shape=sds((comps * rows, LANES), f32),
        in_specs=[vmem, smem, vmem] + [anywhere] * 5 + [smem, smem],
        out_specs=vmem,
        scratch_shapes=[
            VMEM((nreact,), f32),
            VMEM((nreact,), f32),
            VMEM((nreact,), f32),
            VMEM((comps - 1, 2 * nreact), f32),
            VMEM((comps - 1, nreact), f32),
            VMEM((PIECE, padded), f32),
            VMEM((2 * PIECE, padded), f32),
            VMEM((wide, 3 * PIECE), jnp.bfloat16),
            VMEM((2 * PIECE, 2 * padded), jnp.bfloat16),
            VMEM((PIECE, GROUP * LANES), f32),
            VMEM((1, GROUP * LANES), f32),
            VMEM((1, GROUP * LANES), f32),
            SMEM((rows + 1,), jnp.int32),
            pltpu.SemaphoreType.DMA((5,)),
        ],
        compiler_params=params(24),
        cost_estimate=pl.CostEstimate(
            flops=2_000_000_000, bytes_accessed=16_000_000, transcendentals=1_000_000
        ),
        name="main",
    )(
        flat,
        diffusivity,
        shift_matrix(),
        log_prefactor,
        activation,
        heat,
        reactants.T,
        products,
        substeps,
        flame,
    )

    whole = sds((comps * rows, LANES), f32)
    cost = pl.CostEstimate(flops=1_000_000, bytes_accessed=3_000_000, transcendentals=0)
    part, out = pl.pallas_call(
        functools.partial(inner_edges_kernel, comps, planes, tiles, split),
        out_shape=(whole, whole),
        in_specs=[vmem, smem, vmem, vmem, vmem, vmem],
        out_specs=(vmem, anywhere),
        scratch_shapes=[pltpu.SemaphoreType.DMA((8,))],
        input_output_aliases={0: 0},
        compiler_params=params(16),
        cost_estimate=cost,
        name="inner_edges",
    )(part, diffusivity, ha0, hb, zl, zh)
    part, out = pl.pallas_call(
        functools.partial(outer_edges_kernel, comps, planes, tiles, split),
        out_shape=(whole, whole),
        in_specs=[vmem, smem, vmem, anywhere],
        out_specs=(vmem, anywhere),
        scratch_shapes=[pltpu.SemaphoreType.DMA((8,))],
        input_output_aliases={0: 0, 3: 1},
        compiler_params=params(16),
        cost_estimate=cost,
        name="outer_edges",
    )(part, diffusivity, ha1, out)
    return (
        out.reshape(comps, tiles, planes, LANES).transpose(0, 2, 1, 3).reshape(comps, planes, cells)
    )


def solution(mesh):
    in_specs = (P(None, "gx", "gy"), P(), P(), P(), P(), P(), P(), P("gx", "gy"), P("gx", "gy"))
    out_specs = P(None, "gx", "gy")

    return jax.shard_map(
        per_device, mesh=mesh, in_specs=in_specs, out_specs=out_specs, check_vma=False
    )
```

```python
import functools

import jax
import jax.numpy as jnp
import numpy as np
from jax import lax
from jax.experimental import pallas as pl
from jax.experimental.pallas import tpu as pltpu
from jax.sharding import PartitionSpec as P

NZ = 32
LANES = 128
near_weight = 4.0 / 3.0
far_weight = 1.0 / 12.0
LOG2E = 1.4426950408889634
GROUP = 4
PIECE = 64

VMEM = pltpu.VMEM
SMEM = pltpu.SMEM


def params(mib):
    return pltpu.CompilerParams(vmem_limit_bytes=mib << 20)


def odd_place(axis):
    return lax.rem(lax.axis_index(axis), 2)


def outer_kernel(comps, planes, tiles, s_hbm, o_ref, sem):
    pair = odd_place("gx") * (planes // 2 - 1)
    total = comps * tiles
    parts = 6
    copies = []
    for i in range(parts):
        begin, end = total * i // parts, total * (i + 1) // parts
        where = pl.ds(begin, end - begin)
        copies.append(
            pltpu.make_async_copy(s_hbm.at[where, pair], o_ref.at[where], sem.at[i])
        )
        copies[-1].start()
    for copy in copies:
        copy.wait()


def pack_kernel(comps, planes, tiles, s_ref, b_ref, first_ref, second_ref):
    rows = planes * tiles
    odd = odd_place("gy")
    lane = lax.broadcasted_iota(jnp.int32, (planes, LANES), 1)
    off_b = (1 - odd_place("gx")) * (planes - 2)
    for c in range(comps):
        for p in range(2):
            b_ref[c, p] = s_ref[pl.ds(c * rows + off_b + p, tiles, stride=planes), :]
    swap = jnp.broadcast_to(odd, (planes, LANES)) == 1
    last = (tiles - 1) * planes
    for k in range(comps // 2):
        first, second = 2 * k * rows, (2 * k + 1) * rows
        low_a = s_ref[first : first + planes, :]
        low_b = s_ref[second : second + planes, :]
        high_a = s_ref[first + last : first + last + planes, :]
        high_b = s_ref[second + last : second + last + planes, :]
        low = jnp.where(lane < 64, low_a, pltpu.roll(low_b, 64, 1))
        high = jnp.where(lane < 64, pltpu.roll(high_a, 64, 1), high_b)
        first_ref[k] = jnp.where(swap, low, high)
        second_ref[k] = jnp.where(swap, high, low)


def split3(value):
    high = value.astype(jnp.bfloat16)
    rest = value - high.astype(jnp.float32)
    middle = rest.astype(jnp.bfloat16)
    low = (rest - middle.astype(jnp.float32)).astype(jnp.bfloat16)
    return high, middle, low


def main_kernel(
    comps,
    planes,
    tiles,
    nreact,
    s_ref,
    d_ref,
    shift_ref,
    lp_hbm,
    act_hbm,
    heat_hbm,
    rt_hbm,
    pr_hbm,
    sub_ref,
    flame_ref,
    o_ref,
    lp_ref,
    act_ref,
    heat_ref,
    rt_ref,
    pr_ref,
    q_ref,
    p_ref,
    w1_ref,
    w2_ref,
    a_ref,
    t_ref,
    st_ref,
    pos_ref,
    sem,
):
    rows = planes * tiles
    species = comps - 1
    block_rows = planes * tiles
    loads = [
        pltpu.make_async_copy(source, target, sem.at[i])
        for i, (source, target) in enumerate(
            (
                (lp_hbm, lp_ref),
                (act_hbm, act_ref),
                (heat_hbm, heat_ref),
                (rt_hbm, rt_ref),
                (pr_hbm, pr_ref),
            )
        )
    ]
    for load in loads:
        load.start()

    count = jnp.int32(0)
    for x in range(planes):
        for b in range(tiles):
            pos_ref[count] = b * planes + x
            count = count + flame_ref[x, b]

    many = max(n for n in range(1, 7) if comps % n == 0)
    shape = (many, tiles, planes, LANES)
    lane = lax.broadcasted_iota(jnp.int32, (1, 1, planes, LANES), 3)
    x = lax.broadcasted_iota(jnp.int32, (1, 1, planes, LANES), 2)
    zero = jnp.zeros((many, 1, planes, LANES), jnp.float32)
    near, far = near_weight * 12.0, -far_weight * 12.0
    up1 = jnp.where(x > 0, near, 0.0)
    down1 = jnp.where(x < planes - 1, near, 0.0)
    up2 = jnp.where(x > 1, far, 0.0)
    down2 = jnp.where(x < planes - 2, far, 0.0)
    shifts = shift_ref[...]

    def components(i, carry):
        start = pl.multiple_of(i * many * rows, many * rows)
        flat = s_ref[pl.ds(start, many * rows), :]
        high = flat.astype(jnp.bfloat16)
        low = (flat - high.astype(jnp.float32)).astype(jnp.bfloat16)
        both = jnp.concatenate([high, low], 1)
        out = jnp.dot(both, shifts, preferred_element_type=jnp.float32)
        v = flat.reshape(shape)
        own = out[:, :LANES].reshape(shape)
        cross = out[:, LANES:].reshape(shape)
        before = jnp.concatenate([zero, cross[:, :-1]], 1)
        after = jnp.concatenate([cross[:, 1:], zero], 1)
        own = own + jnp.where(lane < 64, before, after)
        own = own + (pltpu.roll(v, 1, 2) * up1 + pltpu.roll(v, planes - 1, 2) * down1)
        own = own + (pltpu.roll(v, 2, 2) * up2 + pltpu.roll(v, planes - 2, 2) * down2)
        for j in range(many):
            where = pl.ds(pl.multiple_of(start + j * rows, rows), rows)
            scale = d_ref[i * many + j] * (1.0 / 12.0)
            o_ref[where, :] = (v[j] + scale * own[j]).reshape(rows, LANES)
        return carry

    lax.fori_loop(0, comps // many, components, 0)
    for load in loads:
        load.wait()

    @pl.when(count > 0)
    def _():
        padded = q_ref.shape[1]
        wide = w1_ref.shape[0]
        q_ref[...] = jnp.zeros_like(q_ref)
        p_ref[...] = jnp.zeros_like(p_ref)
        q_ref[0:species, 0:nreact] = rt_ref[:, 0:nreact] + rt_ref[:, nreact : 2 * nreact]
        p_ref[0:species, 0:nreact] = pr_ref[...]
        p_ref[PIECE : PIECE + species, 0:nreact] = q_ref[0:species, 0:nreact]
        for i, piece in enumerate(split3(act_ref[...].reshape(1, nreact) * (-LOG2E))):
            q_ref[species + i : species + i + 1, 0:nreact] = piece.astype(jnp.float32)
        for i, piece in enumerate(split3(lp_ref[...].reshape(1, nreact) * LOG2E)):
            q_ref[species + 3 + i : species + 4 + i, 0:nreact] = piece.astype(jnp.float32)
        for i, piece in enumerate(split3(heat_ref[...].reshape(1, nreact))):
            p_ref[species + i : species + i + 1, 0:nreact] = piece.astype(jnp.float32)
        q = q_ref[...]
        w1 = jnp.transpose(jnp.concatenate([q, q, q], 0))
        w1_ref[...] = w1[0:wide].astype(jnp.bfloat16)
        w = p_ref[...].astype(jnp.bfloat16)
        head, rest = w[:, :256], w[:, 256:padded]
        w2_ref[...] = jnp.concatenate([head, head, rest, rest], 1)

        a_ref[...] = jnp.ones_like(a_ref)
        arow = lax.broadcasted_iota(jnp.int32, a_ref.shape, 0)

        def group(g, carry):
            most = jnp.int32(0)
            pieces = []
            for i in range(GROUP):
                slot = g * GROUP + i
                here = jnp.where(slot < count, slot, 0)
                at = pos_ref[here]
                n = jnp.where(
                    slot < count, sub_ref[lax.rem(at, planes), lax.div(at, planes)], 0
                )
                most = jnp.maximum(most, n)
                cols = slice(i * LANES, (i + 1) * LANES)
                a_ref[0:species, cols] = s_ref[pl.ds(block_rows + at, species, stride=rows), :]
                t_ref[:, cols] = s_ref[pl.ds(at, 1), :]
                pieces.append(jnp.full((1, LANES), n, jnp.int32))
            counts = jnp.concatenate(pieces, 1)
            st_ref[...] = 1.0 / jnp.maximum(counts, 1).astype(jnp.float32)

            def substep(k, inner):
                step = jnp.where(counts > k, st_ref[...], 0.0)
                amounts = a_ref[...]
                thermal = t_ref[...]
                inverse = 1.0 / thermal
                terms = jnp.where(
                    arow < species,
                    jnp.log2(amounts),
                    jnp.where(
                        arow < species + 3, inverse, jnp.where(arow < species + 6, 1.0, 0.0)
                    ),
                )
                rhs = jnp.concatenate(split3(terms), 0)
                exponent = jnp.dot(w1_ref[...], rhs, preferred_element_type=jnp.float32)
                progress = jnp.exp2(exponent)
                high = progress.astype(jnp.bfloat16)
                low = (progress - high.astype(jnp.float32)).astype(jnp.bfloat16)
                gap = 2 * LANES - wide + LANES
                rhs = jnp.concatenate(
                    [high[:256], low[:256], high[256:], high[:gap], low[256:], low[:gap]], 0
                )
                out = jnp.dot(w2_ref[...], rhs, preferred_element_type=jnp.float32)
                produced = out[:PIECE]
                loss = out[PIECE:]
                warm = out[species : species + 1] + (
                    out[species + 1 : species + 2] + out[species + 2 : species + 3]
                )
                a_ref[...] = (amounts + step * produced) * (amounts / (amounts + step * loss))
                t_ref[...] = thermal + step * warm
                return inner

            lax.fori_loop(0, most, substep, 0)

            for i in range(GROUP):
                slot = g * GROUP + i

                @pl.when(slot < count)
                def _(i=i, slot=slot):
                    at = pos_ref[slot]
                    cols = slice(i * LANES, (i + 1) * LANES)
                    where = pl.ds(block_rows + at, species, stride=rows)
                    o_ref[where, :] = o_ref[where, :] + (a_ref[0:species, cols] - s_ref[where, :])
                    top = pl.ds(at, 1)
                    o_ref[top, :] = o_ref[top, :] + (t_ref[:, cols] - s_ref[top, :])

            return carry

        lax.fori_loop(0, (count + (GROUP - 1)) // GROUP, group, 0)


def edge_kernel(
    comps, planes, tiles, part_ref, d_ref, ha_ref, hb_ref, z1_ref, z2_ref, out, work, sem
):
    rows = planes * tiles
    lane = lax.broadcasted_iota(jnp.int32, (planes, LANES), 1)
    x = lax.broadcasted_iota(jnp.int32, (planes, LANES), 0)
    side_a = odd_place("gx")
    swap = jnp.broadcast_to(odd_place("gy"), (planes, LANES)) == 1
    last = tiles - 1

    def sided(side):
        low = jnp.broadcast_to(side, (planes, LANES)) == 0
        place = jnp.where(low, x, planes - 1 - x)
        near = jnp.where(place == 0, near_weight, jnp.where(place == 1, -far_weight, 0.0))
        far = jnp.where(place == 0, -far_weight, 0.0)
        return near, far

    near_a, far_a = sided(side_a)
    near_b, far_b = sided(1 - side_a)
    above = jnp.where(lane % 64 < NZ, near_weight, 0.0)
    below = jnp.where(lane % 64 >= NZ, near_weight, 0.0)
    copies = []
    done = 0
    for k in range(comps // 2):
        one, two = z1_ref[k], z2_ref[k]
        low = jnp.where(swap, one, two)
        high = jnp.where(swap, two, one)
        low = pltpu.roll(low, LANES - NZ, 1) * above - far_weight * low
        high = pltpu.roll(high, NZ, 1) * below - far_weight * high
        lows = (low, pltpu.roll(low, 64, 1))
        highs = (pltpu.roll(high, 64, 1), high)
        for j in range(2):
            c = 2 * k + j
            weight = d_ref[c]
            na, fa = near_a * weight, far_a * weight
            nb, fb = near_b * weight, far_b * weight
            for t in range(tiles):
                where = slice(c * rows + t * planes, c * rows + (t + 1) * planes)

                def row(ref, start):
                    return ref[pl.ds(start, planes, stride=0), :]

                base_a = (c * tiles + t) * 2
                base_b = c * 2 * tiles + t
                value = part_ref[where, :]
                value = value + row(ha_ref, base_a + 1 - side_a) * na
                value = value + row(ha_ref, base_a + side_a) * fa
                value = value + row(hb_ref, base_b + side_a * tiles) * nb
                value = value + row(hb_ref, base_b + (1 - side_a) * tiles) * fb
                if t == 0:
                    value = value + jnp.where(lane < 64, weight * lows[j], 0.0)
                if t == last:
                    value = value + jnp.where(lane >= 64, weight * highs[j], 0.0)
                work[where, :] = value
        now = 2 * k + 2
        if now - done >= 8 or now == comps:
            where = pl.ds(done * rows, (now - done) * rows)
            copies.append(
                pltpu.make_async_copy(work.at[where, :], out.at[where, :], sem.at[len(copies)])
            )
            copies[-1].start()
            done = now
    for copy in copies:
        copy.wait()


def shift_matrix():
    source = np.arange(LANES)[:, None]
    target = np.arange(LANES)[None, :]
    weights = {1: 16.0, 2: -1.0}
    ys, yt, zs, zt = source // NZ, target // NZ, source % NZ, target % NZ
    rows = LANES // NZ
    own = np.where(source == target, -90.0, 0.0)
    cross = np.zeros_like(own)
    for distance, weight in weights.items():
        turn = (zt - zs) % NZ
        own += np.where((ys == yt) & ((turn == distance) | (turn == NZ - distance)), weight, 0.0)
        own += np.where((zs == zt) & (abs(yt - ys) == distance), weight, 0.0)
        to_next = (target < 64) & (zs == zt) & (yt + rows - ys == distance)
        to_previous = (target >= 64) & (zs == zt) & (ys + rows - yt == distance)
        cross += np.where(to_next | to_previous, weight, 0.0)
    one = np.concatenate([own, cross], 1)
    return jnp.asarray(np.concatenate([one, one], 0), jnp.bfloat16)


def per_device(
    state, diffusivity, log_prefactor, activation, heat, reactants, products, substeps, flame
):
    comps, planes, cells = state.shape
    tiles = cells // LANES
    rows = planes * tiles
    nreact = log_prefactor.shape[0]
    gx, gy = lax.axis_size("gx"), lax.axis_size("gy")
    f32 = jnp.float32
    flat = (
        state.reshape(comps, planes, tiles, LANES)
        .transpose(0, 2, 1, 3)
        .reshape(comps * rows, LANES)
    )
    vmem = pl.BlockSpec(memory_space=VMEM)
    smem = pl.BlockSpec(memory_space=SMEM)
    anywhere = pl.BlockSpec(memory_space=pl.ANY)

    hbm = pl.BlockSpec(memory_space=pltpu.HBM)
    sds = jax.ShapeDtypeStruct
    a = pl.pallas_call(
        functools.partial(outer_kernel, comps, planes, tiles),
        out_shape=sds((comps * tiles, 2, LANES), f32),
        in_specs=[hbm],
        out_specs=vmem,
        scratch_shapes=[pltpu.SemaphoreType.DMA((6,))],
        compiler_params=params(8),
        name="outer_planes",
    )(
        pltpu.with_memory_space_constraint(
            flat.reshape(comps * tiles, planes // 2, 2, LANES), pltpu.HBM
        )
    )
    b, first, second = pl.pallas_call(
        functools.partial(pack_kernel, comps, planes, tiles),
        out_shape=(
            sds((comps, 2, tiles, LANES), f32),
            sds((comps // 2, planes, LANES), f32),
            sds((comps // 2, planes, LANES), f32),
        ),
        in_specs=[vmem],
        out_specs=[vmem] * 3,
        compiler_params=params(16),
        name="pack",
    )(flat)

    outer = [(i, (i + 1) % gx) for i in range(1, gx, 2)]
    outer = outer + [(t, s) for s, t in outer]
    inner = [(i, i + 1) for i in range(0, gx, 2)]
    inner = inner + [(t, s) for s, t in inner]
    along_a = [(i, i + 1) for i in range(0, gy, 2)]
    along_a = along_a + [(t, s) for s, t in along_a]
    along_b = [(i, (i + 1) % gy) for i in range(1, gy, 2)]
    along_b = along_b + [(t, s) for s, t in along_b]
    ha = lax.ppermute(a, "gx", outer)
    hb = lax.ppermute(b, "gx", inner)
    z1 = lax.ppermute(first, "gy", along_a)
    z2 = lax.ppermute(second, "gy", along_b)

    padded = pl.cdiv(nreact, LANES) * LANES
    wide = pl.cdiv(nreact, 16) * 16
    part = pl.pallas_call(
        functools.partial(main_kernel, comps, planes, tiles, nreact),
        out_shape=sds((comps * rows, LANES), f32),
        in_specs=[vmem, smem, vmem] + [hbm] * 5 + [smem, smem],
        out_specs=vmem,
        scratch_shapes=[
            VMEM((nreact,), f32),
            VMEM((nreact,), f32),
            VMEM((nreact,), f32),
            VMEM((comps - 1, 2 * nreact), f32),
            VMEM((comps - 1, nreact), f32),
            VMEM((PIECE, padded), f32),
            VMEM((2 * PIECE, padded), f32),
            VMEM((wide, 3 * PIECE), jnp.bfloat16),
            VMEM((2 * PIECE, 2 * padded), jnp.bfloat16),
            VMEM((PIECE, GROUP * LANES), f32),
            VMEM((1, GROUP * LANES), f32),
            VMEM((1, GROUP * LANES), f32),
            SMEM((rows + 1,), jnp.int32),
            pltpu.SemaphoreType.DMA((5,)),
        ],
        compiler_params=params(24),
        cost_estimate=pl.CostEstimate(
            flops=2_000_000_000, bytes_accessed=16_000_000, transcendentals=1_000_000
        ),
        name="main",
    )(
        flat,
        diffusivity,
        shift_matrix(),
        log_prefactor,
        activation,
        heat,
        reactants.T,
        products,
        substeps,
        flame,
    )

    out = pl.pallas_call(
        functools.partial(edge_kernel, comps, planes, tiles),
        out_shape=sds((comps * rows, LANES), f32),
        in_specs=[vmem, smem, vmem, vmem, vmem, vmem],
        out_specs=anywhere,
        scratch_shapes=[VMEM((comps * rows, LANES), f32), pltpu.SemaphoreType.DMA((8,))],
        compiler_params=params(16),
        cost_estimate=pl.CostEstimate(
            flops=1_000_000, bytes_accessed=3_000_000, transcendentals=0
        ),
        name="edges",
    )(
        part,
        diffusivity,
        ha.reshape(comps * tiles * 2, LANES),
        hb.reshape(comps * 2 * tiles, LANES),
        z1,
        z2,
    )
    return (
        out.reshape(comps, tiles, planes, LANES).transpose(0, 2, 1, 3).reshape(comps, planes, cells)
    )


def solution(mesh):
    in_specs = (P(None, "gx", "gy"), P(), P(), P(), P(), P(), P(), P("gx", "gy"), P("gx", "gy"))
    out_specs = P(None, "gx", "gy")

    return jax.shard_map(
        per_device, mesh=mesh, in_specs=in_specs, out_specs=out_specs, check_vma=False
    )
```

```python
import functools

import jax
import jax.numpy as jnp
from jax import lax
from jax.experimental import pallas as pl
from jax.experimental.pallas import tpu as pltpu
from jax.sharding import PartitionSpec as P

NZ = 32
LANES = 128
near_weight = 4.0 / 3.0
far_weight = 1.0 / 12.0
LOG2E = 1.4426950408889634
GROUP = 4
PIECE = 64


VMEM = pltpu.VMEM
SMEM = pltpu.SMEM


def params(mib):
    return pltpu.CompilerParams(vmem_limit_bytes=mib << 20)


def odd_place(axis):
    return lax.rem(lax.axis_index(axis), 2)


def ahead_kernel(comps, planes, tiles, s_hbm, o_ref, sem):
    pair = odd_place("gx") * (planes // 2 - 1)
    total = comps * tiles
    parts = sem.shape[0]
    copies = []
    for i in range(parts):
        begin, end = total * i // parts, total * (i + 1) // parts
        where = pl.ds(begin, end - begin)
        copies.append(pltpu.make_async_copy(s_hbm.at[where, pair], o_ref.at[where], sem.at[i]))
        copies[-1].start()
    for copy in copies:
        copy.wait()


def pack_kernel(comps, planes, tiles, cuts, s_ref, *out_refs):
    a_refs, (b_ref, first_ref, second_ref) = out_refs[:-3], out_refs[-3:]
    rows = planes * tiles
    odd = odd_place("gy")
    lane = lax.broadcasted_iota(jnp.int32, (planes, LANES), 1)
    off_a = odd_place("gx") * (planes - 2)
    off_b = (planes - 2) - off_a

    def plane(c, x):
        return s_ref[pl.ds(c * rows + x, tiles, stride=planes), :]

    for a_ref, begin, end in zip(a_refs, cuts, cuts[1:]):
        for c in range(begin, end):
            for p in range(2):
                a_ref[c - begin, p] = plane(c, off_a + p)
    for c in range(comps):
        for p in range(2):
            b_ref[c, p] = plane(c, off_b + p)
    swap = jnp.broadcast_to(odd, (planes, LANES)) == 1
    last = (tiles - 1) * planes
    for k in range(comps // 2):
        first, second = 2 * k * rows, (2 * k + 1) * rows
        low_a = s_ref[first : first + planes, :]
        low_b = s_ref[second : second + planes, :]
        high_a = s_ref[first + last : first + last + planes, :]
        high_b = s_ref[second + last : second + last + planes, :]
        low = jnp.where(lane < 64, low_a, pltpu.roll(low_b, 64, 1))
        high = jnp.where(lane < 64, pltpu.roll(high_a, 64, 1), high_b)
        first_ref[k] = jnp.where(swap, low, high)
        second_ref[k] = jnp.where(swap, high, low)


def split3(value):
    high = value.astype(jnp.bfloat16)
    rest = value - high.astype(jnp.float32)
    middle = rest.astype(jnp.bfloat16)
    low = (rest - middle.astype(jnp.float32)).astype(jnp.bfloat16)
    return high, middle, low


def shift_matrix():
    shape = (LANES, LANES)
    source = lax.broadcasted_iota(jnp.int32, shape, 0)
    target = lax.broadcasted_iota(jnp.int32, shape, 1)
    rows = LANES // NZ
    ys, yt = source // NZ, target // NZ
    turn = (target - source) & (NZ - 1)
    same_z = turn == 0

    def weight(distance):
        return jnp.where(distance == 1, 16.0, jnp.where(distance == 2, -1.0, 0.0))

    turn = jnp.minimum(turn, NZ - turn)
    along_z = jnp.where(same_z, -90.0, weight(turn))
    own = jnp.where(ys == yt, along_z, jnp.where(same_z, weight(jnp.abs(yt - ys)), 0.0))
    apart = jnp.where(target < LANES // 2, yt + rows - ys, ys + rows - yt)
    cross = jnp.where(same_z, weight(apart), 0.0)
    one = jnp.concatenate([own, cross], 1).astype(jnp.bfloat16)
    return jnp.concatenate([one, one], 0)


def many_of(comps):
    return max(n for n in range(1, 7) if comps % n == 0)


def main_kernel(
    comps,
    planes,
    tiles,
    nreact,
    s_ref,
    d_ref,
    lp_hbm,
    act_hbm,
    heat_hbm,
    rt_hbm,
    pr_hbm,
    sub_ref,
    flame_ref,
    o_ref,
    lp_ref,
    act_ref,
    heat_ref,
    rt_ref,
    pr_ref,
    q_ref,
    p_ref,
    w1_ref,
    w2_ref,
    a_ref,
    t_ref,
    st_ref,
    shift_ref,
    even_ref,
    odd_ref,
    pos_ref,
    sem,
):
    rows = planes * tiles
    species = comps - 1
    block_rows = planes * tiles
    loads = [
        pltpu.make_async_copy(source, target, sem.at[i])
        for i, (source, target) in enumerate(
            (
                (lp_hbm, lp_ref),
                (act_hbm, act_ref),
                (heat_hbm, heat_ref),
                (rt_hbm, rt_ref),
                (pr_hbm, pr_ref),
            )
        )
    ]
    for load in loads:
        load.start()

    shift_ref[...] = shift_matrix()

    count = jnp.int32(0)
    for x in range(planes):
        for b in range(tiles):
            pos_ref[count] = b * planes + x
            count = count + flame_ref[x, b]

    many = many_of(comps)
    size = many * rows
    groups = comps // many
    shape = (many, tiles, planes, LANES)
    lane = lax.broadcasted_iota(jnp.int32, (1, 1, planes, LANES), 3)
    x = lax.broadcasted_iota(jnp.int32, (1, 1, planes, LANES), 2)
    zero = jnp.zeros((many, 1, planes, LANES), jnp.float32)
    near, far = near_weight * 12.0, -far_weight * 12.0
    weights = {
        -1: jnp.where(x > 0, near, 0.0),
        1: jnp.where(x < planes - 1, near, 0.0),
        -2: jnp.where(x > 1, far, 0.0),
        2: jnp.where(x < planes - 2, far, 0.0),
    }

    def product(i, buffer):
        flat = s_ref[pl.ds(pl.multiple_of(i * size, size), size), :]
        high = flat.astype(jnp.bfloat16)
        low = (flat - high.astype(jnp.float32)).astype(jnp.bfloat16)
        both = jnp.concatenate([high, low], 1)
        buffer[...] = jnp.dot(both, shift_ref[...], preferred_element_type=jnp.float32)

    def combine(i, buffer, inside):
        start = pl.multiple_of(i * size, size)
        v = s_ref[pl.ds(start, size), :].reshape(shape)
        own = buffer[:, :LANES].reshape(shape)
        cross = buffer[:, LANES:].reshape(shape)
        before = jnp.concatenate([zero, cross[:, :-1]], 1)
        after = jnp.concatenate([cross[:, 1:], zero], 1)
        own = own + jnp.where(lane < 64, before, after)
        for offset, weight in weights.items():
            if inside:
                moved = s_ref[pl.ds(start + offset, size), :].reshape(shape)
            else:
                moved = pltpu.roll(v, (-offset) % planes, 2)
            own = own + moved * weight
        for j in range(many):
            where = pl.ds(pl.multiple_of(start + j * rows, rows), rows)
            scale = d_ref[i * many + j] * (1.0 / 12.0)
            o_ref[where, :] = (v[j] + scale * own[j]).reshape(rows, LANES)

    product(0, even_ref)
    if groups % 2 == 1 and groups > 2:
        product(1, odd_ref)
        combine(0, even_ref, False)

        def two(i, carry):
            g = 2 * i + 1
            product(g + 1, even_ref)
            combine(g, odd_ref, True)
            product(g + 2, odd_ref)
            combine(g + 1, even_ref, True)
            return carry

        lax.fori_loop(0, (groups - 3) // 2, two, 0)
        product(groups - 1, even_ref)
        combine(groups - 2, odd_ref, True)
        combine(groups - 1, even_ref, False)
    else:
        for i in range(groups):
            combine(i, even_ref, False)
            if i < groups - 1:
                product(i + 1, even_ref)
    for load in loads:
        load.wait()

    @pl.when(count > 0)
    def _():
        padded = q_ref.shape[1]
        wide = w1_ref.shape[0]
        q_ref[...] = jnp.zeros_like(q_ref)
        p_ref[...] = jnp.zeros_like(p_ref)
        q_ref[0:species, 0:nreact] = rt_ref[:, 0:nreact] + rt_ref[:, nreact : 2 * nreact]
        p_ref[0:species, 0:nreact] = pr_ref[...]
        p_ref[PIECE : PIECE + species, 0:nreact] = q_ref[0:species, 0:nreact]
        for i, piece in enumerate(split3(act_ref[...].reshape(1, nreact) * (-LOG2E))):
            q_ref[species + i : species + i + 1, 0:nreact] = piece.astype(jnp.float32)
        for i, piece in enumerate(split3(lp_ref[...].reshape(1, nreact) * LOG2E)):
            q_ref[species + 3 + i : species + 4 + i, 0:nreact] = piece.astype(jnp.float32)
        for i, piece in enumerate(split3(heat_ref[...].reshape(1, nreact))):
            p_ref[species + i : species + i + 1, 0:nreact] = piece.astype(jnp.float32)
        q = q_ref[...]
        w1 = jnp.transpose(jnp.concatenate([q, q, q], 0))
        w1_ref[...] = w1[0:wide].astype(jnp.bfloat16)
        w = p_ref[...].astype(jnp.bfloat16)
        head, rest = w[:, :256], w[:, 256:padded]
        w2_ref[...] = jnp.concatenate([head, head, rest, rest], 1)

        a_ref[...] = jnp.ones_like(a_ref)
        arow = lax.broadcasted_iota(jnp.int32, a_ref.shape, 0)

        def group(g, carry):
            most = jnp.int32(0)
            pieces = []
            for i in range(GROUP):
                slot = g * GROUP + i
                here = jnp.where(slot < count, slot, 0)
                at = pos_ref[here]
                n = jnp.where(
                    slot < count, sub_ref[lax.rem(at, planes), lax.div(at, planes)], 0
                )
                most = jnp.maximum(most, n)
                cols = slice(i * LANES, (i + 1) * LANES)
                a_ref[0:species, cols] = s_ref[pl.ds(block_rows + at, species, stride=rows), :]
                t_ref[:, cols] = s_ref[pl.ds(at, 1), :]
                pieces.append(jnp.full((1, LANES), n, jnp.int32))
            counts = jnp.concatenate(pieces, 1)
            st_ref[...] = 1.0 / jnp.maximum(counts, 1).astype(jnp.float32)

            def substep(k, inner):
                step = jnp.where(counts > k, st_ref[...], 0.0)
                amounts = a_ref[...]
                thermal = t_ref[...]
                inverse = 1.0 / thermal
                terms = jnp.where(
                    arow < species,
                    jnp.log2(amounts),
                    jnp.where(
                        arow < species + 3, inverse, jnp.where(arow < species + 6, 1.0, 0.0)
                    ),
                )
                rhs = jnp.concatenate(split3(terms), 0)
                exponent = jnp.dot(w1_ref[...], rhs, preferred_element_type=jnp.float32)
                progress = jnp.exp2(exponent)
                high = progress.astype(jnp.bfloat16)
                low = (progress - high.astype(jnp.float32)).astype(jnp.bfloat16)
                gap = 2 * LANES - wide + LANES
                rhs = jnp.concatenate(
                    [high[:256], low[:256], high[256:], high[:gap], low[256:], low[:gap]], 0
                )
                out = jnp.dot(w2_ref[...], rhs, preferred_element_type=jnp.float32)
                produced = out[:PIECE]
                loss = out[PIECE:]
                warm = out[species : species + 1] + (
                    out[species + 1 : species + 2] + out[species + 2 : species + 3]
                )
                a_ref[...] = (amounts + step * produced) * (amounts / (amounts + step * loss))
                t_ref[...] = thermal + step * warm
                return inner

            lax.fori_loop(0, most, substep, 0)

            for i in range(GROUP):
                slot = g * GROUP + i

                @pl.when(slot < count)
                def _(i=i, slot=slot):
                    at = pos_ref[slot]
                    cols = slice(i * LANES, (i + 1) * LANES)
                    where = pl.ds(block_rows + at, species, stride=rows)
                    o_ref[where, :] = o_ref[where, :] + (a_ref[0:species, cols] - s_ref[where, :])
                    top = pl.ds(at, 1)
                    o_ref[top, :] = o_ref[top, :] + (t_ref[:, cols] - s_ref[top, :])

            return carry

        lax.fori_loop(0, (count + (GROUP - 1)) // GROUP, group, 0)


def add_planes(planes, tiles, work, d_ref, plane, begin, end, side):
    rows = planes * tiles
    for c in range(begin, end):
        near = plane(c, 1 - side)
        far = plane(c, side)
        weight = d_ref[c]
        first = pl.ds(c * rows + side * (planes - 1), tiles, stride=planes)
        second = pl.ds(c * rows + 1 + side * (planes - 3), tiles, stride=planes)
        one, two = work[first, :], work[second, :]
        work[first, :] = one + weight * (near_weight * near - far_weight * far)
        work[second, :] = two - (weight * far_weight) * near


def inner_edges_kernel(comps, planes, tiles, part_ref, d_ref, hb_ref, z1_ref, z2_ref, work):
    del part_ref
    rows = planes * tiles
    lane = lax.broadcasted_iota(jnp.int32, (planes, LANES), 1)
    swap = jnp.broadcast_to(odd_place("gy"), (planes, LANES)) == 1
    last = (tiles - 1) * planes
    above = jnp.where(lane % 64 < NZ, near_weight, 0.0)
    below = jnp.where(lane % 64 >= NZ, near_weight, 0.0)
    lower = jnp.where(lane < 64, 1.0, 0.0)
    upper = jnp.where(lane < 64, 0.0, 1.0)

    def pair(k, carry):
        one, two = z1_ref[k], z2_ref[k]
        low = jnp.where(swap, one, two)
        high = jnp.where(swap, two, one)
        low = pltpu.roll(low, LANES - NZ, 1) * above - far_weight * low
        high = pltpu.roll(high, NZ, 1) * below - far_weight * high
        lows = (low * lower, pltpu.roll(low * upper, 64, 1))
        highs = (pltpu.roll(high * lower, 64, 1), high * upper)
        for j in range(2):
            weight = d_ref[2 * k + j]
            base = pl.multiple_of((2 * k + j) * rows, planes)
            top = pl.ds(base, planes)
            end = pl.ds(pl.multiple_of(base + last, planes), planes)
            work[top, :] = work[top, :] + weight * lows[j]
            work[end, :] = work[end, :] + weight * highs[j]
        return carry

    for k in range(comps // 2):
        pair(k, 0)
    odd = odd_place("gx")
    for side in range(2):

        @pl.when(odd == 1 - side)
        def _(side=side):
            add_planes(
                planes, tiles, work, d_ref, lambda c, p: hb_ref[c, p], 0, comps, side
            )


def outer_edges_kernel(planes, tiles, cuts, parts, ahead, part_ref, d_ref, *rest):
    h_refs, (work, out, sem) = rest[: len(cuts) - 1], rest[-3:]
    rows = planes * tiles
    odd = odd_place("gx")
    begin, end = cuts[0], cuts[-1]

    def plane(c, p):
        i = max(i for i, cut in enumerate(cuts) if cut <= c)
        if i == 0 and ahead:
            return h_refs[i][pl.ds((c - cuts[i]) * 2 * tiles + p, tiles, stride=2), :]
        return h_refs[i][c - cuts[i], p]

    def send(i, first, last):
        where = pl.ds(first * rows, (last - first) * rows)
        return pltpu.make_async_copy(work.at[where, :], out.at[where, :], sem.at[i])

    bounds = [begin + (end - begin) * i // parts for i in range(parts + 1)]
    for i, (first, last) in enumerate(zip(bounds, bounds[1:])):
        for side in range(2):

            @pl.when(odd == side)
            def _(side=side, first=first, last=last):
                add_planes(planes, tiles, work, d_ref, plane, first, last, side)

        send(i, first, last).start()
    for i, (first, last) in enumerate(zip(bounds, bounds[1:])):
        send(i, first, last).wait()


def per_device(
    state, diffusivity, log_prefactor, activation, heat, reactants, products, substeps, flame
):
    comps, planes, cells = state.shape
    tiles = cells // LANES
    rows = planes * tiles
    nreact = log_prefactor.shape[0]
    gx, gy = lax.axis_size("gx"), lax.axis_size("gy")
    f32 = jnp.float32
    flat = (
        state.reshape(comps, planes, tiles, LANES)
        .transpose(0, 2, 1, 3)
        .reshape(comps * rows, LANES)
    )

    def stay(array):
        return pltpu.with_memory_space_constraint(array, pltpu.HBM)

    vmem = pl.BlockSpec(memory_space=VMEM)
    smem = pl.BlockSpec(memory_space=SMEM)
    anywhere = pl.BlockSpec(memory_space=pl.ANY)

    hbm = pl.BlockSpec(memory_space=pltpu.HBM)
    sds = jax.ShapeDtypeStruct
    ahead_count, late = comps // 4, comps // 4
    cuts = (0, ahead_count, comps - late, comps)
    early = pl.pallas_call(
        functools.partial(ahead_kernel, ahead_count, planes, tiles),
        out_shape=sds((ahead_count * tiles, 2, LANES), f32),
        in_specs=[hbm],
        out_specs=vmem,
        scratch_shapes=[pltpu.SemaphoreType.DMA((4,))],
        compiler_params=params(8),
        name="ahead",
    )(stay(flat.reshape(comps * tiles, planes // 2, 2, LANES)))
    *a, b, first, second = pl.pallas_call(
        functools.partial(pack_kernel, comps, planes, tiles, cuts[1:]),
        out_shape=tuple(
            [sds((end - begin, 2, tiles, LANES), f32) for begin, end in zip(cuts[1:], cuts[2:])]
            + [sds((comps, 2, tiles, LANES), f32)]
            + [sds((comps // 2, planes, LANES), f32)] * 2
        ),
        in_specs=[vmem],
        out_specs=[vmem] * 5,
        compiler_params=params(16),
        name="pack",
    )(flat)

    outer = [(i, (i + 1) % gx) for i in range(1, gx, 2)]
    outer = outer + [(t, s) for s, t in outer]
    inner = [(i, i + 1) for i in range(0, gx, 2)]
    inner = inner + [(t, s) for s, t in inner]
    along_a = [(i, i + 1) for i in range(0, gy, 2)]
    along_a = along_a + [(t, s) for s, t in along_a]
    along_b = [(i, (i + 1) % gy) for i in range(1, gy, 2)]
    along_b = along_b + [(t, s) for s, t in along_b]
    ha = []
    for piece in [early, *a]:
        ha.append(lax.ppermute(piece, "gx", outer))
    ha[0] = ha[0].reshape(ahead_count * tiles * 2, LANES)
    hb = lax.ppermute(b, "gx", inner)
    z1 = lax.ppermute(first, "gy", along_a)
    z2 = lax.ppermute(second, "gy", along_b)

    padded = pl.cdiv(nreact, LANES) * LANES
    wide = pl.cdiv(nreact, 16) * 16
    part = pl.pallas_call(
        functools.partial(main_kernel, comps, planes, tiles, nreact),
        out_shape=sds((comps * rows, LANES), f32),
        in_specs=[vmem, smem] + [hbm] * 5 + [smem, smem],
        out_specs=vmem,
        scratch_shapes=[
            VMEM((nreact,), f32),
            VMEM((nreact,), f32),
            VMEM((nreact,), f32),
            VMEM((comps - 1, 2 * nreact), f32),
            VMEM((comps - 1, nreact), f32),
            VMEM((PIECE, padded), f32),
            VMEM((2 * PIECE, padded), f32),
            VMEM((wide, 3 * PIECE), jnp.bfloat16),
            VMEM((2 * PIECE, 2 * padded), jnp.bfloat16),
            VMEM((PIECE, GROUP * LANES), f32),
            VMEM((1, GROUP * LANES), f32),
            VMEM((1, GROUP * LANES), f32),
            VMEM((2 * LANES, 2 * LANES), jnp.bfloat16),
            VMEM((many_of(comps) * rows, 2 * LANES), f32),
            VMEM((many_of(comps) * rows, 2 * LANES), f32),
            SMEM((rows + 1,), jnp.int32),
            pltpu.SemaphoreType.DMA((5,)),
        ],
        compiler_params=params(24),
        cost_estimate=pl.CostEstimate(
            flops=2_000_000_000, bytes_accessed=16_000_000, transcendentals=1_000_000
        ),
        name="main",
    )(
        flat,
        diffusivity,
        stay(log_prefactor),
        stay(activation),
        stay(heat),
        stay(reactants.T),
        stay(products),
        substeps,
        flame,
    )

    whole = sds((comps * rows, LANES), f32)
    cost = pl.CostEstimate(flops=1_000_000, bytes_accessed=3_000_000, transcendentals=0)
    part = pl.pallas_call(
        functools.partial(inner_edges_kernel, comps, planes, tiles),
        out_shape=whole,
        in_specs=[vmem, smem, vmem, vmem, vmem],
        out_specs=vmem,
        input_output_aliases={0: 0},
        compiler_params=params(16),
        cost_estimate=cost,
        name="inner_edges",
    )(part, diffusivity, hb, z1, z2)
    out = None
    for begin, end, parts in ((0, 2, 3), (2, 3, 2)):
        extra = [] if out is None else [out]
        count = end - begin
        part, out = pl.pallas_call(
            functools.partial(
                outer_edges_kernel, planes, tiles, cuts[begin : end + 1], parts, begin == 0
            ),
            out_shape=(whole, whole),
            in_specs=[vmem, smem] + [vmem] * count + [anywhere] * len(extra),
            out_specs=(vmem, anywhere),
            scratch_shapes=[pltpu.SemaphoreType.DMA((parts,))],
            input_output_aliases={0: 0, 2 + count: 1} if extra else {0: 0},
            compiler_params=params(16),
            cost_estimate=cost,
            name="outer_edges",
        )(part, diffusivity, *ha[begin:end], *extra)
    return (
        out.reshape(comps, tiles, planes, LANES).transpose(0, 2, 1, 3).reshape(comps, planes, cells)
    )


def solution(mesh):
    in_specs = (P(None, "gx", "gy"), P(), P(), P(), P(), P(), P(), P("gx", "gy"), P("gx", "gy"))
    out_specs = P(None, "gx", "gy")

    return jax.shard_map(
        per_device, mesh=mesh, in_specs=in_specs, out_specs=out_specs, check_vma=False
    )
```

```python
import functools

import jax
import jax.numpy as jnp
from jax import lax
from jax.experimental import pallas as pl
from jax.experimental.pallas import tpu as pltpu
from jax.sharding import PartitionSpec as P

NZ = 32
LANES = 128
near_weight = 4.0 / 3.0
far_weight = 1.0 / 12.0
LOG2E = 1.4426950408889634
GROUP = 4
PIECE = 64


VMEM = pltpu.VMEM
SMEM = pltpu.SMEM


def params(mib):
    return pltpu.CompilerParams(vmem_limit_bytes=mib << 20)


def odd_place(axis):
    return lax.rem(lax.axis_index(axis), 2)


def ahead_kernel(comps, planes, tiles, s_hbm, o_ref, sem):
    pair = odd_place("gx") * (planes // 2 - 1)
    total = comps * tiles
    parts = sem.shape[0]
    copies = []
    for i in range(parts):
        begin, end = total * i // parts, total * (i + 1) // parts
        where = pl.ds(begin, end - begin)
        copies.append(pltpu.make_async_copy(s_hbm.at[where, pair], o_ref.at[where], sem.at[i]))
        copies[-1].start()
    for copy in copies:
        copy.wait()


def pack_kernel(comps, planes, tiles, s_ref, b_ref, low_ref, high_ref):
    rows = planes * tiles
    lane = lax.broadcasted_iota(jnp.int32, (planes, LANES), 1)
    off_b = (1 - odd_place("gx")) * (planes - 2)
    for c in range(comps):
        for p in range(2):
            b_ref[c, p] = s_ref[pl.ds(c * rows + off_b + p, tiles, stride=planes), :]
    last = (tiles - 1) * planes
    for k in range(comps // 2):
        first, second = 2 * k * rows, (2 * k + 1) * rows
        low_a = s_ref[first : first + planes, :]
        low_b = s_ref[second : second + planes, :]
        high_a = s_ref[first + last : first + last + planes, :]
        high_b = s_ref[second + last : second + last + planes, :]
        low_ref[k] = jnp.where(lane < 64, low_a, pltpu.roll(low_b, 64, 1))
        high_ref[k] = jnp.where(lane < 64, pltpu.roll(high_a, 64, 1), high_b)


def split3(value):
    high = value.astype(jnp.bfloat16)
    rest = value - high.astype(jnp.float32)
    middle = rest.astype(jnp.bfloat16)
    low = (rest - middle.astype(jnp.float32)).astype(jnp.bfloat16)
    return high, middle, low


def shift_matrix():
    shape = (LANES, LANES)
    source = lax.broadcasted_iota(jnp.int32, shape, 0)
    target = lax.broadcasted_iota(jnp.int32, shape, 1)
    rows = LANES // NZ
    ys, yt = source // NZ, target // NZ
    turn = (target - source) & (NZ - 1)
    same_z = turn == 0

    def weight(distance):
        return jnp.where(distance == 1, 16.0, jnp.where(distance == 2, -1.0, 0.0))

    turn = jnp.minimum(turn, NZ - turn)
    along_z = jnp.where(same_z, -90.0, weight(turn))
    own = jnp.where(ys == yt, along_z, jnp.where(same_z, weight(jnp.abs(yt - ys)), 0.0))
    apart = jnp.where(target < LANES // 2, yt + rows - ys, ys + rows - yt)
    cross = jnp.where(same_z, weight(apart), 0.0)
    one = jnp.concatenate([own, cross], 1).astype(jnp.bfloat16)
    return jnp.concatenate([one, one], 0)


def many_of(comps):
    return max(n for n in range(1, 7) if comps % n == 0)


def main_kernel(
    comps,
    planes,
    tiles,
    nreact,
    s_ref,
    d_ref,
    lp_hbm,
    act_hbm,
    heat_hbm,
    rt_hbm,
    pr_hbm,
    sub_ref,
    flame_ref,
    o_ref,
    lp_ref,
    act_ref,
    heat_ref,
    rt_ref,
    pr_ref,
    q_ref,
    p_ref,
    w1_ref,
    w2_ref,
    a_ref,
    t_ref,
    st_ref,
    shift_ref,
    even_ref,
    odd_ref,
    pos_ref,
    sem,
):
    rows = planes * tiles
    species = comps - 1
    block_rows = planes * tiles
    loads = [
        pltpu.make_async_copy(source, target, sem.at[i])
        for i, (source, target) in enumerate(
            (
                (lp_hbm, lp_ref),
                (act_hbm, act_ref),
                (heat_hbm, heat_ref),
                (rt_hbm, rt_ref),
                (pr_hbm, pr_ref),
            )
        )
    ]
    for load in loads:
        load.start()

    shift_ref[...] = shift_matrix()

    count = jnp.int32(0)
    for x in range(planes):
        for b in range(tiles):
            pos_ref[count] = b * planes + x
            count = count + flame_ref[x, b]

    many = many_of(comps)
    size = many * rows
    groups = comps // many
    shape = (many, tiles, planes, LANES)
    lane = lax.broadcasted_iota(jnp.int32, (1, 1, planes, LANES), 3)
    x = lax.broadcasted_iota(jnp.int32, (1, 1, planes, LANES), 2)
    zero = jnp.zeros((many, 1, planes, LANES), jnp.float32)
    near, far = near_weight * 12.0, -far_weight * 12.0
    weights = {
        -1: jnp.where(x > 0, near, 0.0),
        1: jnp.where(x < planes - 1, near, 0.0),
        -2: jnp.where(x > 1, far, 0.0),
        2: jnp.where(x < planes - 2, far, 0.0),
    }

    def product(i, buffer):
        flat = s_ref[pl.ds(pl.multiple_of(i * size, size), size), :]
        high = flat.astype(jnp.bfloat16)
        low = (flat - high.astype(jnp.float32)).astype(jnp.bfloat16)
        both = jnp.concatenate([high, low], 1)
        buffer[...] = jnp.dot(both, shift_ref[...], preferred_element_type=jnp.float32)

    def combine(i, buffer, inside):
        start = pl.multiple_of(i * size, size)
        v = s_ref[pl.ds(start, size), :].reshape(shape)
        own = buffer[:, :LANES].reshape(shape)
        cross = buffer[:, LANES:].reshape(shape)
        before = jnp.concatenate([zero, cross[:, :-1]], 1)
        after = jnp.concatenate([cross[:, 1:], zero], 1)
        own = own + jnp.where(lane < 64, before, after)
        for offset, weight in weights.items():
            if inside:
                moved = s_ref[pl.ds(start + offset, size), :].reshape(shape)
            else:
                moved = pltpu.roll(v, (-offset) % planes, 2)
            own = own + moved * weight
        for j in range(many):
            where = pl.ds(pl.multiple_of(start + j * rows, rows), rows)
            scale = d_ref[i * many + j] * (1.0 / 12.0)
            o_ref[where, :] = (v[j] + scale * own[j]).reshape(rows, LANES)

    product(0, even_ref)
    if groups % 2 == 1 and groups > 2:
        product(1, odd_ref)
        combine(0, even_ref, False)

        def two(i, carry):
            g = 2 * i + 1
            product(g + 1, even_ref)
            combine(g, odd_ref, True)
            product(g + 2, odd_ref)
            combine(g + 1, even_ref, True)
            return carry

        lax.fori_loop(0, (groups - 3) // 2, two, 0)
        product(groups - 1, even_ref)
        combine(groups - 2, odd_ref, True)
        combine(groups - 1, even_ref, False)
    else:
        for i in range(groups):
            combine(i, even_ref, False)
            if i < groups - 1:
                product(i + 1, even_ref)
    for load in loads:
        load.wait()

    @pl.when(count > 0)
    def _():
        padded = q_ref.shape[1]
        wide = w1_ref.shape[0]
        q_ref[...] = jnp.zeros_like(q_ref)
        p_ref[...] = jnp.zeros_like(p_ref)
        q_ref[0:species, 0:nreact] = rt_ref[:, 0:nreact] + rt_ref[:, nreact : 2 * nreact]
        p_ref[0:species, 0:nreact] = pr_ref[...]
        p_ref[PIECE : PIECE + species, 0:nreact] = q_ref[0:species, 0:nreact]
        for i, piece in enumerate(split3(act_ref[...].reshape(1, nreact) * (-LOG2E))):
            q_ref[species + i : species + i + 1, 0:nreact] = piece.astype(jnp.float32)
        for i, piece in enumerate(split3(lp_ref[...].reshape(1, nreact) * LOG2E)):
            q_ref[species + 3 + i : species + 4 + i, 0:nreact] = piece.astype(jnp.float32)
        for i, piece in enumerate(split3(heat_ref[...].reshape(1, nreact))):
            p_ref[species + i : species + i + 1, 0:nreact] = piece.astype(jnp.float32)
        q = q_ref[...]
        w1 = jnp.transpose(jnp.concatenate([q, q, q], 0))
        w1_ref[...] = w1[0:wide].astype(jnp.bfloat16)
        w = p_ref[...].astype(jnp.bfloat16)
        head, rest = w[:, :256], w[:, 256:padded]
        w2_ref[...] = jnp.concatenate([head, head, rest, rest], 1)

        a_ref[...] = jnp.ones_like(a_ref)
        arow = lax.broadcasted_iota(jnp.int32, a_ref.shape, 0)

        def group(g, carry):
            most = jnp.int32(0)
            pieces = []
            for i in range(GROUP):
                slot = g * GROUP + i
                here = jnp.where(slot < count, slot, 0)
                at = pos_ref[here]
                n = jnp.where(
                    slot < count, sub_ref[lax.rem(at, planes), lax.div(at, planes)], 0
                )
                most = jnp.maximum(most, n)
                cols = slice(i * LANES, (i + 1) * LANES)
                a_ref[0:species, cols] = s_ref[pl.ds(block_rows + at, species, stride=rows), :]
                t_ref[:, cols] = s_ref[pl.ds(at, 1), :]
                pieces.append(jnp.full((1, LANES), n, jnp.int32))
            counts = jnp.concatenate(pieces, 1)
            st_ref[...] = 1.0 / jnp.maximum(counts, 1).astype(jnp.float32)

            def substep(k, inner):
                step = jnp.where(counts > k, st_ref[...], 0.0)
                amounts = a_ref[...]
                thermal = t_ref[...]
                inverse = 1.0 / thermal
                terms = jnp.where(
                    arow < species,
                    jnp.log2(amounts),
                    jnp.where(
                        arow < species + 3, inverse, jnp.where(arow < species + 6, 1.0, 0.0)
                    ),
                )
                rhs = jnp.concatenate(split3(terms), 0)
                exponent = jnp.dot(w1_ref[...], rhs, preferred_element_type=jnp.float32)
                progress = jnp.exp2(exponent)
                high = progress.astype(jnp.bfloat16)
                low = (progress - high.astype(jnp.float32)).astype(jnp.bfloat16)
                gap = 2 * LANES - wide + LANES
                rhs = jnp.concatenate(
                    [high[:256], low[:256], high[256:], high[:gap], low[256:], low[:gap]], 0
                )
                out = jnp.dot(w2_ref[...], rhs, preferred_element_type=jnp.float32)
                produced = out[:PIECE]
                loss = out[PIECE:]
                warm = out[species : species + 1] + (
                    out[species + 1 : species + 2] + out[species + 2 : species + 3]
                )
                a_ref[...] = (amounts + step * produced) * (amounts / (amounts + step * loss))
                t_ref[...] = thermal + step * warm
                return inner

            lax.fori_loop(0, most, substep, 0)

            for i in range(GROUP):
                slot = g * GROUP + i

                @pl.when(slot < count)
                def _(i=i, slot=slot):
                    at = pos_ref[slot]
                    cols = slice(i * LANES, (i + 1) * LANES)
                    where = pl.ds(block_rows + at, species, stride=rows)
                    o_ref[where, :] = o_ref[where, :] + (a_ref[0:species, cols] - s_ref[where, :])
                    top = pl.ds(at, 1)
                    o_ref[top, :] = o_ref[top, :] + (t_ref[:, cols] - s_ref[top, :])

            return carry

        lax.fori_loop(0, (count + (GROUP - 1)) // GROUP, group, 0)


def add_planes(planes, tiles, work, d_ref, plane, begin, end, side):
    rows = planes * tiles
    for c in range(begin, end):
        near = plane(c, 1 - side)
        far = plane(c, side)
        weight = d_ref[c]
        first = pl.ds(c * rows + side * (planes - 1), tiles, stride=planes)
        second = pl.ds(c * rows + 1 + side * (planes - 3), tiles, stride=planes)
        one, two = work[first, :], work[second, :]
        work[first, :] = one + weight * (near_weight * near - far_weight * far)
        work[second, :] = two - (weight * far_weight) * near


def inner_edges_kernel(comps, planes, tiles, part_ref, d_ref, hb_ref, zl_ref, zh_ref, work):
    del part_ref
    rows = planes * tiles
    lane = lax.broadcasted_iota(jnp.int32, (planes, LANES), 1)
    last = (tiles - 1) * planes
    above = jnp.where(lane % 64 < NZ, near_weight, 0.0)
    below = jnp.where(lane % 64 >= NZ, near_weight, 0.0)
    lower = jnp.where(lane < 64, 1.0, 0.0)
    upper = jnp.where(lane < 64, 0.0, 1.0)

    def pair(k, carry):
        low, high = zl_ref[k], zh_ref[k]
        low = pltpu.roll(low, LANES - NZ, 1) * above - far_weight * low
        high = pltpu.roll(high, NZ, 1) * below - far_weight * high
        lows = (low * lower, pltpu.roll(low * upper, 64, 1))
        highs = (pltpu.roll(high * lower, 64, 1), high * upper)
        for j in range(2):
            weight = d_ref[2 * k + j]
            base = pl.multiple_of((2 * k + j) * rows, planes)
            top = pl.ds(base, planes)
            end = pl.ds(pl.multiple_of(base + last, planes), planes)
            work[top, :] = work[top, :] + weight * lows[j]
            work[end, :] = work[end, :] + weight * highs[j]
        return carry

    for k in range(comps // 2):
        pair(k, 0)
    odd = odd_place("gx")
    for side in range(2):

        @pl.when(odd == 1 - side)
        def _(side=side):
            add_planes(
                planes, tiles, work, d_ref, lambda c, p: hb_ref[c, p], 0, comps, side
            )


def outer_edges_kernel(comps, planes, tiles, parts, part_ref, d_ref, h_ref, work, out, sem):
    del part_ref
    rows = planes * tiles
    odd = odd_place("gx")

    def plane(c, p):
        return h_ref[pl.ds(c * 2 * tiles + p, tiles, stride=2), :]

    def send(i, first, last):
        where = pl.ds(first * rows, (last - first) * rows)
        return pltpu.make_async_copy(work.at[where, :], out.at[where, :], sem.at[i])

    bounds = [comps * i // parts for i in range(parts + 1)]
    spans = list(zip(bounds, bounds[1:]))
    for side in range(2):

        @pl.when(odd == side)
        def _(side=side):
            for i, (first, last) in enumerate(spans):
                add_planes(planes, tiles, work, d_ref, plane, first, last, side)
                send(i, first, last).start()

    for i, (first, last) in enumerate(spans):
        send(i, first, last).wait()


def per_device(
    state, diffusivity, log_prefactor, activation, heat, reactants, products, substeps, flame
):
    comps, planes, cells = state.shape
    tiles = cells // LANES
    rows = planes * tiles
    nreact = log_prefactor.shape[0]
    gx, gy = lax.axis_size("gx"), lax.axis_size("gy")
    f32 = jnp.float32
    flat = (
        state.reshape(comps, planes, tiles, LANES)
        .transpose(0, 2, 1, 3)
        .reshape(comps * rows, LANES)
    )

    def stay(array):
        return pltpu.with_memory_space_constraint(array, pltpu.HBM)

    vmem = pl.BlockSpec(memory_space=VMEM)
    smem = pl.BlockSpec(memory_space=SMEM)
    anywhere = pl.BlockSpec(memory_space=pl.ANY)

    hbm = pl.BlockSpec(memory_space=pltpu.HBM)
    sds = jax.ShapeDtypeStruct
    ahead = pl.pallas_call(
        functools.partial(ahead_kernel, comps, planes, tiles),
        out_shape=sds((comps * tiles, 2, LANES), f32),
        in_specs=[hbm],
        out_specs=vmem,
        scratch_shapes=[pltpu.SemaphoreType.DMA((6,))],
        compiler_params=params(8),
        name="ahead",
    )(stay(flat.reshape(comps * tiles, planes // 2, 2, LANES)))
    beside, low, high = pl.pallas_call(
        functools.partial(pack_kernel, comps, planes, tiles),
        out_shape=(
            sds((comps, 2, tiles, LANES), f32),
            sds((comps // 2, planes, LANES), f32),
            sds((comps // 2, planes, LANES), f32),
        ),
        in_specs=[vmem],
        out_specs=[vmem] * 3,
        compiler_params=params(16),
        name="pack",
    )(flat)

    outer = [(i, (i + 1) % gx) for i in range(1, gx, 2)]
    outer = outer + [(t, s) for s, t in outer]
    inner = [(i, i + 1) for i in range(0, gx, 2)]
    inner = inner + [(t, s) for s, t in inner]
    forward = [(i, (i + 1) % gy) for i in range(gy)]
    backward = [(t, s) for s, t in forward]
    ha = lax.ppermute(ahead, "gx", outer)
    hb = lax.ppermute(beside, "gx", inner)
    zl = lax.ppermute(high, "gy", forward)
    zh = lax.ppermute(low, "gy", backward)

    padded = pl.cdiv(nreact, LANES) * LANES
    wide = pl.cdiv(nreact, 16) * 16
    part = pl.pallas_call(
        functools.partial(main_kernel, comps, planes, tiles, nreact),
        out_shape=sds((comps * rows, LANES), f32),
        in_specs=[vmem, smem] + [hbm] * 5 + [smem, smem],
        out_specs=vmem,
        scratch_shapes=[
            VMEM((nreact,), f32),
            VMEM((nreact,), f32),
            VMEM((nreact,), f32),
            VMEM((comps - 1, 2 * nreact), f32),
            VMEM((comps - 1, nreact), f32),
            VMEM((PIECE, padded), f32),
            VMEM((2 * PIECE, padded), f32),
            VMEM((wide, 3 * PIECE), jnp.bfloat16),
            VMEM((2 * PIECE, 2 * padded), jnp.bfloat16),
            VMEM((PIECE, GROUP * LANES), f32),
            VMEM((1, GROUP * LANES), f32),
            VMEM((1, GROUP * LANES), f32),
            VMEM((2 * LANES, 2 * LANES), jnp.bfloat16),
            VMEM((many_of(comps) * rows, 2 * LANES), f32),
            VMEM((many_of(comps) * rows, 2 * LANES), f32),
            SMEM((rows + 1,), jnp.int32),
            pltpu.SemaphoreType.DMA((5,)),
        ],
        compiler_params=params(24),
        cost_estimate=pl.CostEstimate(
            flops=2_000_000_000, bytes_accessed=16_000_000, transcendentals=1_000_000
        ),
        name="main",
    )(
        flat,
        diffusivity,
        stay(log_prefactor),
        stay(activation),
        stay(heat),
        stay(reactants.T),
        stay(products),
        substeps,
        flame,
    )

    whole = sds((comps * rows, LANES), f32)
    cost = pl.CostEstimate(flops=1_000_000, bytes_accessed=3_000_000, transcendentals=0)
    part = pl.pallas_call(
        functools.partial(inner_edges_kernel, comps, planes, tiles),
        out_shape=whole,
        in_specs=[vmem, smem, vmem, vmem, vmem],
        out_specs=vmem,
        input_output_aliases={0: 0},
        compiler_params=params(16),
        cost_estimate=cost,
        name="inner_edges",
    )(part, diffusivity, hb, zl, zh)
    parts = 6
    _, out = pl.pallas_call(
        functools.partial(outer_edges_kernel, comps, planes, tiles, parts),
        out_shape=(whole, whole),
        in_specs=[vmem, smem, vmem],
        out_specs=(vmem, anywhere),
        scratch_shapes=[pltpu.SemaphoreType.DMA((parts,))],
        input_output_aliases={0: 0},
        compiler_params=params(16),
        cost_estimate=cost,
        name="outer_edges",
    )(part, diffusivity, ha.reshape(comps * tiles * 2, LANES))
    return (
        out.reshape(comps, tiles, planes, LANES).transpose(0, 2, 1, 3).reshape(comps, planes, cells)
    )


def solution(mesh):
    in_specs = (P(None, "gx", "gy"), P(), P(), P(), P(), P(), P(), P("gx", "gy"), P("gx", "gy"))
    out_specs = P(None, "gx", "gy")

    return jax.shard_map(
        per_device, mesh=mesh, in_specs=in_specs, out_specs=out_specs, check_vma=False
    )
```

```python
import functools

import jax
import jax.numpy as jnp
import numpy as np
from jax import lax
from jax.experimental import pallas as pl
from jax.experimental.pallas import tpu as pltpu
from jax.sharding import PartitionSpec as P

NZ = 32
LANES = 128
near_weight = 4.0 / 3.0
far_weight = 1.0 / 12.0
LOG2E = 1.4426950408889634
GROUP = 4
PIECE = 64


VMEM = pltpu.VMEM
SMEM = pltpu.SMEM


def params(mib):
    return pltpu.CompilerParams(vmem_limit_bytes=mib << 20)


def odd_place(axis):
    return lax.rem(lax.axis_index(axis), 2)


def ahead_kernel(comps, planes, tiles, s_hbm, o_ref, sem):
    pair = odd_place("gx") * (planes // 2 - 1)
    total = comps * tiles
    parts = sem.shape[0]
    copies = []
    for i in range(parts):
        begin, end = total * i // parts, total * (i + 1) // parts
        where = pl.ds(begin, end - begin)
        copies.append(pltpu.make_async_copy(s_hbm.at[where, pair], o_ref.at[where], sem.at[i]))
        copies[-1].start()
    for copy in copies:
        copy.wait()


def pack_kernel(comps, planes, tiles, s_ref, b_ref, low_ref, high_ref):
    rows = planes * tiles
    lane = lax.broadcasted_iota(jnp.int32, (planes, LANES), 1)
    off_b = (1 - odd_place("gx")) * (planes - 2)
    for c in range(comps):
        for p in range(2):
            b_ref[c, p] = s_ref[pl.ds(c * rows + off_b + p, tiles, stride=planes), :]
    last = (tiles - 1) * planes
    for k in range(comps // 2):
        first, second = 2 * k * rows, (2 * k + 1) * rows
        low_a = s_ref[first : first + planes, :]
        low_b = s_ref[second : second + planes, :]
        high_a = s_ref[first + last : first + last + planes, :]
        high_b = s_ref[second + last : second + last + planes, :]
        low_ref[k] = jnp.where(lane < 64, low_a, pltpu.roll(low_b, 64, 1))
        high_ref[k] = jnp.where(lane < 64, pltpu.roll(high_a, 64, 1), high_b)


def split3(value):
    high = value.astype(jnp.bfloat16)
    rest = value - high.astype(jnp.float32)
    middle = rest.astype(jnp.bfloat16)
    low = (rest - middle.astype(jnp.float32)).astype(jnp.bfloat16)
    return high, middle, low


def shift_matrix():
    source = np.arange(LANES)[:, None]
    target = np.arange(LANES)[None, :]
    rows = LANES // NZ
    ys, yt = source // NZ, target // NZ
    turn = (target - source) % NZ
    same_z = turn == 0
    weights = {1: 16.0, 2: -1.0}
    own = np.where(source == target, -90.0, 0.0)
    cross = np.zeros_like(own)
    apart = np.where(target < LANES // 2, yt + rows - ys, ys + rows - yt)
    for distance, weight in weights.items():
        own += np.where((ys == yt) & (np.minimum(turn, NZ - turn) == distance), weight, 0.0)
        own += np.where(same_z & (abs(yt - ys) == distance), weight, 0.0)
        cross += np.where(same_z & (apart == distance), weight, 0.0)
    one = np.concatenate([own, cross], 1)
    return jnp.asarray(np.concatenate([one, one], 0), jnp.bfloat16)


def many_of(comps):
    return max(n for n in range(1, 7) if comps % n == 0)


def main_kernel(
    comps,
    planes,
    tiles,
    nreact,
    s_ref,
    shift_ref,
    d_hbm,
    sub_hbm,
    flame_hbm,
    lp_hbm,
    act_hbm,
    heat_hbm,
    rt_hbm,
    pr_hbm,
    o_ref,
    dv_ref,
    d_ref,
    sub_ref,
    flame_ref,
    lp_ref,
    act_ref,
    heat_ref,
    rt_ref,
    pr_ref,
    q_ref,
    p_ref,
    w1_ref,
    w2_ref,
    a_ref,
    old_ref,
    t_ref,
    st_ref,
    even_ref,
    odd_ref,
    pos_ref,
    sem,
):
    rows = planes * tiles
    species = comps - 1
    block_rows = planes * tiles
    loads = [
        pltpu.make_async_copy(source, target, sem.at[i])
        for i, (source, target) in enumerate(
            (
                (d_hbm, d_ref),
                (sub_hbm, sub_ref),
                (flame_hbm, flame_ref),
                (lp_hbm, lp_ref),
                (act_hbm, act_ref),
                (heat_hbm, heat_ref),
                (rt_hbm, rt_ref),
                (pr_hbm, pr_ref),
            )
        )
    ]
    for load in loads:
        load.start()

    def scan_blocks():
        for load in loads[:3]:
            load.wait()
        count = jnp.int32(0)
        for x in range(planes):
            for b in range(tiles):
                pos_ref[count] = b * planes + x
                count = count + flame_ref[x, b]
        for c in range(comps):
            dv_ref[c * planes : (c + 1) * planes, :] = jnp.full(
                (planes, LANES), d_ref[c], jnp.float32
            )
        return count

    padded = q_ref.shape[1]
    wide = w1_ref.shape[0]

    def tables():
        q_ref[...] = jnp.zeros_like(q_ref)
        p_ref[...] = jnp.zeros_like(p_ref)
        q_ref[0:species, 0:nreact] = rt_ref[:, 0:nreact] + rt_ref[:, nreact : 2 * nreact]
        p_ref[0:species, 0:nreact] = pr_ref[...]
        p_ref[PIECE : PIECE + species, 0:nreact] = q_ref[0:species, 0:nreact]
        for i, piece in enumerate(split3(act_ref[...].reshape(1, nreact) * (-LOG2E))):
            q_ref[species + i : species + i + 1, 0:nreact] = piece.astype(jnp.float32)
        for i, piece in enumerate(split3(lp_ref[...].reshape(1, nreact) * LOG2E)):
            q_ref[species + 3 + i : species + 4 + i, 0:nreact] = piece.astype(jnp.float32)
        for i, piece in enumerate(split3(heat_ref[...].reshape(1, nreact))):
            p_ref[species + i : species + i + 1, 0:nreact] = piece.astype(jnp.float32)
        q = q_ref[...]
        w1 = jnp.transpose(jnp.concatenate([q, q, q], 0))
        w1_ref[...] = w1[0:wide].astype(jnp.bfloat16)
        w = p_ref[...].astype(jnp.bfloat16)
        head, rest = w[:, :256], w[:, 256:padded]
        w2_ref[...] = jnp.concatenate([head, head, rest, rest], 1)
        a_ref[...] = jnp.ones_like(a_ref)

    many = many_of(comps)
    size = many * rows
    groups = comps // many
    shape = (many, tiles, planes, LANES)
    lane = lax.broadcasted_iota(jnp.int32, (1, 1, planes, LANES), 3)
    x = lax.broadcasted_iota(jnp.int32, (1, 1, planes, LANES), 2)
    zero = jnp.zeros((many, 1, planes, LANES), jnp.float32)
    near, far = near_weight * 12.0, -far_weight * 12.0
    weights = {
        -1: jnp.where(x > 0, near, 0.0),
        1: jnp.where(x < planes - 1, near, 0.0),
        -2: jnp.where(x > 1, far, 0.0),
        2: jnp.where(x < planes - 2, far, 0.0),
    }

    def product(i, buffer):
        flat = s_ref[pl.ds(pl.multiple_of(i * size, size), size), :]
        high = flat.astype(jnp.bfloat16)
        low = (flat - high.astype(jnp.float32)).astype(jnp.bfloat16)
        both = jnp.concatenate([high, low], 1)
        buffer[...] = jnp.dot(both, shift_ref[...], preferred_element_type=jnp.float32)

    def combine(i, buffer, inside):
        start = pl.multiple_of(i * size, size)
        v = s_ref[pl.ds(start, size), :].reshape(shape)
        own = buffer[:, :LANES].reshape(shape)
        cross = buffer[:, LANES:].reshape(shape)
        before = jnp.concatenate([zero, cross[:, :-1]], 1)
        after = jnp.concatenate([cross[:, 1:], zero], 1)
        own = own + jnp.where(lane < 64, before, after)
        for offset, weight in weights.items():
            if inside:
                moved = s_ref[pl.ds(start + offset, size), :].reshape(shape)
            else:
                moved = pltpu.roll(v, (-offset) % planes, 2)
            own = own + moved * weight
        for j in range(many):
            where = pl.ds(pl.multiple_of(start + j * rows, rows), rows)
            scale = d_ref[i * many + j] * (1.0 / 12.0)
            o_ref[where, :] = (v[j] + scale * own[j]).reshape(rows, LANES)

    product(0, even_ref)
    if groups % 2 == 1 and groups > 2:
        product(1, odd_ref)
        count = scan_blocks()
        combine(0, even_ref, False)

        def two(i, carry):
            g = 2 * i + 1
            product(g + 1, even_ref)
            combine(g, odd_ref, True)
            product(g + 2, odd_ref)
            combine(g + 1, even_ref, True)
            return carry

        lax.fori_loop(0, (groups - 3) // 2, two, 0)
        for load in loads[3:]:
            load.wait()
        product(groups - 1, even_ref)
        tables()
        combine(groups - 2, odd_ref, True)
        combine(groups - 1, even_ref, False)
    else:
        count = scan_blocks()
        for load in loads[3:]:
            load.wait()
        tables()
        for i in range(groups):
            combine(i, even_ref, False)
            if i < groups - 1:
                product(i + 1, even_ref)

    @pl.when(count > 0)
    def _():
        arow = lax.broadcasted_iota(jnp.int32, a_ref.shape, 0)

        def group(g, carry):
            most = jnp.int32(0)
            pieces = []
            for i in range(GROUP):
                slot = g * GROUP + i
                here = jnp.where(slot < count, slot, 0)
                at = pos_ref[here]
                n = jnp.where(
                    slot < count, sub_ref[lax.rem(at, planes), lax.div(at, planes)], 0
                )
                most = jnp.maximum(most, n)
                cols = slice(i * LANES, (i + 1) * LANES)
                mine = s_ref[pl.ds(block_rows + at, species, stride=rows), :]
                a_ref[0:species, cols] = mine
                old_ref[0:species, cols] = mine
                t_ref[:, cols] = s_ref[pl.ds(at, 1), :]
                pieces.append(jnp.full((1, LANES), n, jnp.int32))
            counts = jnp.concatenate(pieces, 1)
            st_ref[...] = 1.0 / jnp.maximum(counts, 1).astype(jnp.float32)

            def substep(k, inner):
                step = jnp.where(counts > k, st_ref[...], 0.0)
                amounts = a_ref[...]
                thermal = t_ref[...]
                inverse = 1.0 / thermal
                terms = jnp.where(
                    arow < species,
                    jnp.log2(amounts),
                    jnp.where(
                        arow < species + 3, inverse, jnp.where(arow < species + 6, 1.0, 0.0)
                    ),
                )
                rhs = jnp.concatenate(split3(terms), 0)
                exponent = jnp.dot(w1_ref[...], rhs, preferred_element_type=jnp.float32)
                progress = jnp.exp2(exponent)
                high = progress.astype(jnp.bfloat16)
                low = (progress - high.astype(jnp.float32)).astype(jnp.bfloat16)
                gap = 2 * LANES - wide + LANES
                rhs = jnp.concatenate(
                    [high[:256], low[:256], high[256:], high[:gap], low[256:], low[:gap]], 0
                )
                out = jnp.dot(w2_ref[...], rhs, preferred_element_type=jnp.float32)
                produced = out[:PIECE]
                loss = out[PIECE:]
                warm = out[species : species + 1] + (
                    out[species + 1 : species + 2] + out[species + 2 : species + 3]
                )
                a_ref[...] = (amounts + step * produced) * (amounts / (amounts + step * loss))
                t_ref[...] = thermal + step * warm
                return inner

            lax.fori_loop(0, most, substep, 0)

            for i in range(GROUP):
                slot = g * GROUP + i

                @pl.when(slot < count)
                def _(i=i, slot=slot):
                    at = pos_ref[slot]
                    cols = slice(i * LANES, (i + 1) * LANES)
                    where = pl.ds(block_rows + at, species, stride=rows)
                    change = a_ref[0:species, cols] - old_ref[0:species, cols]
                    o_ref[where, :] = o_ref[where, :] + change
                    top = pl.ds(at, 1)
                    o_ref[top, :] = o_ref[top, :] + (t_ref[:, cols] - s_ref[top, :])

            return carry

        lax.fori_loop(0, (count + (GROUP - 1)) // GROUP, group, 0)


def add_planes(planes, tiles, work, dv_ref, plane, begin, end, side):
    rows = planes * tiles
    for c in range(begin, end):
        near = plane(c, 1 - side)
        far = plane(c, side)
        weight = dv_ref[c * planes : (c + 1) * planes, :]
        first = pl.ds(c * rows + side * (planes - 1), tiles, stride=planes)
        second = pl.ds(c * rows + 1 + side * (planes - 3), tiles, stride=planes)
        one, two = work[first, :], work[second, :]
        work[first, :] = one + weight * (near_weight * near - far_weight * far)
        work[second, :] = two - (weight * far_weight) * near


def inner_edges_kernel(comps, planes, tiles, part_ref, dv_ref, hb_ref, zl_ref, zh_ref, work):
    del part_ref
    rows = planes * tiles
    lane = lax.broadcasted_iota(jnp.int32, (planes, LANES), 1)
    last = (tiles - 1) * planes
    above = jnp.where(lane % 64 < NZ, near_weight, 0.0)
    below = jnp.where(lane % 64 >= NZ, near_weight, 0.0)
    lower = jnp.where(lane < 64, 1.0, 0.0)
    upper = jnp.where(lane < 64, 0.0, 1.0)

    def pair(k, carry):
        low, high = zl_ref[k], zh_ref[k]
        low = pltpu.roll(low, LANES - NZ, 1) * above - far_weight * low
        high = pltpu.roll(high, NZ, 1) * below - far_weight * high
        lows = (low * lower, pltpu.roll(low * upper, 64, 1))
        highs = (pltpu.roll(high * lower, 64, 1), high * upper)
        for j in range(2):
            weight = dv_ref[pl.ds(pl.multiple_of((2 * k + j) * planes, planes), planes), :]
            base = pl.multiple_of((2 * k + j) * rows, planes)
            top = pl.ds(base, planes)
            end = pl.ds(pl.multiple_of(base + last, planes), planes)
            work[top, :] = work[top, :] + weight * lows[j]
            work[end, :] = work[end, :] + weight * highs[j]
        return carry

    for k in range(comps // 2):
        pair(k, 0)
    odd = odd_place("gx")
    for side in range(2):

        @pl.when(odd == 1 - side)
        def _(side=side):
            add_planes(
                planes, tiles, work, dv_ref, lambda c, p: hb_ref[c, p], 0, comps, side
            )


def outer_edges_kernel(comps, planes, tiles, parts, part_ref, dv_ref, h_ref, work, out, sem):
    del part_ref
    rows = planes * tiles
    odd = odd_place("gx")

    def plane(c, p):
        return h_ref[pl.ds(c * 2 * tiles + p, tiles, stride=2), :]

    def send(i, first, last):
        where = pl.ds(first * rows, (last - first) * rows)
        return pltpu.make_async_copy(work.at[where, :], out.at[where, :], sem.at[i])

    bounds = [comps * i // parts for i in range(parts + 1)]
    spans = list(zip(bounds, bounds[1:]))
    for side in range(2):

        @pl.when(odd == side)
        def _(side=side):
            for i, (first, last) in enumerate(spans):
                add_planes(planes, tiles, work, dv_ref, plane, first, last, side)
                send(i, first, last).start()

    for i, (first, last) in enumerate(spans):
        send(i, first, last).wait()


def per_device(
    state, diffusivity, log_prefactor, activation, heat, reactants, products, substeps, flame
):
    comps, planes, cells = state.shape
    tiles = cells // LANES
    rows = planes * tiles
    nreact = log_prefactor.shape[0]
    gx, gy = lax.axis_size("gx"), lax.axis_size("gy")
    f32 = jnp.float32
    flat = (
        state.reshape(comps, planes, tiles, LANES)
        .transpose(0, 2, 1, 3)
        .reshape(comps * rows, LANES)
    )

    def stay(array):
        return pltpu.with_memory_space_constraint(array, pltpu.HBM)

    vmem = pl.BlockSpec(memory_space=VMEM)
    anywhere = pl.BlockSpec(memory_space=pl.ANY)

    hbm = pl.BlockSpec(memory_space=pltpu.HBM)
    sds = jax.ShapeDtypeStruct
    ahead = pl.pallas_call(
        functools.partial(ahead_kernel, comps, planes, tiles),
        out_shape=sds((comps * tiles, 2, LANES), f32),
        in_specs=[hbm],
        out_specs=vmem,
        scratch_shapes=[pltpu.SemaphoreType.DMA((1,))],
        compiler_params=params(8),
        name="ahead",
    )(stay(flat.reshape(comps * tiles, planes // 2, 2, LANES)))
    beside, low, high = pl.pallas_call(
        functools.partial(pack_kernel, comps, planes, tiles),
        out_shape=(
            sds((comps, 2, tiles, LANES), f32),
            sds((comps // 2, planes, LANES), f32),
            sds((comps // 2, planes, LANES), f32),
        ),
        in_specs=[vmem],
        out_specs=[vmem] * 3,
        compiler_params=params(16),
        name="pack",
    )(flat)

    outer = [(i, (i + 1) % gx) for i in range(1, gx, 2)]
    outer = outer + [(t, s) for s, t in outer]
    inner = [(i, i + 1) for i in range(0, gx, 2)]
    inner = inner + [(t, s) for s, t in inner]
    forward = [(i, (i + 1) % gy) for i in range(gy)]
    backward = [(t, s) for s, t in forward]
    ha = lax.ppermute(ahead, "gx", outer)
    hb = lax.ppermute(beside, "gx", inner)
    zl = lax.ppermute(high, "gy", forward)
    zh = lax.ppermute(low, "gy", backward)

    padded = pl.cdiv(nreact, LANES) * LANES
    wide = pl.cdiv(nreact, 16) * 16
    part, dv = pl.pallas_call(
        functools.partial(main_kernel, comps, planes, tiles, nreact),
        out_shape=(sds((comps * rows, LANES), f32), sds((comps * planes, LANES), f32)),
        in_specs=[vmem, vmem] + [hbm] * 8,
        out_specs=(vmem, vmem),
        scratch_shapes=[
            SMEM((comps,), f32),
            SMEM(substeps.shape, jnp.int32),
            SMEM(flame.shape, jnp.int32),
            VMEM((nreact,), f32),
            VMEM((nreact,), f32),
            VMEM((nreact,), f32),
            VMEM((comps - 1, 2 * nreact), f32),
            VMEM((comps - 1, nreact), f32),
            VMEM((PIECE, padded), f32),
            VMEM((2 * PIECE, padded), f32),
            VMEM((wide, 3 * PIECE), jnp.bfloat16),
            VMEM((2 * PIECE, 2 * padded), jnp.bfloat16),
            VMEM((PIECE, GROUP * LANES), f32),
            VMEM((PIECE, GROUP * LANES), f32),
            VMEM((1, GROUP * LANES), f32),
            VMEM((1, GROUP * LANES), f32),
            VMEM((many_of(comps) * rows, 2 * LANES), f32),
            VMEM((many_of(comps) * rows, 2 * LANES), f32),
            SMEM((rows + 1,), jnp.int32),
            pltpu.SemaphoreType.DMA((8,)),
        ],
        compiler_params=params(24),
        cost_estimate=pl.CostEstimate(
            flops=2_000_000_000, bytes_accessed=16_000_000, transcendentals=1_000_000
        ),
        name="main",
    )(
        flat,
        shift_matrix(),
        *map(
            stay,
            (
                diffusivity,
                substeps,
                flame,
                log_prefactor,
                activation,
                heat,
                reactants.T,
                products,
            ),
        ),
    )

    whole = sds((comps * rows, LANES), f32)
    cost = pl.CostEstimate(flops=1_000_000, bytes_accessed=3_000_000, transcendentals=0)
    part = pl.pallas_call(
        functools.partial(inner_edges_kernel, comps, planes, tiles),
        out_shape=whole,
        in_specs=[vmem] * 5,
        out_specs=vmem,
        input_output_aliases={0: 0},
        compiler_params=params(16),
        cost_estimate=cost,
        name="inner_edges",
    )(part, dv, hb, zl, zh)
    parts = 3
    _, out = pl.pallas_call(
        functools.partial(outer_edges_kernel, comps, planes, tiles, parts),
        out_shape=(whole, whole),
        in_specs=[vmem] * 3,
        out_specs=(vmem, anywhere),
        scratch_shapes=[pltpu.SemaphoreType.DMA((parts,))],
        input_output_aliases={0: 0},
        compiler_params=params(16),
        cost_estimate=cost,
        name="outer_edges",
    )(part, dv, ha.reshape(comps * tiles * 2, LANES))
    return (
        out.reshape(comps, tiles, planes, LANES).transpose(0, 2, 1, 3).reshape(comps, planes, cells)
    )


def solution(mesh):
    in_specs = (P(None, "gx", "gy"), P(), P(), P(), P(), P(), P(), P("gx", "gy"), P("gx", "gy"))
    out_specs = P(None, "gx", "gy")

    return jax.shard_map(
        per_device, mesh=mesh, in_specs=in_specs, out_specs=out_specs, check_vma=False
    )
```

```python
import functools

import jax
import jax.numpy as jnp
import numpy as np
from jax import lax
from jax.experimental import pallas as pl
from jax.experimental.pallas import tpu as pltpu
from jax.sharding import PartitionSpec as P

NZ = 32
LANES = 128
near_weight = 4.0 / 3.0
far_weight = 1.0 / 12.0
LOG2E = 1.4426950408889634
GROUP = 4
PIECE = 64


VMEM = pltpu.VMEM
SMEM = pltpu.SMEM


def params(mib):
    return pltpu.CompilerParams(vmem_limit_bytes=mib << 20)


def odd_place(axis):
    return lax.rem(lax.axis_index(axis), 2)


def ahead_kernel(comps, planes, tiles, s_hbm, o_ref, sem):
    pair = odd_place("gx") * (planes // 2 - 1)
    total = comps * tiles
    parts = sem.shape[0]
    copies = []
    for i in range(parts):
        begin, end = total * i // parts, total * (i + 1) // parts
        where = pl.ds(begin, end - begin)
        copies.append(pltpu.make_async_copy(s_hbm.at[where, pair], o_ref.at[where], sem.at[i]))
        copies[-1].start()
    for copy in copies:
        copy.wait()


def pack_kernel(comps, planes, tiles, s_ref, b_ref, low_ref, high_ref):
    rows = planes * tiles
    lane = lax.broadcasted_iota(jnp.int32, (planes, LANES), 1)
    off_b = (1 - odd_place("gx")) * (planes - 2)
    for c in range(comps):
        for p in range(2):
            b_ref[c, p] = s_ref[pl.ds(c * rows + off_b + p, tiles, stride=planes), :]
    last = (tiles - 1) * planes
    for k in range(comps // 2):
        first, second = 2 * k * rows, (2 * k + 1) * rows
        low_a = s_ref[first : first + planes, :]
        low_b = s_ref[second : second + planes, :]
        high_a = s_ref[first + last : first + last + planes, :]
        high_b = s_ref[second + last : second + last + planes, :]
        low_ref[k] = jnp.where(lane < 64, low_a, pltpu.roll(low_b, 64, 1))
        high_ref[k] = jnp.where(lane < 64, pltpu.roll(high_a, 64, 1), high_b)


def split3(value):
    high = value.astype(jnp.bfloat16)
    rest = value - high.astype(jnp.float32)
    middle = rest.astype(jnp.bfloat16)
    low = (rest - middle.astype(jnp.float32)).astype(jnp.bfloat16)
    return high, middle, low


def shift_matrix():
    source = np.arange(LANES)[:, None]
    target = np.arange(LANES)[None, :]
    rows = LANES // NZ
    ys, yt = source // NZ, target // NZ
    turn = (target - source) % NZ
    same_z = turn == 0
    weights = {1: 16.0, 2: -1.0}
    own = np.where(source == target, -90.0, 0.0)
    cross = np.zeros_like(own)
    apart = np.where(target < LANES // 2, yt + rows - ys, ys + rows - yt)
    for distance, weight in weights.items():
        own += np.where((ys == yt) & (np.minimum(turn, NZ - turn) == distance), weight, 0.0)
        own += np.where(same_z & (abs(yt - ys) == distance), weight, 0.0)
        cross += np.where(same_z & (apart == distance), weight, 0.0)
    one = np.concatenate([own, cross], 1)
    return jnp.asarray(np.concatenate([one, one], 0), jnp.bfloat16)


def many_of(comps):
    return max(n for n in range(1, 7) if comps % n == 0)


def main_kernel(
    comps,
    planes,
    tiles,
    nreact,
    s_ref,
    shift_ref,
    d_hbm,
    sub_hbm,
    flame_hbm,
    lp_hbm,
    act_hbm,
    heat_hbm,
    rt_hbm,
    pr_hbm,
    o_ref,
    dv_ref,
    d_ref,
    sub_ref,
    flame_ref,
    lp_ref,
    act_ref,
    heat_ref,
    rt_ref,
    pr_ref,
    q_ref,
    p_ref,
    w1_ref,
    w2_ref,
    a_ref,
    old_ref,
    t_ref,
    st_ref,
    even_ref,
    odd_ref,
    pos_ref,
    sem,
):
    rows = planes * tiles
    species = comps - 1
    block_rows = planes * tiles
    loads = [
        pltpu.make_async_copy(source, target, sem.at[i])
        for i, (source, target) in enumerate(
            (
                (d_hbm, d_ref),
                (sub_hbm, sub_ref),
                (flame_hbm, flame_ref),
                (lp_hbm, lp_ref),
                (act_hbm, act_ref),
                (heat_hbm, heat_ref),
                (rt_hbm, rt_ref),
                (pr_hbm, pr_ref),
            )
        )
    ]
    for load in loads:
        load.start()

    def scan_blocks():
        for load in loads[:3]:
            load.wait()
        count = jnp.int32(0)
        for x in range(planes):
            for b in range(tiles):
                pos_ref[count] = b * planes + x
                count = count + flame_ref[x, b]
        for c in range(comps):
            dv_ref[c * planes : (c + 1) * planes, :] = jnp.full(
                (planes, LANES), d_ref[c], jnp.float32
            )
        return count

    padded = q_ref.shape[1]
    wide = w1_ref.shape[0]

    def tables():
        q_ref[...] = jnp.zeros_like(q_ref)
        p_ref[...] = jnp.zeros_like(p_ref)
        q_ref[0:species, 0:nreact] = rt_ref[:, 0:nreact] + rt_ref[:, nreact : 2 * nreact]
        p_ref[0:species, 0:nreact] = pr_ref[...]
        p_ref[PIECE : PIECE + species, 0:nreact] = q_ref[0:species, 0:nreact]
        for i, piece in enumerate(split3(act_ref[...].reshape(1, nreact) * (-LOG2E))):
            q_ref[species + i : species + i + 1, 0:nreact] = piece.astype(jnp.float32)
        for i, piece in enumerate(split3(lp_ref[...].reshape(1, nreact) * LOG2E)):
            q_ref[species + 3 + i : species + 4 + i, 0:nreact] = piece.astype(jnp.float32)
        for i, piece in enumerate(split3(heat_ref[...].reshape(1, nreact))):
            p_ref[species + i : species + i + 1, 0:nreact] = piece.astype(jnp.float32)
        q = q_ref[...]
        w1 = jnp.transpose(jnp.concatenate([q, q, q], 0))
        w1_ref[...] = w1[0:wide].astype(jnp.bfloat16)
        w = p_ref[...].astype(jnp.bfloat16)
        head, rest = w[:, :256], w[:, 256:padded]
        w2_ref[...] = jnp.concatenate([head, head, rest, rest], 1)
        a_ref[...] = jnp.ones_like(a_ref)

    many = many_of(comps)
    size = many * rows
    groups = comps // many
    shape = (many, tiles, planes, LANES)
    lane = lax.broadcasted_iota(jnp.int32, (1, 1, planes, LANES), 3)
    x = lax.broadcasted_iota(jnp.int32, (1, 1, planes, LANES), 2)
    zero = jnp.zeros((many, 1, planes, LANES), jnp.float32)
    near, far = near_weight * 12.0, -far_weight * 12.0
    weights = {
        -1: jnp.where(x > 0, near, 0.0),
        1: jnp.where(x < planes - 1, near, 0.0),
        -2: jnp.where(x > 1, far, 0.0),
        2: jnp.where(x < planes - 2, far, 0.0),
    }

    def product(i, buffer):
        flat = s_ref[pl.ds(pl.multiple_of(i * size, size), size), :]
        high = flat.astype(jnp.bfloat16)
        low = (flat - high.astype(jnp.float32)).astype(jnp.bfloat16)
        both = jnp.concatenate([high, low], 1)
        buffer[...] = jnp.dot(both, shift_ref[...], preferred_element_type=jnp.float32)

    def combine(i, buffer, inside):
        start = pl.multiple_of(i * size, size)
        v = s_ref[pl.ds(start, size), :].reshape(shape)
        own = buffer[:, :LANES].reshape(shape)
        cross = buffer[:, LANES:].reshape(shape)
        before = jnp.concatenate([zero, cross[:, :-1]], 1)
        after = jnp.concatenate([cross[:, 1:], zero], 1)
        own = own + jnp.where(lane < 64, before, after)
        for offset, weight in weights.items():
            if inside:
                moved = s_ref[pl.ds(start + offset, size), :].reshape(shape)
            else:
                moved = pltpu.roll(v, (-offset) % planes, 2)
            own = own + moved * weight
        for j in range(many):
            where = pl.ds(pl.multiple_of(start + j * rows, rows), rows)
            scale = d_ref[i * many + j] * (1.0 / 12.0)
            o_ref[where, :] = (v[j] + scale * own[j]).reshape(rows, LANES)

    product(0, even_ref)
    if groups % 2 == 1 and groups > 2:
        product(1, odd_ref)
        count = scan_blocks()
        combine(0, even_ref, False)

        def two(i, carry):
            g = 2 * i + 1
            product(g + 1, even_ref)
            combine(g, odd_ref, True)
            product(g + 2, odd_ref)
            combine(g + 1, even_ref, True)
            return carry

        lax.fori_loop(0, (groups - 3) // 2, two, 0)
        for load in loads[3:]:
            load.wait()
        product(groups - 1, even_ref)
        tables()
        combine(groups - 2, odd_ref, True)
        combine(groups - 1, even_ref, False)
    else:
        count = scan_blocks()
        for load in loads[3:]:
            load.wait()
        tables()
        for i in range(groups):
            combine(i, even_ref, False)
            if i < groups - 1:
                product(i + 1, even_ref)

    @pl.when(count > 0)
    def _():
        arow = lax.broadcasted_iota(jnp.int32, a_ref.shape, 0)

        def group(g, carry):
            most = jnp.int32(0)
            pieces = []
            for i in range(GROUP):
                slot = g * GROUP + i
                here = jnp.where(slot < count, slot, 0)
                at = pos_ref[here]
                n = jnp.where(
                    slot < count, sub_ref[lax.rem(at, planes), lax.div(at, planes)], 0
                )
                most = jnp.maximum(most, n)
                cols = slice(i * LANES, (i + 1) * LANES)
                mine = s_ref[pl.ds(block_rows + at, species, stride=rows), :]
                a_ref[0:species, cols] = mine
                old_ref[0:species, cols] = mine
                t_ref[:, cols] = s_ref[pl.ds(at, 1), :]
                pieces.append(jnp.full((1, LANES), n, jnp.int32))
            counts = jnp.concatenate(pieces, 1)
            st_ref[...] = 1.0 / jnp.maximum(counts, 1).astype(jnp.float32)

            def substep(k, inner):
                step = jnp.where(counts > k, st_ref[...], 0.0)
                amounts = a_ref[...]
                thermal = t_ref[...]
                inverse = 1.0 / thermal
                terms = jnp.where(
                    arow < species,
                    jnp.log2(amounts),
                    jnp.where(
                        arow < species + 3, inverse, jnp.where(arow < species + 6, 1.0, 0.0)
                    ),
                )
                rhs = jnp.concatenate(split3(terms), 0)
                exponent = jnp.dot(w1_ref[...], rhs, preferred_element_type=jnp.float32)
                progress = jnp.exp2(exponent)
                high = progress.astype(jnp.bfloat16)
                low = (progress - high.astype(jnp.float32)).astype(jnp.bfloat16)
                gap = 2 * LANES - wide + LANES
                rhs = jnp.concatenate(
                    [high[:256], low[:256], high[256:], high[:gap], low[256:], low[:gap]], 0
                )
                out = jnp.dot(w2_ref[...], rhs, preferred_element_type=jnp.float32)
                produced = out[:PIECE]
                loss = out[PIECE:]
                warm = out[species : species + 1] + (
                    out[species + 1 : species + 2] + out[species + 2 : species + 3]
                )
                a_ref[...] = (amounts + step * produced) * (amounts / (amounts + step * loss))
                t_ref[...] = thermal + step * warm
                return inner

            lax.fori_loop(0, most, substep, 0)

            for i in range(GROUP):
                slot = g * GROUP + i

                @pl.when(slot < count)
                def _(i=i, slot=slot):
                    at = pos_ref[slot]
                    cols = slice(i * LANES, (i + 1) * LANES)
                    where = pl.ds(block_rows + at, species, stride=rows)
                    change = a_ref[0:species, cols] - old_ref[0:species, cols]
                    o_ref[where, :] = o_ref[where, :] + change
                    top = pl.ds(at, 1)
                    o_ref[top, :] = o_ref[top, :] + (t_ref[:, cols] - s_ref[top, :])

            return carry

        lax.fori_loop(0, (count + (GROUP - 1)) // GROUP, group, 0)


def add_planes(planes, tiles, work, dv_ref, plane, begin, end, side):
    rows = planes * tiles
    for c in range(begin, end):
        near = plane(c, 1 - side)
        far = plane(c, side)
        weight = dv_ref[c * planes : (c + 1) * planes, :]
        first = pl.ds(c * rows + side * (planes - 1), tiles, stride=planes)
        second = pl.ds(c * rows + 1 + side * (planes - 3), tiles, stride=planes)
        one, two = work[first, :], work[second, :]
        work[first, :] = one + weight * (near_weight * near - far_weight * far)
        work[second, :] = two - (weight * far_weight) * near


def inner_edges_kernel(comps, planes, tiles, part_ref, dv_ref, hb_ref, zl_ref, zh_ref, work):
    del part_ref
    rows = planes * tiles
    lane = lax.broadcasted_iota(jnp.int32, (planes, LANES), 1)
    last = (tiles - 1) * planes
    above = jnp.where(lane % 64 < NZ, near_weight, 0.0)
    below = jnp.where(lane % 64 >= NZ, near_weight, 0.0)
    lower = jnp.where(lane < 64, 1.0, 0.0)
    upper = jnp.where(lane < 64, 0.0, 1.0)

    def pair(k, carry):
        low, high = zl_ref[k], zh_ref[k]
        low = pltpu.roll(low, LANES - NZ, 1) * above - far_weight * low
        high = pltpu.roll(high, NZ, 1) * below - far_weight * high
        lows = (low * lower, pltpu.roll(low * upper, 64, 1))
        highs = (pltpu.roll(high * lower, 64, 1), high * upper)
        for j in range(2):
            weight = dv_ref[pl.ds(pl.multiple_of((2 * k + j) * planes, planes), planes), :]
            base = pl.multiple_of((2 * k + j) * rows, planes)
            top = pl.ds(base, planes)
            end = pl.ds(pl.multiple_of(base + last, planes), planes)
            work[top, :] = work[top, :] + weight * lows[j]
            work[end, :] = work[end, :] + weight * highs[j]
        return carry

    for k in range(comps // 2):
        pair(k, 0)
    odd = odd_place("gx")
    for side in range(2):

        @pl.when(odd == 1 - side)
        def _(side=side):
            add_planes(
                planes, tiles, work, dv_ref, lambda c, p: hb_ref[c, p], 0, comps, side
            )


def outer_edges_kernel(comps, planes, tiles, part_ref, dv_ref, h_ref, work, out, sem):
    del part_ref
    rows = planes * tiles
    odd = odd_place("gx")

    def plane(c, p):
        return h_ref[pl.ds(c * 2 * tiles + p, tiles, stride=2), :]

    def send(i, first, last):
        where = pl.ds(first * rows, (last - first) * rows)
        return pltpu.make_async_copy(work.at[where, :], out.at[where, :], sem.at[i])

    bounds = [0, comps // 9, comps // 3, comps]
    spans = list(zip(bounds, bounds[1:]))
    for side in range(2):

        @pl.when(odd == side)
        def _(side=side):
            for i, (first, last) in enumerate(spans):
                add_planes(planes, tiles, work, dv_ref, plane, first, last, side)
                send(i, first, last).start()

    for i, (first, last) in enumerate(spans):
        send(i, first, last).wait()


def per_device(
    state, diffusivity, log_prefactor, activation, heat, reactants, products, substeps, flame
):
    comps, planes, cells = state.shape
    tiles = cells // LANES
    rows = planes * tiles
    nreact = log_prefactor.shape[0]
    gx, gy = lax.axis_size("gx"), lax.axis_size("gy")
    f32 = jnp.float32
    flat = (
        state.reshape(comps, planes, tiles, LANES)
        .transpose(0, 2, 1, 3)
        .reshape(comps * rows, LANES)
    )

    def stay(array):
        return pltpu.with_memory_space_constraint(array, pltpu.HBM)

    vmem = pl.BlockSpec(memory_space=VMEM)
    anywhere = pl.BlockSpec(memory_space=pl.ANY)

    hbm = pl.BlockSpec(memory_space=pltpu.HBM)
    sds = jax.ShapeDtypeStruct
    ahead = pl.pallas_call(
        functools.partial(ahead_kernel, comps, planes, tiles),
        out_shape=sds((comps * tiles, 2, LANES), f32),
        in_specs=[hbm],
        out_specs=vmem,
        scratch_shapes=[pltpu.SemaphoreType.DMA((1,))],
        compiler_params=params(8),
        name="ahead",
    )(stay(flat.reshape(comps * tiles, planes // 2, 2, LANES)))
    beside, low, high = pl.pallas_call(
        functools.partial(pack_kernel, comps, planes, tiles),
        out_shape=(
            sds((comps, 2, tiles, LANES), f32),
            sds((comps // 2, planes, LANES), f32),
            sds((comps // 2, planes, LANES), f32),
        ),
        in_specs=[vmem],
        out_specs=[vmem] * 3,
        compiler_params=params(16),
        name="pack",
    )(flat)

    outer = [(i, (i + 1) % gx) for i in range(1, gx, 2)]
    outer = outer + [(t, s) for s, t in outer]
    inner = [(i, i + 1) for i in range(0, gx, 2)]
    inner = inner + [(t, s) for s, t in inner]
    forward = [(i, (i + 1) % gy) for i in range(gy)]
    backward = [(t, s) for s, t in forward]
    ha = lax.ppermute(ahead, "gx", outer)
    hb = lax.ppermute(beside, "gx", inner)
    zl = lax.ppermute(high, "gy", forward)
    zh = lax.ppermute(low, "gy", backward)

    padded = pl.cdiv(nreact, LANES) * LANES
    wide = pl.cdiv(nreact, 16) * 16
    part, dv = pl.pallas_call(
        functools.partial(main_kernel, comps, planes, tiles, nreact),
        out_shape=(sds((comps * rows, LANES), f32), sds((comps * planes, LANES), f32)),
        in_specs=[vmem, vmem] + [hbm] * 8,
        out_specs=(vmem, vmem),
        scratch_shapes=[
            SMEM((comps,), f32),
            SMEM(substeps.shape, jnp.int32),
            SMEM(flame.shape, jnp.int32),
            VMEM((nreact,), f32),
            VMEM((nreact,), f32),
            VMEM((nreact,), f32),
            VMEM((comps - 1, 2 * nreact), f32),
            VMEM((comps - 1, nreact), f32),
            VMEM((PIECE, padded), f32),
            VMEM((2 * PIECE, padded), f32),
            VMEM((wide, 3 * PIECE), jnp.bfloat16),
            VMEM((2 * PIECE, 2 * padded), jnp.bfloat16),
            VMEM((PIECE, GROUP * LANES), f32),
            VMEM((PIECE, GROUP * LANES), f32),
            VMEM((1, GROUP * LANES), f32),
            VMEM((1, GROUP * LANES), f32),
            VMEM((many_of(comps) * rows, 2 * LANES), f32),
            VMEM((many_of(comps) * rows, 2 * LANES), f32),
            SMEM((rows + 1,), jnp.int32),
            pltpu.SemaphoreType.DMA((8,)),
        ],
        compiler_params=params(24),
        cost_estimate=pl.CostEstimate(
            flops=2_000_000_000, bytes_accessed=16_000_000, transcendentals=1_000_000
        ),
        name="main",
    )(
        flat,
        shift_matrix(),
        *map(
            stay,
            (
                diffusivity,
                substeps,
                flame,
                log_prefactor,
                activation,
                heat,
                reactants.T,
                products,
            ),
        ),
    )

    whole = sds((comps * rows, LANES), f32)
    cost = pl.CostEstimate(flops=1_000_000, bytes_accessed=3_000_000, transcendentals=0)
    part = pl.pallas_call(
        functools.partial(inner_edges_kernel, comps, planes, tiles),
        out_shape=whole,
        in_specs=[vmem] * 5,
        out_specs=vmem,
        input_output_aliases={0: 0},
        compiler_params=params(16),
        cost_estimate=cost,
        name="inner_edges",
    )(part, dv, hb, zl, zh)
    _, out = pl.pallas_call(
        functools.partial(outer_edges_kernel, comps, planes, tiles),
        out_shape=(whole, whole),
        in_specs=[vmem] * 3,
        out_specs=(vmem, anywhere),
        scratch_shapes=[pltpu.SemaphoreType.DMA((3,))],
        input_output_aliases={0: 0},
        compiler_params=params(16),
        cost_estimate=cost,
        name="outer_edges",
    )(part, dv, ha.reshape(comps * tiles * 2, LANES))
    return (
        out.reshape(comps, tiles, planes, LANES).transpose(0, 2, 1, 3).reshape(comps, planes, cells)
    )


def solution(mesh):
    in_specs = (P(None, "gx", "gy"), P(), P(), P(), P(), P(), P(), P("gx", "gy"), P("gx", "gy"))
    out_specs = P(None, "gx", "gy")

    return jax.shard_map(
        per_device, mesh=mesh, in_specs=in_specs, out_specs=out_specs, check_vma=False
    )
```

```python
import functools

import jax
import jax.numpy as jnp
import numpy as np
from jax import lax
from jax.experimental import pallas as pl
from jax.experimental.pallas import tpu as pltpu
from jax.sharding import PartitionSpec as P

NZ = 32
LANES = 128
near_weight = 4.0 / 3.0
far_weight = 1.0 / 12.0
LOG2E = 1.4426950408889634
GROUP = 4
PIECE = 64


VMEM = pltpu.VMEM
SMEM = pltpu.SMEM


def params(mib):
    return pltpu.CompilerParams(vmem_limit_bytes=mib << 20)


def odd_place(axis):
    return lax.rem(lax.axis_index(axis), 2)


def ahead_kernel(comps, planes, tiles, s_hbm, o_ref, sem):
    pair = odd_place("gx") * (planes // 2 - 1)
    total = comps * tiles
    parts = sem.shape[0]
    copies = []
    for i in range(parts):
        begin, end = total * i // parts, total * (i + 1) // parts
        where = pl.ds(begin, end - begin)
        copies.append(pltpu.make_async_copy(s_hbm.at[where, pair], o_ref.at[where], sem.at[i]))
        copies[-1].start()
    for copy in copies:
        copy.wait()


def pack_kernel(comps, planes, tiles, s_ref, b_ref, low_ref, high_ref):
    rows = planes * tiles
    lane = lax.broadcasted_iota(jnp.int32, (planes, LANES), 1)
    off_b = (1 - odd_place("gx")) * (planes - 2)
    for c in range(comps):
        for p in range(2):
            b_ref[c, p] = s_ref[pl.ds(c * rows + off_b + p, tiles, stride=planes), :]
    last = (tiles - 1) * planes
    for k in range(comps // 2):
        first, second = 2 * k * rows, (2 * k + 1) * rows
        low_a = s_ref[first : first + planes, :]
        low_b = s_ref[second : second + planes, :]
        high_a = s_ref[first + last : first + last + planes, :]
        high_b = s_ref[second + last : second + last + planes, :]
        low_ref[k] = jnp.where(lane < 64, low_a, pltpu.roll(low_b, 64, 1))
        high_ref[k] = jnp.where(lane < 64, pltpu.roll(high_a, 64, 1), high_b)


def split3(value):
    high = value.astype(jnp.bfloat16)
    rest = value - high.astype(jnp.float32)
    middle = rest.astype(jnp.bfloat16)
    low = (rest - middle.astype(jnp.float32)).astype(jnp.bfloat16)
    return high, middle, low


def shift_matrix():
    source = np.arange(LANES)[:, None]
    target = np.arange(LANES)[None, :]
    rows = LANES // NZ
    ys, yt = source // NZ, target // NZ
    turn = (target - source) % NZ
    same_z = turn == 0
    weights = {1: 16.0, 2: -1.0}
    own = np.where(source == target, -90.0, 0.0)
    cross = np.zeros_like(own)
    apart = np.where(target < LANES // 2, yt + rows - ys, ys + rows - yt)
    for distance, weight in weights.items():
        own += np.where((ys == yt) & (np.minimum(turn, NZ - turn) == distance), weight, 0.0)
        own += np.where(same_z & (abs(yt - ys) == distance), weight, 0.0)
        cross += np.where(same_z & (apart == distance), weight, 0.0)
    one = np.concatenate([own, cross], 1)
    return jnp.asarray(np.concatenate([one, one], 0), jnp.bfloat16)


def many_of(comps):
    return max(n for n in range(1, 7) if comps % n == 0)


def main_kernel(
    comps,
    planes,
    tiles,
    nreact,
    s_ref,
    shift_ref,
    d_hbm,
    sub_hbm,
    flame_hbm,
    lp_hbm,
    act_hbm,
    heat_hbm,
    rt_hbm,
    pr_hbm,
    o_ref,
    dv_ref,
    d_ref,
    sub_ref,
    flame_ref,
    lp_ref,
    act_ref,
    heat_ref,
    rt_ref,
    pr_ref,
    q_ref,
    p_ref,
    w1_ref,
    w2_ref,
    a_ref,
    old_ref,
    t_ref,
    st_ref,
    even_ref,
    odd_ref,
    pos_ref,
    sem,
):
    rows = planes * tiles
    species = comps - 1
    block_rows = planes * tiles
    loads = [
        pltpu.make_async_copy(source, target, sem.at[i])
        for i, (source, target) in enumerate(
            (
                (d_hbm, d_ref),
                (sub_hbm, sub_ref),
                (flame_hbm, flame_ref),
                (lp_hbm, lp_ref),
                (act_hbm, act_ref),
                (heat_hbm, heat_ref),
                (rt_hbm, rt_ref),
                (pr_hbm, pr_ref),
            )
        )
    ]
    for load in loads:
        load.start()

    def scan_blocks():
        for load in loads[:3]:
            load.wait()
        count = jnp.int32(0)
        for x in range(planes):
            for b in range(tiles):
                pos_ref[count] = b * planes + x
                count = count + flame_ref[x, b]
        for c in range(comps):
            dv_ref[c * planes : (c + 1) * planes, :] = jnp.full(
                (planes, LANES), d_ref[c], jnp.float32
            )
        return count

    padded = q_ref.shape[1]
    wide = w1_ref.shape[0]

    def tables():
        q_ref[...] = jnp.zeros_like(q_ref)
        p_ref[...] = jnp.zeros_like(p_ref)
        q_ref[0:species, 0:nreact] = rt_ref[:, 0:nreact] + rt_ref[:, nreact : 2 * nreact]
        p_ref[0:species, 0:nreact] = pr_ref[...]
        p_ref[PIECE : PIECE + species, 0:nreact] = q_ref[0:species, 0:nreact]
        for i, piece in enumerate(split3(act_ref[...].reshape(1, nreact) * (-LOG2E))):
            q_ref[species + i : species + i + 1, 0:nreact] = piece.astype(jnp.float32)
        for i, piece in enumerate(split3(lp_ref[...].reshape(1, nreact) * LOG2E)):
            q_ref[species + 3 + i : species + 4 + i, 0:nreact] = piece.astype(jnp.float32)
        for i, piece in enumerate(split3(heat_ref[...].reshape(1, nreact))):
            p_ref[species + i : species + i + 1, 0:nreact] = piece.astype(jnp.float32)
        q = q_ref[...]
        w1 = jnp.transpose(jnp.concatenate([q, q, q], 0))
        w1_ref[...] = w1[0:wide].astype(jnp.bfloat16)
        w = p_ref[...].astype(jnp.bfloat16)
        head, rest = w[:, :256], w[:, 256:padded]
        w2_ref[...] = jnp.concatenate([head, head, rest, rest], 1)
        a_ref[...] = jnp.ones_like(a_ref)

    many = many_of(comps)
    size = many * rows
    groups = comps // many
    shape = (many, tiles, planes, LANES)
    lane = lax.broadcasted_iota(jnp.int32, (1, 1, planes, LANES), 3)
    x = lax.broadcasted_iota(jnp.int32, (1, 1, planes, LANES), 2)
    zero = jnp.zeros((many, 1, planes, LANES), jnp.float32)
    near, far = near_weight * 12.0, -far_weight * 12.0
    weights = {
        -1: jnp.where(x > 0, near, 0.0),
        1: jnp.where(x < planes - 1, near, 0.0),
        -2: jnp.where(x > 1, far, 0.0),
        2: jnp.where(x < planes - 2, far, 0.0),
    }

    def product(i, buffer):
        flat = s_ref[pl.ds(pl.multiple_of(i * size, size), size), :]
        high = flat.astype(jnp.bfloat16)
        low = (flat - high.astype(jnp.float32)).astype(jnp.bfloat16)
        both = jnp.concatenate([high, low], 1)
        buffer[...] = jnp.dot(both, shift_ref[...], preferred_element_type=jnp.float32)

    def combine(i, buffer, inside):
        start = pl.multiple_of(i * size, size)
        v = s_ref[pl.ds(start, size), :].reshape(shape)
        own = buffer[:, :LANES].reshape(shape)
        cross = buffer[:, LANES:].reshape(shape)
        before = jnp.concatenate([zero, cross[:, :-1]], 1)
        after = jnp.concatenate([cross[:, 1:], zero], 1)
        own = own + jnp.where(lane < 64, before, after)
        for offset, weight in weights.items():
            if inside:
                moved = s_ref[pl.ds(start + offset, size), :].reshape(shape)
            else:
                moved = pltpu.roll(v, (-offset) % planes, 2)
            own = own + moved * weight
        for j in range(many):
            where = pl.ds(pl.multiple_of(start + j * rows, rows), rows)
            scale = d_ref[i * many + j] * (1.0 / 12.0)
            o_ref[where, :] = (v[j] + scale * own[j]).reshape(rows, LANES)

    product(0, even_ref)
    if groups % 2 == 1 and groups > 2:
        product(1, odd_ref)
        count = scan_blocks()
        combine(0, even_ref, False)

        def two(i, carry):
            g = 2 * i + 1
            product(g + 1, even_ref)
            combine(g, odd_ref, True)
            product(g + 2, odd_ref)
            combine(g + 1, even_ref, True)
            return carry

        lax.fori_loop(0, (groups - 3) // 2, two, 0)
        for load in loads[3:]:
            load.wait()
        product(groups - 1, even_ref)
        tables()
        combine(groups - 2, odd_ref, True)
        combine(groups - 1, even_ref, False)
    else:
        count = scan_blocks()
        for load in loads[3:]:
            load.wait()
        tables()
        for i in range(groups):
            combine(i, even_ref, False)
            if i < groups - 1:
                product(i + 1, even_ref)

    @pl.when(count > 0)
    def _():
        arow = lax.broadcasted_iota(jnp.int32, a_ref.shape, 0)

        def group(g, carry):
            most = jnp.int32(0)
            pieces = []
            for i in range(GROUP):
                slot = g * GROUP + i
                here = jnp.where(slot < count, slot, 0)
                at = pos_ref[here]
                n = jnp.where(
                    slot < count, sub_ref[lax.rem(at, planes), lax.div(at, planes)], 0
                )
                most = jnp.maximum(most, n)
                cols = slice(i * LANES, (i + 1) * LANES)
                mine = s_ref[pl.ds(block_rows + at, species, stride=rows), :]
                a_ref[0:species, cols] = mine
                old_ref[0:species, cols] = mine
                t_ref[:, cols] = s_ref[pl.ds(at, 1), :]
                pieces.append(jnp.full((1, LANES), n, jnp.int32))
            counts = jnp.concatenate(pieces, 1)
            st_ref[...] = 1.0 / jnp.maximum(counts, 1).astype(jnp.float32)

            def substep(k, inner):
                step = jnp.where(counts > k, st_ref[...], 0.0)
                amounts = a_ref[...]
                thermal = t_ref[...]
                inverse = 1.0 / thermal
                terms = jnp.where(
                    arow < species,
                    jnp.log2(amounts),
                    jnp.where(
                        arow < species + 3, inverse, jnp.where(arow < species + 6, 1.0, 0.0)
                    ),
                )
                rhs = jnp.concatenate(split3(terms), 0)
                exponent = jnp.dot(w1_ref[...], rhs, preferred_element_type=jnp.float32)
                progress = jnp.exp2(exponent)
                high = progress.astype(jnp.bfloat16)
                low = (progress - high.astype(jnp.float32)).astype(jnp.bfloat16)
                gap = 2 * LANES - wide + LANES
                rhs = jnp.concatenate(
                    [high[:256], low[:256], high[256:], high[:gap], low[256:], low[:gap]], 0
                )
                out = jnp.dot(w2_ref[...], rhs, preferred_element_type=jnp.float32)
                produced = out[:PIECE]
                loss = out[PIECE:]
                warm = out[species : species + 1] + (
                    out[species + 1 : species + 2] + out[species + 2 : species + 3]
                )
                a_ref[...] = (amounts + step * produced) * (amounts / (amounts + step * loss))
                t_ref[...] = thermal + step * warm
                return inner

            lax.fori_loop(0, most, substep, 0)

            for i in range(GROUP):
                slot = g * GROUP + i

                @pl.when(slot < count)
                def _(i=i, slot=slot):
                    at = pos_ref[slot]
                    cols = slice(i * LANES, (i + 1) * LANES)
                    where = pl.ds(block_rows + at, species, stride=rows)
                    change = a_ref[0:species, cols] - old_ref[0:species, cols]
                    o_ref[where, :] = o_ref[where, :] + change
                    top = pl.ds(at, 1)
                    o_ref[top, :] = o_ref[top, :] + (t_ref[:, cols] - s_ref[top, :])

            return carry

        lax.fori_loop(0, (count + (GROUP - 1)) // GROUP, group, 0)


def add_planes(planes, tiles, work, dv_ref, plane, begin, end, side):
    rows = planes * tiles
    for c in range(begin, end):
        near = plane(c, 1 - side)
        far = plane(c, side)
        weight = dv_ref[c * planes : (c + 1) * planes, :]
        first = pl.ds(c * rows + side * (planes - 1), tiles, stride=planes)
        second = pl.ds(c * rows + 1 + side * (planes - 3), tiles, stride=planes)
        one, two = work[first, :], work[second, :]
        work[first, :] = one + weight * (near_weight * near - far_weight * far)
        work[second, :] = two - (weight * far_weight) * near


def write_out(planes, tiles, work, out, sem, first, last, side=None):
    where = pl.ds(first * tiles, (last - first) * tiles)
    kept = pl.ds(0, planes) if side is None else pl.ds(side * (planes - 2), 2)
    rows = work.shape[0]
    shape = (rows // planes, planes, LANES)
    return pltpu.make_async_copy(
        work.reshape(*shape).at[where, kept], out.reshape(*shape).at[where, kept], sem
    )


def inner_edges_kernel(
    comps, planes, tiles, part_ref, dv_ref, hb_ref, zl_ref, zh_ref, work, out, sem
):
    del part_ref
    rows = planes * tiles
    lane = lax.broadcasted_iota(jnp.int32, (planes, LANES), 1)
    last = (tiles - 1) * planes
    above = jnp.where(lane % 64 < NZ, near_weight, 0.0)
    below = jnp.where(lane % 64 >= NZ, near_weight, 0.0)
    lower = jnp.where(lane < 64, 1.0, 0.0)
    upper = jnp.where(lane < 64, 0.0, 1.0)

    def pair(k):
        low, high = zl_ref[k], zh_ref[k]
        low = pltpu.roll(low, LANES - NZ, 1) * above - far_weight * low
        high = pltpu.roll(high, NZ, 1) * below - far_weight * high
        lows = (low * lower, pltpu.roll(low * upper, 64, 1))
        highs = (pltpu.roll(high * lower, 64, 1), high * upper)
        for j in range(2):
            c = 2 * k + j
            weight = dv_ref[c * planes : (c + 1) * planes, :]
            top = slice(c * rows, c * rows + planes)
            end = slice(c * rows + last, c * rows + last + planes)
            work[top, :] = work[top, :] + weight * lows[j]
            work[end, :] = work[end, :] + weight * highs[j]

    half = comps // 2
    cuts = (0, 2 * (half // 6), 2 * (half // 2), comps)
    spans = list(zip(cuts, cuts[1:]))
    odd = odd_place("gx")
    for side in range(2):

        @pl.when(odd == 1 - side)
        def _(side=side):
            for i, (first, end) in enumerate(spans):
                for k in range(first // 2, end // 2):
                    pair(k)
                add_planes(
                    planes, tiles, work, dv_ref, lambda c, p: hb_ref[c, p], first, end, side
                )
                write_out(planes, tiles, work, out, sem.at[i], first, end).start()

    for i, (first, end) in enumerate(spans):
        write_out(planes, tiles, work, out, sem.at[i], first, end).wait()


def outer_edges_kernel(comps, planes, tiles, part_ref, dv_ref, h_ref, prev, work, out, sem):
    del part_ref, prev
    odd = odd_place("gx")

    def plane(c, p):
        return h_ref[pl.ds(c * 2 * tiles + p, tiles, stride=2), :]

    bounds = [0, comps // 3, comps]
    spans = list(zip(bounds, bounds[1:]))
    for side in range(2):

        @pl.when(odd == side)
        def _(side=side):
            for i, (first, last) in enumerate(spans):
                add_planes(planes, tiles, work, dv_ref, plane, first, last, side)
                write_out(planes, tiles, work, out, sem.at[i], first, last, side).start()
            for i, (first, last) in enumerate(spans):
                write_out(planes, tiles, work, out, sem.at[i], first, last, side).wait()


def per_device(
    state, diffusivity, log_prefactor, activation, heat, reactants, products, substeps, flame
):
    comps, planes, cells = state.shape
    tiles = cells // LANES
    rows = planes * tiles
    nreact = log_prefactor.shape[0]
    gx, gy = lax.axis_size("gx"), lax.axis_size("gy")
    f32 = jnp.float32
    flat = (
        state.reshape(comps, planes, tiles, LANES)
        .transpose(0, 2, 1, 3)
        .reshape(comps * rows, LANES)
    )

    def stay(array):
        return pltpu.with_memory_space_constraint(array, pltpu.HBM)

    vmem = pl.BlockSpec(memory_space=VMEM)
    anywhere = pl.BlockSpec(memory_space=pl.ANY)

    hbm = pl.BlockSpec(memory_space=pltpu.HBM)
    sds = jax.ShapeDtypeStruct
    ahead = pl.pallas_call(
        functools.partial(ahead_kernel, comps, planes, tiles),
        out_shape=sds((comps * tiles, 2, LANES), f32),
        in_specs=[hbm],
        out_specs=vmem,
        scratch_shapes=[pltpu.SemaphoreType.DMA((1,))],
        compiler_params=params(8),
        name="ahead",
    )(stay(flat.reshape(comps * tiles, planes // 2, 2, LANES)))
    beside, low, high = pl.pallas_call(
        functools.partial(pack_kernel, comps, planes, tiles),
        out_shape=(
            sds((comps, 2, tiles, LANES), f32),
            sds((comps // 2, planes, LANES), f32),
            sds((comps // 2, planes, LANES), f32),
        ),
        in_specs=[vmem],
        out_specs=[vmem] * 3,
        compiler_params=params(16),
        name="pack",
    )(flat)

    outer = [(i, (i + 1) % gx) for i in range(1, gx, 2)]
    outer = outer + [(t, s) for s, t in outer]
    inner = [(i, i + 1) for i in range(0, gx, 2)]
    inner = inner + [(t, s) for s, t in inner]
    forward = [(i, (i + 1) % gy) for i in range(gy)]
    backward = [(t, s) for s, t in forward]
    ha = lax.ppermute(ahead, "gx", outer)
    hb = lax.ppermute(beside, "gx", inner)
    zl = lax.ppermute(high, "gy", forward)
    zh = lax.ppermute(low, "gy", backward)

    padded = pl.cdiv(nreact, LANES) * LANES
    wide = pl.cdiv(nreact, 16) * 16
    part, dv = pl.pallas_call(
        functools.partial(main_kernel, comps, planes, tiles, nreact),
        out_shape=(sds((comps * rows, LANES), f32), sds((comps * planes, LANES), f32)),
        in_specs=[vmem, vmem] + [hbm] * 8,
        out_specs=(vmem, vmem),
        scratch_shapes=[
            SMEM((comps,), f32),
            SMEM(substeps.shape, jnp.int32),
            SMEM(flame.shape, jnp.int32),
            VMEM((nreact,), f32),
            VMEM((nreact,), f32),
            VMEM((nreact,), f32),
            VMEM((comps - 1, 2 * nreact), f32),
            VMEM((comps - 1, nreact), f32),
            VMEM((PIECE, padded), f32),
            VMEM((2 * PIECE, padded), f32),
            VMEM((wide, 3 * PIECE), jnp.bfloat16),
            VMEM((2 * PIECE, 2 * padded), jnp.bfloat16),
            VMEM((PIECE, GROUP * LANES), f32),
            VMEM((PIECE, GROUP * LANES), f32),
            VMEM((1, GROUP * LANES), f32),
            VMEM((1, GROUP * LANES), f32),
            VMEM((many_of(comps) * rows, 2 * LANES), f32),
            VMEM((many_of(comps) * rows, 2 * LANES), f32),
            SMEM((rows + 1,), jnp.int32),
            pltpu.SemaphoreType.DMA((8,)),
        ],
        compiler_params=params(24),
        cost_estimate=pl.CostEstimate(
            flops=2_000_000_000, bytes_accessed=16_000_000, transcendentals=1_000_000
        ),
        name="main",
    )(
        flat,
        shift_matrix(),
        *map(
            stay,
            (
                diffusivity,
                substeps,
                flame,
                log_prefactor,
                activation,
                heat,
                reactants.T,
                products,
            ),
        ),
    )

    whole = sds((comps * rows, LANES), f32)
    cost = pl.CostEstimate(flops=1_000_000, bytes_accessed=3_000_000, transcendentals=0)
    part, out = pl.pallas_call(
        functools.partial(inner_edges_kernel, comps, planes, tiles),
        out_shape=(whole, whole),
        in_specs=[vmem] * 5,
        out_specs=(vmem, anywhere),
        scratch_shapes=[pltpu.SemaphoreType.DMA((3,))],
        input_output_aliases={0: 0},
        compiler_params=params(16),
        cost_estimate=cost,
        name="inner_edges",
    )(part, dv, hb, zl, zh)
    _, out = pl.pallas_call(
        functools.partial(outer_edges_kernel, comps, planes, tiles),
        out_shape=(whole, whole),
        in_specs=[vmem] * 3 + [anywhere],
        out_specs=(vmem, anywhere),
        scratch_shapes=[pltpu.SemaphoreType.DMA((2,))],
        input_output_aliases={0: 0, 3: 1},
        compiler_params=params(16),
        cost_estimate=cost,
        name="outer_edges",
    )(part, dv, ha.reshape(comps * tiles * 2, LANES), out)
    return (
        out.reshape(comps, tiles, planes, LANES).transpose(0, 2, 1, 3).reshape(comps, planes, cells)
    )


def solution(mesh):
    in_specs = (P(None, "gx", "gy"), P(), P(), P(), P(), P(), P(), P("gx", "gy"), P("gx", "gy"))
    out_specs = P(None, "gx", "gy")

    return jax.shard_map(
        per_device, mesh=mesh, in_specs=in_specs, out_specs=out_specs, check_vma=False
    )
```

```python
import functools

import jax
import jax.numpy as jnp
import numpy as np
from jax import lax
from jax.experimental import pallas as pl
from jax.experimental.pallas import tpu as pltpu
from jax.sharding import PartitionSpec as P

NZ = 32
LANES = 128
near_weight = 4.0 / 3.0
far_weight = 1.0 / 12.0
LOG2E = 1.4426950408889634
GROUP = 4
PIECE = 64


VMEM = pltpu.VMEM
SMEM = pltpu.SMEM


def params(mib):
    return pltpu.CompilerParams(vmem_limit_bytes=mib << 20)


def odd_place(axis):
    return lax.rem(lax.axis_index(axis), 2)


def ahead_kernel(comps, planes, tiles, s_hbm, o_ref, sem):
    pair = odd_place("gx") * (planes // 2 - 1)
    total = comps * tiles
    parts = sem.shape[0]
    copies = []
    for i in range(parts):
        begin, end = total * i // parts, total * (i + 1) // parts
        where = pl.ds(begin, end - begin)
        copies.append(pltpu.make_async_copy(s_hbm.at[where, pair], o_ref.at[where], sem.at[i]))
        copies[-1].start()
    for copy in copies:
        copy.wait()


def pack_kernel(comps, planes, tiles, s_ref, b_ref, low_ref, high_ref):
    rows = planes * tiles
    lane = lax.broadcasted_iota(jnp.int32, (planes, LANES), 1)
    off_b = (1 - odd_place("gx")) * (planes - 2)
    for c in range(comps):
        for p in range(2):
            b_ref[c, p] = s_ref[pl.ds(c * rows + off_b + p, tiles, stride=planes), :]
    last = (tiles - 1) * planes
    for k in range(comps // 2):
        first, second = 2 * k * rows, (2 * k + 1) * rows
        low_a = s_ref[first : first + planes, :]
        low_b = s_ref[second : second + planes, :]
        high_a = s_ref[first + last : first + last + planes, :]
        high_b = s_ref[second + last : second + last + planes, :]
        low_ref[k] = jnp.where(lane < 64, low_a, pltpu.roll(low_b, 64, 1))
        high_ref[k] = jnp.where(lane < 64, pltpu.roll(high_a, 64, 1), high_b)


def split3(value):
    high = value.astype(jnp.bfloat16)
    rest = value - high.astype(jnp.float32)
    middle = rest.astype(jnp.bfloat16)
    low = (rest - middle.astype(jnp.float32)).astype(jnp.bfloat16)
    return high, middle, low


def shift_matrix():
    source = np.arange(LANES)[:, None]
    target = np.arange(LANES)[None, :]
    rows = LANES // NZ
    ys, yt = source // NZ, target // NZ
    turn = (target - source) % NZ
    same_z = turn == 0
    weights = {1: 16.0, 2: -1.0}
    own = np.where(source == target, -90.0, 0.0)
    cross = np.zeros_like(own)
    apart = np.where(target < LANES // 2, yt + rows - ys, ys + rows - yt)
    for distance, weight in weights.items():
        own += np.where((ys == yt) & (np.minimum(turn, NZ - turn) == distance), weight, 0.0)
        own += np.where(same_z & (abs(yt - ys) == distance), weight, 0.0)
        cross += np.where(same_z & (apart == distance), weight, 0.0)
    one = np.concatenate([own, cross], 1)
    return jnp.asarray(np.concatenate([one, one], 0), jnp.bfloat16)


def many_of(comps):
    return max(n for n in range(1, 7) if comps % n == 0)


def main_kernel(
    comps,
    planes,
    tiles,
    nreact,
    s_ref,
    shift_ref,
    d_hbm,
    sub_hbm,
    flame_hbm,
    lp_hbm,
    act_hbm,
    heat_hbm,
    rt_hbm,
    pr_hbm,
    o_ref,
    dv_ref,
    d_ref,
    sub_ref,
    flame_ref,
    lp_ref,
    act_ref,
    heat_ref,
    rt_ref,
    pr_ref,
    q_ref,
    p_ref,
    w1_ref,
    w2_ref,
    a_ref,
    old_ref,
    t_ref,
    st_ref,
    even_ref,
    odd_ref,
    pos_ref,
    sem,
):
    rows = planes * tiles
    species = comps - 1
    block_rows = planes * tiles
    loads = [
        pltpu.make_async_copy(source, target, sem.at[i])
        for i, (source, target) in enumerate(
            (
                (d_hbm, d_ref),
                (sub_hbm, sub_ref),
                (flame_hbm, flame_ref),
                (lp_hbm, lp_ref),
                (act_hbm, act_ref),
                (heat_hbm, heat_ref),
                (rt_hbm, rt_ref),
                (pr_hbm, pr_ref),
            )
        )
    ]
    for load in loads:
        load.start()

    def scan_blocks():
        for load in loads[:3]:
            load.wait()
        count = jnp.int32(0)
        for x in range(planes):
            for b in range(tiles):
                pos_ref[count] = b * planes + x
                count = count + flame_ref[x, b]
        for c in range(comps):
            dv_ref[c * planes : (c + 1) * planes, :] = jnp.full(
                (planes, LANES), d_ref[c], jnp.float32
            )
        return count

    padded = q_ref.shape[1]
    wide = w1_ref.shape[0]

    def tables():
        q_ref[...] = jnp.zeros_like(q_ref)
        p_ref[...] = jnp.zeros_like(p_ref)
        q_ref[0:species, 0:nreact] = rt_ref[:, 0:nreact] + rt_ref[:, nreact : 2 * nreact]
        p_ref[0:species, 0:nreact] = pr_ref[...]
        p_ref[PIECE : PIECE + species, 0:nreact] = q_ref[0:species, 0:nreact]
        for i, piece in enumerate(split3(act_ref[...].reshape(1, nreact) * (-LOG2E))):
            q_ref[species + i : species + i + 1, 0:nreact] = piece.astype(jnp.float32)
        for i, piece in enumerate(split3(lp_ref[...].reshape(1, nreact) * LOG2E)):
            q_ref[species + 3 + i : species + 4 + i, 0:nreact] = piece.astype(jnp.float32)
        for i, piece in enumerate(split3(heat_ref[...].reshape(1, nreact))):
            p_ref[species + i : species + i + 1, 0:nreact] = piece.astype(jnp.float32)
        q = q_ref[...]
        w1 = jnp.transpose(jnp.concatenate([q, q, q], 0))
        w1_ref[...] = w1[0:wide].astype(jnp.bfloat16)
        w = p_ref[...].astype(jnp.bfloat16)
        head, rest = w[:, :256], w[:, 256:padded]
        w2_ref[...] = jnp.concatenate([head, head, rest, rest], 1)
        a_ref[...] = jnp.ones_like(a_ref)

    many = many_of(comps)
    size = many * rows
    groups = comps // many
    shape = (many, tiles, planes, LANES)
    lane = lax.broadcasted_iota(jnp.int32, (1, 1, planes, LANES), 3)
    x = lax.broadcasted_iota(jnp.int32, (1, 1, planes, LANES), 2)
    zero = jnp.zeros((many, 1, planes, LANES), jnp.float32)
    near, far = near_weight * 12.0, -far_weight * 12.0
    weights = {
        -1: jnp.where(x > 0, near, 0.0),
        1: jnp.where(x < planes - 1, near, 0.0),
        -2: jnp.where(x > 1, far, 0.0),
        2: jnp.where(x < planes - 2, far, 0.0),
    }

    def product(i, buffer):
        flat = s_ref[pl.ds(pl.multiple_of(i * size, size), size), :]
        high = flat.astype(jnp.bfloat16)
        low = (flat - high.astype(jnp.float32)).astype(jnp.bfloat16)
        both = jnp.concatenate([high, low], 1)
        buffer[...] = jnp.dot(both, shift_ref[...], preferred_element_type=jnp.float32)

    def combine(i, buffer, inside):
        start = pl.multiple_of(i * size, size)
        v = s_ref[pl.ds(start, size), :].reshape(shape)
        own = buffer[:, :LANES].reshape(shape)
        cross = buffer[:, LANES:].reshape(shape)
        before = jnp.concatenate([zero, cross[:, :-1]], 1)
        after = jnp.concatenate([cross[:, 1:], zero], 1)
        own = own + jnp.where(lane < 64, before, after)
        for offset, weight in weights.items():
            if inside:
                moved = s_ref[pl.ds(start + offset, size), :].reshape(shape)
            else:
                moved = pltpu.roll(v, (-offset) % planes, 2)
            own = own + moved * weight
        for j in range(many):
            where = pl.ds(pl.multiple_of(start + j * rows, rows), rows)
            scale = d_ref[i * many + j] * (1.0 / 12.0)
            o_ref[where, :] = (v[j] + scale * own[j]).reshape(rows, LANES)

    product(0, even_ref)
    if groups % 2 == 1 and groups > 2:
        product(1, odd_ref)
        count = scan_blocks()
        combine(0, even_ref, False)

        def two(i, carry):
            g = 2 * i + 1
            product(g + 1, even_ref)
            combine(g, odd_ref, True)
            product(g + 2, odd_ref)
            combine(g + 1, even_ref, True)
            return carry

        lax.fori_loop(0, (groups - 3) // 2, two, 0)
        for load in loads[3:]:
            load.wait()
        product(groups - 1, even_ref)
        tables()
        combine(groups - 2, odd_ref, True)
        combine(groups - 1, even_ref, False)
    else:
        count = scan_blocks()
        for load in loads[3:]:
            load.wait()
        tables()
        for i in range(groups):
            combine(i, even_ref, False)
            if i < groups - 1:
                product(i + 1, even_ref)

    @pl.when(count > 0)
    def _():
        arow = lax.broadcasted_iota(jnp.int32, a_ref.shape, 0)

        def group(g, carry):
            most = jnp.int32(0)
            pieces = []
            for i in range(GROUP):
                slot = g * GROUP + i
                here = jnp.where(slot < count, slot, 0)
                at = pos_ref[here]
                n = jnp.where(
                    slot < count, sub_ref[lax.rem(at, planes), lax.div(at, planes)], 0
                )
                most = jnp.maximum(most, n)
                cols = slice(i * LANES, (i + 1) * LANES)
                mine = s_ref[pl.ds(block_rows + at, species, stride=rows), :]
                a_ref[0:species, cols] = mine
                old_ref[0:species, cols] = mine
                t_ref[:, cols] = s_ref[pl.ds(at, 1), :]
                pieces.append(jnp.full((1, LANES), n, jnp.int32))
            counts = jnp.concatenate(pieces, 1)
            st_ref[...] = 1.0 / jnp.maximum(counts, 1).astype(jnp.float32)

            def substep(k, inner):
                step = jnp.where(counts > k, st_ref[...], 0.0)
                amounts = a_ref[...]
                thermal = t_ref[...]
                inverse = 1.0 / thermal
                terms = jnp.where(
                    arow < species,
                    jnp.log2(amounts),
                    jnp.where(
                        arow < species + 3, inverse, jnp.where(arow < species + 6, 1.0, 0.0)
                    ),
                )
                rhs = jnp.concatenate(split3(terms), 0)
                exponent = jnp.dot(w1_ref[...], rhs, preferred_element_type=jnp.float32)
                progress = jnp.exp2(exponent)
                high = progress.astype(jnp.bfloat16)
                low = (progress - high.astype(jnp.float32)).astype(jnp.bfloat16)
                gap = 2 * LANES - wide + LANES
                rhs = jnp.concatenate(
                    [high[:256], low[:256], high[256:], high[:gap], low[256:], low[:gap]], 0
                )
                out = jnp.dot(w2_ref[...], rhs, preferred_element_type=jnp.float32)
                produced = out[:PIECE]
                loss = out[PIECE:]
                warm = out[species : species + 1] + (
                    out[species + 1 : species + 2] + out[species + 2 : species + 3]
                )
                a_ref[...] = (amounts + step * produced) * (amounts / (amounts + step * loss))
                t_ref[...] = thermal + step * warm
                return inner

            lax.fori_loop(0, most, substep, 0)

            for i in range(GROUP):
                slot = g * GROUP + i

                @pl.when(slot < count)
                def _(i=i, slot=slot):
                    at = pos_ref[slot]
                    cols = slice(i * LANES, (i + 1) * LANES)
                    where = pl.ds(block_rows + at, species, stride=rows)
                    change = a_ref[0:species, cols] - old_ref[0:species, cols]
                    o_ref[where, :] = o_ref[where, :] + change
                    top = pl.ds(at, 1)
                    o_ref[top, :] = o_ref[top, :] + (t_ref[:, cols] - s_ref[top, :])

            return carry

        lax.fori_loop(0, (count + (GROUP - 1)) // GROUP, group, 0)


def add_planes(planes, tiles, work, dv_ref, plane, begin, end, side):
    rows = planes * tiles
    for c in range(begin, end):
        near = plane(c, 1 - side)
        far = plane(c, side)
        weight = dv_ref[c * planes : (c + 1) * planes, :]
        first = pl.ds(c * rows + side * (planes - 1), tiles, stride=planes)
        second = pl.ds(c * rows + 1 + side * (planes - 3), tiles, stride=planes)
        one, two = work[first, :], work[second, :]
        work[first, :] = one + weight * (near_weight * near - far_weight * far)
        work[second, :] = two - (weight * far_weight) * near


def write_out(planes, tiles, work, out, sem, first, last, x, count):
    shape = (work.shape[0] // planes, planes, LANES)
    where = (pl.ds(first * tiles, (last - first) * tiles), pl.ds(x, count))
    return pltpu.make_async_copy(
        work.reshape(*shape).at[where], out.reshape(*shape).at[where], sem
    )


def inner_edges_kernel(
    comps, planes, tiles, part_ref, dv_ref, hb_ref, zl_ref, zh_ref, work, out, sem
):
    del part_ref
    rows = planes * tiles
    lane = lax.broadcasted_iota(jnp.int32, (planes, LANES), 1)
    last = (tiles - 1) * planes
    above = jnp.where(lane % 64 < NZ, near_weight, 0.0)
    below = jnp.where(lane % 64 >= NZ, near_weight, 0.0)
    lower = jnp.where(lane < 64, 1.0, 0.0)
    upper = jnp.where(lane < 64, 0.0, 1.0)

    def pair(k):
        low, high = zl_ref[k], zh_ref[k]
        low = pltpu.roll(low, LANES - NZ, 1) * above - far_weight * low
        high = pltpu.roll(high, NZ, 1) * below - far_weight * high
        lows = (low * lower, pltpu.roll(low * upper, 64, 1))
        highs = (pltpu.roll(high * lower, 64, 1), high * upper)
        for j in range(2):
            c = 2 * k + j
            weight = dv_ref[c * planes : (c + 1) * planes, :]
            top = slice(c * rows, c * rows + planes)
            end = slice(c * rows + last, c * rows + last + planes)
            work[top, :] = work[top, :] + weight * lows[j]
            work[end, :] = work[end, :] + weight * highs[j]

    half = comps // 2
    cuts = (0, 2 * (half // 7), 2 * (half // 2), 2 * (half * 5 // 6), comps)
    spans = list(zip(cuts, cuts[1:]))
    odd = odd_place("gx")
    for side in range(2):

        @pl.when(odd == 1 - side)
        def _(side=side):
            kept = (2 * side, planes - 2)
            for i, (first, end) in enumerate(spans):
                for k in range(first // 2, end // 2):
                    pair(k)
                add_planes(
                    planes, tiles, work, dv_ref, lambda c, p: hb_ref[c, p], first, end, side
                )
                write_out(planes, tiles, work, out, sem.at[i], first, end, *kept).start()
            for i, (first, end) in enumerate(spans):
                write_out(planes, tiles, work, out, sem.at[i], first, end, *kept).wait()


def outer_edges_kernel(comps, planes, tiles, part_ref, dv_ref, h_ref, prev, work, out, sem):
    del part_ref, prev
    odd = odd_place("gx")

    def plane(c, p):
        return h_ref[pl.ds(c * 2 * tiles + p, tiles, stride=2), :]

    bounds = [0, comps // 3, comps]
    spans = list(zip(bounds, bounds[1:]))
    for side in range(2):

        @pl.when(odd == side)
        def _(side=side):
            kept = (side * (planes - 2), 2)
            for i, (first, last) in enumerate(spans):
                add_planes(planes, tiles, work, dv_ref, plane, first, last, side)
                write_out(planes, tiles, work, out, sem.at[i], first, last, *kept).start()
            for i, (first, last) in enumerate(spans):
                write_out(planes, tiles, work, out, sem.at[i], first, last, *kept).wait()


def per_device(
    state, diffusivity, log_prefactor, activation, heat, reactants, products, substeps, flame
):
    comps, planes, cells = state.shape
    tiles = cells // LANES
    rows = planes * tiles
    nreact = log_prefactor.shape[0]
    gx, gy = lax.axis_size("gx"), lax.axis_size("gy")
    f32 = jnp.float32
    flat = (
        state.reshape(comps, planes, tiles, LANES)
        .transpose(0, 2, 1, 3)
        .reshape(comps * rows, LANES)
    )

    def stay(array):
        return pltpu.with_memory_space_constraint(array, pltpu.HBM)

    vmem = pl.BlockSpec(memory_space=VMEM)
    anywhere = pl.BlockSpec(memory_space=pl.ANY)

    hbm = pl.BlockSpec(memory_space=pltpu.HBM)
    sds = jax.ShapeDtypeStruct
    ahead = pl.pallas_call(
        functools.partial(ahead_kernel, comps, planes, tiles),
        out_shape=sds((comps * tiles, 2, LANES), f32),
        in_specs=[hbm],
        out_specs=vmem,
        scratch_shapes=[pltpu.SemaphoreType.DMA((1,))],
        compiler_params=params(8),
        name="ahead",
    )(stay(flat.reshape(comps * tiles, planes // 2, 2, LANES)))
    beside, low, high = pl.pallas_call(
        functools.partial(pack_kernel, comps, planes, tiles),
        out_shape=(
            sds((comps, 2, tiles, LANES), f32),
            sds((comps // 2, planes, LANES), f32),
            sds((comps // 2, planes, LANES), f32),
        ),
        in_specs=[vmem],
        out_specs=[vmem] * 3,
        compiler_params=params(16),
        name="pack",
    )(flat)

    outer = [(i, (i + 1) % gx) for i in range(1, gx, 2)]
    outer = outer + [(t, s) for s, t in outer]
    inner = [(i, i + 1) for i in range(0, gx, 2)]
    inner = inner + [(t, s) for s, t in inner]
    forward = [(i, (i + 1) % gy) for i in range(gy)]
    backward = [(t, s) for s, t in forward]
    ha = lax.ppermute(ahead, "gx", outer)
    hb = lax.ppermute(beside, "gx", inner)
    zl = lax.ppermute(high, "gy", forward)
    zh = lax.ppermute(low, "gy", backward)

    padded = pl.cdiv(nreact, LANES) * LANES
    wide = pl.cdiv(nreact, 16) * 16
    part, dv = pl.pallas_call(
        functools.partial(main_kernel, comps, planes, tiles, nreact),
        out_shape=(sds((comps * rows, LANES), f32), sds((comps * planes, LANES), f32)),
        in_specs=[vmem, vmem] + [hbm] * 8,
        out_specs=(vmem, vmem),
        scratch_shapes=[
            SMEM((comps,), f32),
            SMEM(substeps.shape, jnp.int32),
            SMEM(flame.shape, jnp.int32),
            VMEM((nreact,), f32),
            VMEM((nreact,), f32),
            VMEM((nreact,), f32),
            VMEM((comps - 1, 2 * nreact), f32),
            VMEM((comps - 1, nreact), f32),
            VMEM((PIECE, padded), f32),
            VMEM((2 * PIECE, padded), f32),
            VMEM((wide, 3 * PIECE), jnp.bfloat16),
            VMEM((2 * PIECE, 2 * padded), jnp.bfloat16),
            VMEM((PIECE, GROUP * LANES), f32),
            VMEM((PIECE, GROUP * LANES), f32),
            VMEM((1, GROUP * LANES), f32),
            VMEM((1, GROUP * LANES), f32),
            VMEM((many_of(comps) * rows, 2 * LANES), f32),
            VMEM((many_of(comps) * rows, 2 * LANES), f32),
            SMEM((rows + 1,), jnp.int32),
            pltpu.SemaphoreType.DMA((8,)),
        ],
        compiler_params=params(24),
        cost_estimate=pl.CostEstimate(
            flops=2_000_000_000, bytes_accessed=16_000_000, transcendentals=1_000_000
        ),
        name="main",
    )(
        flat,
        shift_matrix(),
        *map(
            stay,
            (
                diffusivity,
                substeps,
                flame,
                log_prefactor,
                activation,
                heat,
                reactants.T,
                products,
            ),
        ),
    )

    whole = sds((comps * rows, LANES), f32)
    cost = pl.CostEstimate(flops=1_000_000, bytes_accessed=3_000_000, transcendentals=0)
    part, out = pl.pallas_call(
        functools.partial(inner_edges_kernel, comps, planes, tiles),
        out_shape=(whole, whole),
        in_specs=[vmem] * 5,
        out_specs=(vmem, anywhere),
        scratch_shapes=[pltpu.SemaphoreType.DMA((4,))],
        input_output_aliases={0: 0},
        compiler_params=params(16),
        cost_estimate=cost,
        name="inner_edges",
    )(part, dv, hb, zl, zh)
    _, out = pl.pallas_call(
        functools.partial(outer_edges_kernel, comps, planes, tiles),
        out_shape=(whole, whole),
        in_specs=[vmem] * 3 + [anywhere],
        out_specs=(vmem, anywhere),
        scratch_shapes=[pltpu.SemaphoreType.DMA((2,))],
        input_output_aliases={0: 0, 3: 1},
        compiler_params=params(16),
        cost_estimate=cost,
        name="outer_edges",
    )(part, dv, ha.reshape(comps * tiles * 2, LANES), out)
    return (
        out.reshape(comps, tiles, planes, LANES).transpose(0, 2, 1, 3).reshape(comps, planes, cells)
    )


def solution(mesh):
    in_specs = (P(None, "gx", "gy"), P(), P(), P(), P(), P(), P(), P("gx", "gy"), P("gx", "gy"))
    out_specs = P(None, "gx", "gy")

    return jax.shard_map(
        per_device, mesh=mesh, in_specs=in_specs, out_specs=out_specs, check_vma=False
    )
```

```python
import functools

import jax
import jax.numpy as jnp
import numpy as np
from jax import lax
from jax.experimental import pallas as pl
from jax.experimental.pallas import tpu as pltpu
from jax.sharding import PartitionSpec as P

NZ = 32
LANES = 128
near_weight = 4.0 / 3.0
far_weight = 1.0 / 12.0
LOG2E = 1.4426950408889634
GROUP = 4
PIECE = 64


VMEM = pltpu.VMEM
SMEM = pltpu.SMEM


def params(mib):
    return pltpu.CompilerParams(vmem_limit_bytes=mib << 20)


def odd_place(axis):
    return lax.rem(lax.axis_index(axis), 2)


def ahead_kernel(comps, planes, tiles, s_hbm, o_ref, sem):
    pair = odd_place("gx") * (planes // 2 - 1)
    total = comps * tiles
    parts = sem.shape[0]
    copies = []
    for i in range(parts):
        begin, end = total * i // parts, total * (i + 1) // parts
        where = pl.ds(begin, end - begin)
        copies.append(pltpu.make_async_copy(s_hbm.at[where, pair], o_ref.at[where], sem.at[i]))
        copies[-1].start()
    for copy in copies:
        copy.wait()


def pack_kernel(comps, planes, tiles, s_ref, b_ref, low_ref, high_ref):
    rows = planes * tiles
    lane = lax.broadcasted_iota(jnp.int32, (planes, LANES), 1)
    off_b = (1 - odd_place("gx")) * (planes - 2)
    for c in range(comps):
        for p in range(2):
            b_ref[c, p] = s_ref[pl.ds(c * rows + off_b + p, tiles, stride=planes), :]
    last = (tiles - 1) * planes
    for k in range(comps // 2):
        first, second = 2 * k * rows, (2 * k + 1) * rows
        low_a = s_ref[first : first + planes, :]
        low_b = s_ref[second : second + planes, :]
        high_a = s_ref[first + last : first + last + planes, :]
        high_b = s_ref[second + last : second + last + planes, :]
        low_ref[k] = jnp.where(lane < 64, low_a, pltpu.roll(low_b, 64, 1))
        high_ref[k] = jnp.where(lane < 64, pltpu.roll(high_a, 64, 1), high_b)


def split3(value):
    high = value.astype(jnp.bfloat16)
    rest = value - high.astype(jnp.float32)
    middle = rest.astype(jnp.bfloat16)
    low = (rest - middle.astype(jnp.float32)).astype(jnp.bfloat16)
    return high, middle, low


def shift_matrix():
    source = np.arange(LANES)[:, None]
    target = np.arange(LANES)[None, :]
    rows = LANES // NZ
    ys, yt = source // NZ, target // NZ
    turn = (target - source) % NZ
    same_z = turn == 0
    weights = {1: 16.0, 2: -1.0}
    own = np.where(source == target, -90.0, 0.0)
    cross = np.zeros_like(own)
    apart = np.where(target < LANES // 2, yt + rows - ys, ys + rows - yt)
    for distance, weight in weights.items():
        own += np.where((ys == yt) & (np.minimum(turn, NZ - turn) == distance), weight, 0.0)
        own += np.where(same_z & (abs(yt - ys) == distance), weight, 0.0)
        cross += np.where(same_z & (apart == distance), weight, 0.0)
    one = np.concatenate([own, cross], 1)
    return jnp.asarray(np.concatenate([one, one], 0), jnp.bfloat16)


def many_of(comps):
    return max(n for n in range(1, 7) if comps % n == 0)


def main_kernel(
    comps,
    planes,
    tiles,
    nreact,
    s_ref,
    shift_ref,
    s_hbm,
    d_hbm,
    sub_hbm,
    flame_hbm,
    lp_hbm,
    act_hbm,
    heat_hbm,
    rt_hbm,
    pr_hbm,
    o_ref,
    dv_ref,
    d_ref,
    sub_ref,
    flame_ref,
    lp_ref,
    act_ref,
    heat_ref,
    rt_ref,
    pr_ref,
    q_ref,
    p_ref,
    w1_ref,
    w2_ref,
    a_ref,
    start_ref,
    t_ref,
    st_ref,
    even_ref,
    odd_ref,
    pos_ref,
    sem,
    row_sem,
):
    rows = planes * tiles
    species = comps - 1
    block_rows = planes * tiles
    loads = [
        pltpu.make_async_copy(source, target, sem.at[i])
        for i, (source, target) in enumerate(
            (
                (d_hbm, d_ref),
                (sub_hbm, sub_ref),
                (flame_hbm, flame_ref),
                (lp_hbm, lp_ref),
                (act_hbm, act_ref),
                (heat_hbm, heat_ref),
                (rt_hbm, rt_ref),
                (pr_hbm, pr_ref),
            )
        )
    ]
    for load in loads:
        load.start()

    def scan_blocks():
        for load in loads[:3]:
            load.wait()
        count = jnp.int32(0)
        for x in range(planes):
            for b in range(tiles):
                pos_ref[count] = b * planes + x
                count = count + flame_ref[x, b]
        for c in range(comps):
            dv_ref[c * planes : (c + 1) * planes, :] = jnp.full(
                (planes, LANES), d_ref[c], jnp.float32
            )
        return count

    def slot_place(g, i, count):
        slot = g * GROUP + i
        return pos_ref[jnp.where(slot < count, slot, 0)]

    def gather(g, i, count):
        return pltpu.make_async_copy(
            s_hbm.reshape(comps, rows, LANES).at[:, slot_place(g, i, count)],
            start_ref.at[i],
            row_sem.at[i],
        )

    padded = q_ref.shape[1]
    wide = w1_ref.shape[0]

    def tables():
        q_ref[...] = jnp.zeros_like(q_ref)
        p_ref[...] = jnp.zeros_like(p_ref)
        q_ref[0:species, 0:nreact] = rt_ref[:, 0:nreact] + rt_ref[:, nreact : 2 * nreact]
        p_ref[0:species, 0:nreact] = pr_ref[...]
        p_ref[PIECE : PIECE + species, 0:nreact] = q_ref[0:species, 0:nreact]
        for i, piece in enumerate(split3(act_ref[...].reshape(1, nreact) * (-LOG2E))):
            q_ref[species + i : species + i + 1, 0:nreact] = piece.astype(jnp.float32)
        for i, piece in enumerate(split3(lp_ref[...].reshape(1, nreact) * LOG2E)):
            q_ref[species + 3 + i : species + 4 + i, 0:nreact] = piece.astype(jnp.float32)
        for i, piece in enumerate(split3(heat_ref[...].reshape(1, nreact))):
            p_ref[species + i : species + i + 1, 0:nreact] = piece.astype(jnp.float32)
        q = q_ref[...]
        w1 = jnp.transpose(jnp.concatenate([q, q, q], 0))
        w1_ref[...] = w1[0:wide].astype(jnp.bfloat16)
        w = p_ref[...].astype(jnp.bfloat16)
        head, rest = w[:, :256], w[:, 256:padded]
        w2_ref[...] = jnp.concatenate([head, head, rest, rest], 1)
        a_ref[...] = jnp.ones_like(a_ref)

    many = many_of(comps)
    size = many * rows
    groups = comps // many
    shape = (many, tiles, planes, LANES)
    lane = lax.broadcasted_iota(jnp.int32, (1, 1, planes, LANES), 3)
    x = lax.broadcasted_iota(jnp.int32, (1, 1, planes, LANES), 2)
    zero = jnp.zeros((many, 1, planes, LANES), jnp.float32)
    near, far = near_weight * 12.0, -far_weight * 12.0
    weights = {
        -1: jnp.where(x > 0, near, 0.0),
        1: jnp.where(x < planes - 1, near, 0.0),
        -2: jnp.where(x > 1, far, 0.0),
        2: jnp.where(x < planes - 2, far, 0.0),
    }

    def product(i, buffer):
        flat = s_ref[pl.ds(pl.multiple_of(i * size, size), size), :]
        high = flat.astype(jnp.bfloat16)
        low = (flat - high.astype(jnp.float32)).astype(jnp.bfloat16)
        both = jnp.concatenate([high, low], 1)
        buffer[...] = jnp.dot(both, shift_ref[...], preferred_element_type=jnp.float32)

    def combine(i, buffer, inside):
        start = pl.multiple_of(i * size, size)
        v = s_ref[pl.ds(start, size), :].reshape(shape)
        own = buffer[:, :LANES].reshape(shape)
        cross = buffer[:, LANES:].reshape(shape)
        before = jnp.concatenate([zero, cross[:, :-1]], 1)
        after = jnp.concatenate([cross[:, 1:], zero], 1)
        own = own + jnp.where(lane < 64, before, after)
        for offset, weight in weights.items():
            if inside:
                moved = s_ref[pl.ds(start + offset, size), :].reshape(shape)
            else:
                moved = pltpu.roll(v, (-offset) % planes, 2)
            own = own + moved * weight
        for j in range(many):
            where = pl.ds(pl.multiple_of(start + j * rows, rows), rows)
            scale = d_ref[i * many + j] * (1.0 / 12.0)
            o_ref[where, :] = (v[j] + scale * own[j]).reshape(rows, LANES)

    product(0, even_ref)
    if groups % 2 == 1 and groups > 2:
        product(1, odd_ref)
        count = scan_blocks()
        for i in range(GROUP):
            gather(0, i, count).start()
        combine(0, even_ref, False)

        def two(i, carry):
            g = 2 * i + 1
            product(g + 1, even_ref)
            combine(g, odd_ref, True)
            product(g + 2, odd_ref)
            combine(g + 1, even_ref, True)
            return carry

        lax.fori_loop(0, (groups - 3) // 2, two, 0)
        for load in loads[3:]:
            load.wait()
        product(groups - 1, even_ref)
        tables()
        combine(groups - 2, odd_ref, True)
        combine(groups - 1, even_ref, False)
    else:
        count = scan_blocks()
        for i in range(GROUP):
            gather(0, i, count).start()
        for load in loads[3:]:
            load.wait()
        tables()
        for i in range(groups):
            combine(i, even_ref, False)
            if i < groups - 1:
                product(i + 1, even_ref)

    for i in range(GROUP):
        gather(0, i, count).wait()

    @pl.when(count > 0)
    def _():
        arow = lax.broadcasted_iota(jnp.int32, a_ref.shape, 0)

        def group(g, carry):
            @pl.when(g > 0)
            def _():
                for i in range(GROUP):
                    gather(g, i, count).start()
                for i in range(GROUP):
                    gather(g, i, count).wait()

            most = jnp.int32(0)
            pieces = []
            for i in range(GROUP):
                at = slot_place(g, i, count)
                n = jnp.where(
                    g * GROUP + i < count, sub_ref[lax.rem(at, planes), lax.div(at, planes)], 0
                )
                most = jnp.maximum(most, n)
                cols = slice(i * LANES, (i + 1) * LANES)
                a_ref[0:species, cols] = start_ref[i, 1:comps, :]
                t_ref[:, cols] = start_ref[i, 0:1, :]
                pieces.append(jnp.full((1, LANES), n, jnp.int32))
            counts = jnp.concatenate(pieces, 1)
            st_ref[...] = 1.0 / jnp.maximum(counts, 1).astype(jnp.float32)

            def substep(k, inner):
                step = jnp.where(counts > k, st_ref[...], 0.0)
                amounts = a_ref[...]
                thermal = t_ref[...]
                inverse = 1.0 / thermal
                terms = jnp.where(
                    arow < species,
                    jnp.log2(amounts),
                    jnp.where(
                        arow < species + 3, inverse, jnp.where(arow < species + 6, 1.0, 0.0)
                    ),
                )
                rhs = jnp.concatenate(split3(terms), 0)
                exponent = jnp.dot(w1_ref[...], rhs, preferred_element_type=jnp.float32)
                progress = jnp.exp2(exponent)
                high = progress.astype(jnp.bfloat16)
                low = (progress - high.astype(jnp.float32)).astype(jnp.bfloat16)
                gap = 2 * LANES - wide + LANES
                rhs = jnp.concatenate(
                    [high[:256], low[:256], high[256:], high[:gap], low[256:], low[:gap]], 0
                )
                out = jnp.dot(w2_ref[...], rhs, preferred_element_type=jnp.float32)
                produced = out[:PIECE]
                loss = out[PIECE:]
                warm = out[species : species + 1] + (
                    out[species + 1 : species + 2] + out[species + 2 : species + 3]
                )
                a_ref[...] = (amounts + step * produced) * (amounts / (amounts + step * loss))
                t_ref[...] = thermal + step * warm
                return inner

            lax.fori_loop(0, most, substep, 0)

            for i in range(GROUP):
                slot = g * GROUP + i

                @pl.when(slot < count)
                def _(i=i, slot=slot):
                    at = pos_ref[slot]
                    cols = slice(i * LANES, (i + 1) * LANES)
                    where = pl.ds(block_rows + at, species, stride=rows)
                    change = a_ref[0:species, cols] - start_ref[i, 1:comps, :]
                    o_ref[where, :] = o_ref[where, :] + change
                    warmer = t_ref[:, cols] - start_ref[i, 0:1, :]
                    top = pl.ds(at, 1)
                    o_ref[top, :] = o_ref[top, :] + warmer

            return carry

        lax.fori_loop(0, (count + (GROUP - 1)) // GROUP, group, 0)


def add_planes(planes, tiles, work, dv_ref, plane, begin, end, side):
    rows = planes * tiles
    for c in range(begin, end):
        near = plane(c, 1 - side)
        far = plane(c, side)
        weight = dv_ref[c * planes : (c + 1) * planes, :]
        first = pl.ds(c * rows + side * (planes - 1), tiles, stride=planes)
        second = pl.ds(c * rows + 1 + side * (planes - 3), tiles, stride=planes)
        one, two = work[first, :], work[second, :]
        work[first, :] = one + weight * (near_weight * near - far_weight * far)
        work[second, :] = two - (weight * far_weight) * near


def write_out(planes, tiles, work, out, sem, first, last, x, count):
    shape = (work.shape[0] // planes, planes, LANES)
    where = (pl.ds(first * tiles, (last - first) * tiles), pl.ds(x, count))
    return pltpu.make_async_copy(
        work.reshape(*shape).at[where], out.reshape(*shape).at[where], sem
    )


def inner_edges_kernel(
    comps, planes, tiles, part_ref, dv_ref, hb_ref, zl_ref, zh_ref, work, out, sem
):
    del part_ref
    rows = planes * tiles
    lane = lax.broadcasted_iota(jnp.int32, (planes, LANES), 1)
    last = (tiles - 1) * planes
    above = jnp.where(lane % 64 < NZ, near_weight, 0.0)
    below = jnp.where(lane % 64 >= NZ, near_weight, 0.0)
    lower = jnp.where(lane < 64, 1.0, 0.0)
    upper = jnp.where(lane < 64, 0.0, 1.0)

    def pair(k):
        low, high = zl_ref[k], zh_ref[k]
        low = pltpu.roll(low, LANES - NZ, 1) * above - far_weight * low
        high = pltpu.roll(high, NZ, 1) * below - far_weight * high
        lows = (low * lower, pltpu.roll(low * upper, 64, 1))
        highs = (pltpu.roll(high * lower, 64, 1), high * upper)
        for j in range(2):
            c = 2 * k + j
            weight = dv_ref[c * planes : (c + 1) * planes, :]
            top = slice(c * rows, c * rows + planes)
            end = slice(c * rows + last, c * rows + last + planes)
            work[top, :] = work[top, :] + weight * lows[j]
            work[end, :] = work[end, :] + weight * highs[j]

    half = comps // 2
    cuts = (0, 2 * (half // 7), 2 * (half // 2), 2 * (half * 5 // 6), comps)
    spans = list(zip(cuts, cuts[1:]))
    odd = odd_place("gx")
    for side in range(2):

        @pl.when(odd == 1 - side)
        def _(side=side):
            kept = (2 * side, planes - 2)
            for i, (first, end) in enumerate(spans):
                for k in range(first // 2, end // 2):
                    pair(k)
                add_planes(
                    planes, tiles, work, dv_ref, lambda c, p: hb_ref[c, p], first, end, side
                )
                write_out(planes, tiles, work, out, sem.at[i], first, end, *kept).start()
            for i, (first, end) in enumerate(spans):
                write_out(planes, tiles, work, out, sem.at[i], first, end, *kept).wait()


def outer_edges_kernel(comps, planes, tiles, part_ref, dv_ref, h_ref, prev, work, out, sem):
    del part_ref, prev
    odd = odd_place("gx")

    def plane(c, p):
        return h_ref[pl.ds(c * 2 * tiles + p, tiles, stride=2), :]

    bounds = [0, comps // 3, comps]
    spans = list(zip(bounds, bounds[1:]))
    for side in range(2):

        @pl.when(odd == side)
        def _(side=side):
            kept = (side * (planes - 2), 2)
            for i, (first, last) in enumerate(spans):
                add_planes(planes, tiles, work, dv_ref, plane, first, last, side)
                write_out(planes, tiles, work, out, sem.at[i], first, last, *kept).start()
            for i, (first, last) in enumerate(spans):
                write_out(planes, tiles, work, out, sem.at[i], first, last, *kept).wait()


def per_device(
    state, diffusivity, log_prefactor, activation, heat, reactants, products, substeps, flame
):
    comps, planes, cells = state.shape
    tiles = cells // LANES
    rows = planes * tiles
    nreact = log_prefactor.shape[0]
    gx, gy = lax.axis_size("gx"), lax.axis_size("gy")
    f32 = jnp.float32
    flat = (
        state.reshape(comps, planes, tiles, LANES)
        .transpose(0, 2, 1, 3)
        .reshape(comps * rows, LANES)
    )

    def stay(array):
        return pltpu.with_memory_space_constraint(array, pltpu.HBM)

    vmem = pl.BlockSpec(memory_space=VMEM)
    anywhere = pl.BlockSpec(memory_space=pl.ANY)

    hbm = pl.BlockSpec(memory_space=pltpu.HBM)
    sds = jax.ShapeDtypeStruct
    ahead = pl.pallas_call(
        functools.partial(ahead_kernel, comps, planes, tiles),
        out_shape=sds((comps * tiles, 2, LANES), f32),
        in_specs=[hbm],
        out_specs=vmem,
        scratch_shapes=[pltpu.SemaphoreType.DMA((1,))],
        compiler_params=params(8),
        name="ahead",
    )(stay(flat.reshape(comps * tiles, planes // 2, 2, LANES)))
    beside, low, high = pl.pallas_call(
        functools.partial(pack_kernel, comps, planes, tiles),
        out_shape=(
            sds((comps, 2, tiles, LANES), f32),
            sds((comps // 2, planes, LANES), f32),
            sds((comps // 2, planes, LANES), f32),
        ),
        in_specs=[vmem],
        out_specs=[vmem] * 3,
        compiler_params=params(16),
        name="pack",
    )(flat)

    outer = [(i, (i + 1) % gx) for i in range(1, gx, 2)]
    outer = outer + [(t, s) for s, t in outer]
    inner = [(i, i + 1) for i in range(0, gx, 2)]
    inner = inner + [(t, s) for s, t in inner]
    forward = [(i, (i + 1) % gy) for i in range(gy)]
    backward = [(t, s) for s, t in forward]
    ha = lax.ppermute(ahead, "gx", outer)
    hb = lax.ppermute(beside, "gx", inner)
    zl = lax.ppermute(high, "gy", forward)
    zh = lax.ppermute(low, "gy", backward)

    padded = pl.cdiv(nreact, LANES) * LANES
    wide = pl.cdiv(nreact, 16) * 16
    part, dv = pl.pallas_call(
        functools.partial(main_kernel, comps, planes, tiles, nreact),
        out_shape=(sds((comps * rows, LANES), f32), sds((comps * planes, LANES), f32)),
        in_specs=[vmem, vmem] + [hbm] * 9,
        out_specs=(vmem, vmem),
        scratch_shapes=[
            SMEM((comps,), f32),
            SMEM(substeps.shape, jnp.int32),
            SMEM(flame.shape, jnp.int32),
            VMEM((nreact,), f32),
            VMEM((nreact,), f32),
            VMEM((nreact,), f32),
            VMEM((comps - 1, 2 * nreact), f32),
            VMEM((comps - 1, nreact), f32),
            VMEM((PIECE, padded), f32),
            VMEM((2 * PIECE, padded), f32),
            VMEM((wide, 3 * PIECE), jnp.bfloat16),
            VMEM((2 * PIECE, 2 * padded), jnp.bfloat16),
            VMEM((PIECE, GROUP * LANES), f32),
            VMEM((GROUP, comps, LANES), f32),
            VMEM((1, GROUP * LANES), f32),
            VMEM((1, GROUP * LANES), f32),
            VMEM((many_of(comps) * rows, 2 * LANES), f32),
            VMEM((many_of(comps) * rows, 2 * LANES), f32),
            SMEM((rows + 1,), jnp.int32),
            pltpu.SemaphoreType.DMA((8,)),
            pltpu.SemaphoreType.DMA((GROUP,)),
        ],
        compiler_params=params(24),
        cost_estimate=pl.CostEstimate(
            flops=2_000_000_000, bytes_accessed=16_000_000, transcendentals=1_000_000
        ),
        name="main",
    )(
        flat,
        shift_matrix(),
        *map(
            stay,
            (
                flat,
                diffusivity,
                substeps,
                flame,
                log_prefactor,
                activation,
                heat,
                reactants.T,
                products,
            ),
        ),
    )

    whole = sds((comps * rows, LANES), f32)
    cost = pl.CostEstimate(flops=1_000_000, bytes_accessed=3_000_000, transcendentals=0)
    part, out = pl.pallas_call(
        functools.partial(inner_edges_kernel, comps, planes, tiles),
        out_shape=(whole, whole),
        in_specs=[vmem] * 5,
        out_specs=(vmem, anywhere),
        scratch_shapes=[pltpu.SemaphoreType.DMA((4,))],
        input_output_aliases={0: 0},
        compiler_params=params(16),
        cost_estimate=cost,
        name="inner_edges",
    )(part, dv, hb, zl, zh)
    _, out = pl.pallas_call(
        functools.partial(outer_edges_kernel, comps, planes, tiles),
        out_shape=(whole, whole),
        in_specs=[vmem] * 3 + [anywhere],
        out_specs=(vmem, anywhere),
        scratch_shapes=[pltpu.SemaphoreType.DMA((2,))],
        input_output_aliases={0: 0, 3: 1},
        compiler_params=params(16),
        cost_estimate=cost,
        name="outer_edges",
    )(part, dv, ha.reshape(comps * tiles * 2, LANES), out)
    return (
        out.reshape(comps, tiles, planes, LANES).transpose(0, 2, 1, 3).reshape(comps, planes, cells)
    )


def solution(mesh):
    in_specs = (P(None, "gx", "gy"), P(), P(), P(), P(), P(), P(), P("gx", "gy"), P("gx", "gy"))
    out_specs = P(None, "gx", "gy")

    return jax.shard_map(
        per_device, mesh=mesh, in_specs=in_specs, out_specs=out_specs, check_vma=False
    )
```

```python
import functools

import jax
import jax.numpy as jnp
import numpy as np
from jax import lax
from jax.experimental import pallas as pl
from jax.experimental.pallas import tpu as pltpu
from jax.sharding import PartitionSpec as P

NZ = 32
LANES = 128
near_weight = 4.0 / 3.0
far_weight = 1.0 / 12.0
LOG2E = 1.4426950408889634
GROUP = 4
PIECE = 64


VMEM = pltpu.VMEM
SMEM = pltpu.SMEM


def params(mib):
    return pltpu.CompilerParams(vmem_limit_bytes=mib << 20)


def odd_place(axis):
    return lax.rem(lax.axis_index(axis), 2)


def ahead_kernel(comps, planes, tiles, s_hbm, o_ref, sem):
    pair = odd_place("gx") * (planes // 2 - 1)
    total = comps * tiles
    parts = sem.shape[0]
    copies = []
    for i in range(parts):
        begin, end = total * i // parts, total * (i + 1) // parts
        where = pl.ds(begin, end - begin)
        copies.append(pltpu.make_async_copy(s_hbm.at[where, pair], o_ref.at[where], sem.at[i]))
        copies[-1].start()
    for copy in copies:
        copy.wait()


def pack_kernel(comps, planes, tiles, s_ref, b_ref, low_ref, high_ref):
    rows = planes * tiles
    lane = lax.broadcasted_iota(jnp.int32, (planes, LANES), 1)
    off_b = (1 - odd_place("gx")) * (planes - 2)
    for c in range(comps):
        for p in range(2):
            b_ref[c, p] = s_ref[pl.ds(c * rows + off_b + p, tiles, stride=planes), :]
    last = (tiles - 1) * planes
    for k in range(comps // 2):
        first, second = 2 * k * rows, (2 * k + 1) * rows
        low_a = s_ref[first : first + planes, :]
        low_b = s_ref[second : second + planes, :]
        high_a = s_ref[first + last : first + last + planes, :]
        high_b = s_ref[second + last : second + last + planes, :]
        low_ref[k] = jnp.where(lane < 64, low_a, pltpu.roll(low_b, 64, 1))
        high_ref[k] = jnp.where(lane < 64, pltpu.roll(high_a, 64, 1), high_b)


def split3(value):
    high = value.astype(jnp.bfloat16)
    rest = value - high.astype(jnp.float32)
    middle = rest.astype(jnp.bfloat16)
    low = (rest - middle.astype(jnp.float32)).astype(jnp.bfloat16)
    return high, middle, low


def shift_matrix():
    source = np.arange(LANES)[:, None]
    target = np.arange(LANES)[None, :]
    rows = LANES // NZ
    ys, yt = source // NZ, target // NZ
    turn = (target - source) % NZ
    same_z = turn == 0
    weights = {1: 16.0, 2: -1.0}
    own = np.where(source == target, -90.0, 0.0)
    cross = np.zeros_like(own)
    apart = np.where(target < LANES // 2, yt + rows - ys, ys + rows - yt)
    for distance, weight in weights.items():
        own += np.where((ys == yt) & (np.minimum(turn, NZ - turn) == distance), weight, 0.0)
        own += np.where(same_z & (abs(yt - ys) == distance), weight, 0.0)
        cross += np.where(same_z & (apart == distance), weight, 0.0)
    one = np.concatenate([own, cross], 1)
    return jnp.asarray(np.concatenate([one, one], 0), jnp.bfloat16)


def many_of(comps):
    return max(n for n in range(1, 7) if comps % n == 0)


def main_kernel(
    comps,
    planes,
    tiles,
    nreact,
    s_ref,
    shift_ref,
    d_hbm,
    sub_hbm,
    flame_hbm,
    lp_hbm,
    act_hbm,
    heat_hbm,
    rt_hbm,
    pr_hbm,
    o_ref,
    dv_ref,
    d_ref,
    sub_ref,
    flame_ref,
    lp_ref,
    act_ref,
    heat_ref,
    rt_ref,
    pr_ref,
    q_ref,
    p_ref,
    w1_ref,
    w2_ref,
    a_ref,
    old_ref,
    t_ref,
    st_ref,
    even_ref,
    odd_ref,
    third_ref,
    pos_ref,
    sem,
):
    rows = planes * tiles
    species = comps - 1
    block_rows = planes * tiles
    loads = [
        pltpu.make_async_copy(source, target, sem.at[i])
        for i, (source, target) in enumerate(
            (
                (d_hbm, d_ref),
                (sub_hbm, sub_ref),
                (flame_hbm, flame_ref),
                (lp_hbm, lp_ref),
                (act_hbm, act_ref),
                (heat_hbm, heat_ref),
                (rt_hbm, rt_ref),
                (pr_hbm, pr_ref),
            )
        )
    ]
    for load in loads:
        load.start()

    def scan_blocks():
        count = jnp.int32(0)
        for x in range(planes):
            for b in range(tiles):
                pos_ref[count] = b * planes + x
                count = count + flame_ref[x, b]
        for c in range(comps):
            dv_ref[c * planes : (c + 1) * planes, :] = jnp.full(
                (planes, LANES), d_ref[c], jnp.float32
            )
        return count

    padded = q_ref.shape[1]
    wide = w1_ref.shape[0]

    def tables():
        q_ref[...] = jnp.zeros_like(q_ref)
        p_ref[...] = jnp.zeros_like(p_ref)
        q_ref[0:species, 0:nreact] = rt_ref[:, 0:nreact] + rt_ref[:, nreact : 2 * nreact]
        p_ref[0:species, 0:nreact] = pr_ref[...]
        p_ref[PIECE : PIECE + species, 0:nreact] = q_ref[0:species, 0:nreact]
        for i, piece in enumerate(split3(act_ref[...].reshape(1, nreact) * (-LOG2E))):
            q_ref[species + i : species + i + 1, 0:nreact] = piece.astype(jnp.float32)
        for i, piece in enumerate(split3(lp_ref[...].reshape(1, nreact) * LOG2E)):
            q_ref[species + 3 + i : species + 4 + i, 0:nreact] = piece.astype(jnp.float32)
        for i, piece in enumerate(split3(heat_ref[...].reshape(1, nreact))):
            p_ref[species + i : species + i + 1, 0:nreact] = piece.astype(jnp.float32)
        q = q_ref[...]
        w1 = jnp.transpose(jnp.concatenate([q, q, q], 0))
        w1_ref[...] = w1[0:wide].astype(jnp.bfloat16)
        w = p_ref[...].astype(jnp.bfloat16)
        head, rest = w[:, :256], w[:, 256:padded]
        w2_ref[...] = jnp.concatenate([head, head, rest, rest], 1)
        a_ref[...] = jnp.ones_like(a_ref)

    many = many_of(comps)
    size = many * rows
    groups = comps // many
    shape = (many, tiles, planes, LANES)
    lane = lax.broadcasted_iota(jnp.int32, (1, 1, planes, LANES), 3)
    x = lax.broadcasted_iota(jnp.int32, (1, 1, planes, LANES), 2)
    zero = jnp.zeros((many, 1, planes, LANES), jnp.float32)
    near, far = near_weight * 12.0, -far_weight * 12.0
    weights = {
        -1: jnp.where(x > 0, near, 0.0),
        1: jnp.where(x < planes - 1, near, 0.0),
        -2: jnp.where(x > 1, far, 0.0),
        2: jnp.where(x < planes - 2, far, 0.0),
    }

    def product(i, buffer):
        flat = s_ref[pl.ds(pl.multiple_of(i * size, size), size), :]
        high = flat.astype(jnp.bfloat16)
        low = (flat - high.astype(jnp.float32)).astype(jnp.bfloat16)
        both = jnp.concatenate([high, low], 1)
        buffer[...] = jnp.dot(both, shift_ref[...], preferred_element_type=jnp.float32)

    def combine(i, buffer, inside):
        start = pl.multiple_of(i * size, size)
        v = s_ref[pl.ds(start, size), :].reshape(shape)
        own = buffer[:, :LANES].reshape(shape)
        cross = buffer[:, LANES:].reshape(shape)
        before = jnp.concatenate([zero, cross[:, :-1]], 1)
        after = jnp.concatenate([cross[:, 1:], zero], 1)
        own = own + jnp.where(lane < 64, before, after)
        for offset, weight in weights.items():
            if inside:
                moved = s_ref[pl.ds(start + offset, size), :].reshape(shape)
            else:
                moved = pltpu.roll(v, (-offset) % planes, 2)
            own = own + moved * weight
        for j in range(many):
            where = pl.ds(pl.multiple_of(start + j * rows, rows), rows)
            scale = d_ref[i * many + j] * (1.0 / 12.0)
            o_ref[where, :] = (v[j] + scale * own[j]).reshape(rows, LANES)

    buffers = (even_ref, odd_ref, third_ref)

    def make(i):
        if i < groups:
            product(i, buffers[i % 3])

    def use(i):
        combine(i, buffers[i % 3], 0 < i < groups - 1)

    make(0)
    make(1)
    for load in loads[:3]:
        load.wait()
    turn = groups // 2
    always = flame_ref[0, 0] >= 0

    @pl.when(always)
    def _():
        pos_ref[rows] = scan_blocks()
        for i in range(turn):
            make(i + 2)
            use(i)

    for load in loads[3:]:
        load.wait()

    @pl.when(always)
    def _():
        tables()
        for i in range(turn, groups):
            make(i + 2)
            use(i)

    count = pos_ref[rows]

    @pl.when(count > 0)
    def _():
        arow = lax.broadcasted_iota(jnp.int32, a_ref.shape, 0)

        def group(g, carry):
            most = jnp.int32(0)
            pieces = []
            for i in range(GROUP):
                slot = g * GROUP + i
                here = jnp.where(slot < count, slot, 0)
                at = pos_ref[here]
                n = jnp.where(
                    slot < count, sub_ref[lax.rem(at, planes), lax.div(at, planes)], 0
                )
                most = jnp.maximum(most, n)
                cols = slice(i * LANES, (i + 1) * LANES)
                mine = s_ref[pl.ds(block_rows + at, species, stride=rows), :]
                a_ref[0:species, cols] = mine
                old_ref[0:species, cols] = mine
                t_ref[:, cols] = s_ref[pl.ds(at, 1), :]
                pieces.append(jnp.full((1, LANES), n, jnp.int32))
            counts = jnp.concatenate(pieces, 1)
            st_ref[...] = 1.0 / jnp.maximum(counts, 1).astype(jnp.float32)

            def substep(k, inner):
                step = jnp.where(counts > k, st_ref[...], 0.0)
                amounts = a_ref[...]
                thermal = t_ref[...]
                inverse = 1.0 / thermal
                terms = jnp.where(
                    arow < species,
                    jnp.log2(amounts),
                    jnp.where(
                        arow < species + 3, inverse, jnp.where(arow < species + 6, 1.0, 0.0)
                    ),
                )
                rhs = jnp.concatenate(split3(terms), 0)
                exponent = jnp.dot(w1_ref[...], rhs, preferred_element_type=jnp.float32)
                progress = jnp.exp2(exponent)
                high = progress.astype(jnp.bfloat16)
                low = (progress - high.astype(jnp.float32)).astype(jnp.bfloat16)
                gap = 2 * LANES - wide + LANES
                rhs = jnp.concatenate(
                    [high[:256], low[:256], high[256:], high[:gap], low[256:], low[:gap]], 0
                )
                out = jnp.dot(w2_ref[...], rhs, preferred_element_type=jnp.float32)
                produced = out[:PIECE]
                loss = out[PIECE:]
                warm = out[species : species + 1] + (
                    out[species + 1 : species + 2] + out[species + 2 : species + 3]
                )
                a_ref[...] = (amounts + step * produced) * (amounts / (amounts + step * loss))
                t_ref[...] = thermal + step * warm
                return inner

            lax.fori_loop(0, most, substep, 0)

            for i in range(GROUP):
                slot = g * GROUP + i

                @pl.when(slot < count)
                def _(i=i, slot=slot):
                    at = pos_ref[slot]
                    cols = slice(i * LANES, (i + 1) * LANES)
                    where = pl.ds(block_rows + at, species, stride=rows)
                    change = a_ref[0:species, cols] - old_ref[0:species, cols]
                    o_ref[where, :] = o_ref[where, :] + change
                    top = pl.ds(at, 1)
                    o_ref[top, :] = o_ref[top, :] + (t_ref[:, cols] - s_ref[top, :])

            return carry

        lax.fori_loop(0, (count + (GROUP - 1)) // GROUP, group, 0)


def add_planes(planes, tiles, work, dv_ref, plane, begin, end, side):
    rows = planes * tiles
    for c in range(begin, end):
        near = plane(c, 1 - side)
        far = plane(c, side)
        weight = dv_ref[c * planes : (c + 1) * planes, :]
        first = pl.ds(c * rows + side * (planes - 1), tiles, stride=planes)
        second = pl.ds(c * rows + 1 + side * (planes - 3), tiles, stride=planes)
        one, two = work[first, :], work[second, :]
        work[first, :] = one + weight * (near_weight * near - far_weight * far)
        work[second, :] = two - (weight * far_weight) * near


def write_out(planes, tiles, work, out, sem, first, last, x, count):
    shape = (work.shape[0] // planes, planes, LANES)
    where = (pl.ds(first * tiles, (last - first) * tiles), pl.ds(x, count))
    return pltpu.make_async_copy(
        work.reshape(*shape).at[where], out.reshape(*shape).at[where], sem
    )


def inner_edges_kernel(
    comps, planes, tiles, part_ref, dv_ref, hb_ref, zl_ref, zh_ref, work, out, sem
):
    del part_ref
    rows = planes * tiles
    lane = lax.broadcasted_iota(jnp.int32, (planes, LANES), 1)
    last = (tiles - 1) * planes
    above = jnp.where(lane % 64 < NZ, near_weight, 0.0)
    below = jnp.where(lane % 64 >= NZ, near_weight, 0.0)
    lower = jnp.where(lane < 64, 1.0, 0.0)
    upper = jnp.where(lane < 64, 0.0, 1.0)

    def pair(k):
        low, high = zl_ref[k], zh_ref[k]
        low = pltpu.roll(low, LANES - NZ, 1) * above - far_weight * low
        high = pltpu.roll(high, NZ, 1) * below - far_weight * high
        lows = (low * lower, pltpu.roll(low * upper, 64, 1))
        highs = (pltpu.roll(high * lower, 64, 1), high * upper)
        for j in range(2):
            c = 2 * k + j
            weight = dv_ref[c * planes : (c + 1) * planes, :]
            top = slice(c * rows, c * rows + planes)
            end = slice(c * rows + last, c * rows + last + planes)
            work[top, :] = work[top, :] + weight * lows[j]
            work[end, :] = work[end, :] + weight * highs[j]

    half = comps // 2
    cuts = (0, 2 * (half // 7), 2 * (half // 2), 2 * (half * 5 // 6), comps)
    spans = list(zip(cuts, cuts[1:]))
    odd = odd_place("gx")
    for side in range(2):

        @pl.when(odd == 1 - side)
        def _(side=side):
            kept = (2 * side, planes - 2)
            for i, (first, end) in enumerate(spans):
                for k in range(first // 2, end // 2):
                    pair(k)
                add_planes(
                    planes, tiles, work, dv_ref, lambda c, p: hb_ref[c, p], first, end, side
                )
                write_out(planes, tiles, work, out, sem.at[i], first, end, *kept).start()
            for i, (first, end) in enumerate(spans):
                write_out(planes, tiles, work, out, sem.at[i], first, end, *kept).wait()


def outer_edges_kernel(comps, planes, tiles, part_ref, dv_ref, h_ref, prev, work, out, sem):
    del part_ref, prev
    odd = odd_place("gx")

    def plane(c, p):
        return h_ref[pl.ds(c * 2 * tiles + p, tiles, stride=2), :]

    bounds = [0, comps // 3, comps]
    spans = list(zip(bounds, bounds[1:]))
    for side in range(2):

        @pl.when(odd == side)
        def _(side=side):
            kept = (side * (planes - 2), 2)
            for i, (first, last) in enumerate(spans):
                add_planes(planes, tiles, work, dv_ref, plane, first, last, side)
                write_out(planes, tiles, work, out, sem.at[i], first, last, *kept).start()
            for i, (first, last) in enumerate(spans):
                write_out(planes, tiles, work, out, sem.at[i], first, last, *kept).wait()


def per_device(
    state, diffusivity, log_prefactor, activation, heat, reactants, products, substeps, flame
):
    comps, planes, cells = state.shape
    tiles = cells // LANES
    rows = planes * tiles
    nreact = log_prefactor.shape[0]
    gx, gy = lax.axis_size("gx"), lax.axis_size("gy")
    f32 = jnp.float32
    flat = (
        state.reshape(comps, planes, tiles, LANES)
        .transpose(0, 2, 1, 3)
        .reshape(comps * rows, LANES)
    )

    def stay(array):
        return pltpu.with_memory_space_constraint(array, pltpu.HBM)

    vmem = pl.BlockSpec(memory_space=VMEM)
    anywhere = pl.BlockSpec(memory_space=pl.ANY)

    hbm = pl.BlockSpec(memory_space=pltpu.HBM)
    sds = jax.ShapeDtypeStruct
    ahead = pl.pallas_call(
        functools.partial(ahead_kernel, comps, planes, tiles),
        out_shape=sds((comps * tiles, 2, LANES), f32),
        in_specs=[hbm],
        out_specs=vmem,
        scratch_shapes=[pltpu.SemaphoreType.DMA((1,))],
        compiler_params=params(8),
        name="ahead",
    )(stay(flat.reshape(comps * tiles, planes // 2, 2, LANES)))
    beside, low, high = pl.pallas_call(
        functools.partial(pack_kernel, comps, planes, tiles),
        out_shape=(
            sds((comps, 2, tiles, LANES), f32),
            sds((comps // 2, planes, LANES), f32),
            sds((comps // 2, planes, LANES), f32),
        ),
        in_specs=[vmem],
        out_specs=[vmem] * 3,
        compiler_params=params(16),
        name="pack",
    )(flat)

    outer = [(i, (i + 1) % gx) for i in range(1, gx, 2)]
    outer = outer + [(t, s) for s, t in outer]
    inner = [(i, i + 1) for i in range(0, gx, 2)]
    inner = inner + [(t, s) for s, t in inner]
    forward = [(i, (i + 1) % gy) for i in range(gy)]
    backward = [(t, s) for s, t in forward]
    ha = lax.ppermute(ahead, "gx", outer)
    hb = lax.ppermute(beside, "gx", inner)
    zl = lax.ppermute(high, "gy", forward)
    zh = lax.ppermute(low, "gy", backward)

    padded = pl.cdiv(nreact, LANES) * LANES
    wide = pl.cdiv(nreact, 16) * 16
    part, dv = pl.pallas_call(
        functools.partial(main_kernel, comps, planes, tiles, nreact),
        out_shape=(sds((comps * rows, LANES), f32), sds((comps * planes, LANES), f32)),
        in_specs=[vmem, vmem] + [hbm] * 8,
        out_specs=(vmem, vmem),
        scratch_shapes=[
            SMEM((comps,), f32),
            SMEM(substeps.shape, jnp.int32),
            SMEM(flame.shape, jnp.int32),
            VMEM((nreact,), f32),
            VMEM((nreact,), f32),
            VMEM((nreact,), f32),
            VMEM((comps - 1, 2 * nreact), f32),
            VMEM((comps - 1, nreact), f32),
            VMEM((PIECE, padded), f32),
            VMEM((2 * PIECE, padded), f32),
            VMEM((wide, 3 * PIECE), jnp.bfloat16),
            VMEM((2 * PIECE, 2 * padded), jnp.bfloat16),
            VMEM((PIECE, GROUP * LANES), f32),
            VMEM((PIECE, GROUP * LANES), f32),
            VMEM((1, GROUP * LANES), f32),
            VMEM((1, GROUP * LANES), f32),
            VMEM((many_of(comps) * rows, 2 * LANES), f32),
            VMEM((many_of(comps) * rows, 2 * LANES), f32),
            VMEM((many_of(comps) * rows, 2 * LANES), f32),
            SMEM((rows + 1,), jnp.int32),
            pltpu.SemaphoreType.DMA((8,)),
        ],
        compiler_params=params(24),
        cost_estimate=pl.CostEstimate(
            flops=2_000_000_000, bytes_accessed=16_000_000, transcendentals=1_000_000
        ),
        name="main",
    )(
        flat,
        shift_matrix(),
        *map(
            stay,
            (
                diffusivity,
                substeps,
                flame,
                log_prefactor,
                activation,
                heat,
                reactants.T,
                products,
            ),
        ),
    )

    whole = sds((comps * rows, LANES), f32)
    cost = pl.CostEstimate(flops=1_000_000, bytes_accessed=3_000_000, transcendentals=0)
    part, out = pl.pallas_call(
        functools.partial(inner_edges_kernel, comps, planes, tiles),
        out_shape=(whole, whole),
        in_specs=[vmem] * 5,
        out_specs=(vmem, anywhere),
        scratch_shapes=[pltpu.SemaphoreType.DMA((4,))],
        input_output_aliases={0: 0},
        compiler_params=params(16),
        cost_estimate=cost,
        name="inner_edges",
    )(part, dv, hb, zl, zh)
    _, out = pl.pallas_call(
        functools.partial(outer_edges_kernel, comps, planes, tiles),
        out_shape=(whole, whole),
        in_specs=[vmem] * 3 + [anywhere],
        out_specs=(vmem, anywhere),
        scratch_shapes=[pltpu.SemaphoreType.DMA((2,))],
        input_output_aliases={0: 0, 3: 1},
        compiler_params=params(16),
        cost_estimate=cost,
        name="outer_edges",
    )(part, dv, ha.reshape(comps * tiles * 2, LANES), out)
    return (
        out.reshape(comps, tiles, planes, LANES).transpose(0, 2, 1, 3).reshape(comps, planes, cells)
    )


def solution(mesh):
    in_specs = (P(None, "gx", "gy"), P(), P(), P(), P(), P(), P(), P("gx", "gy"), P("gx", "gy"))
    out_specs = P(None, "gx", "gy")

    return jax.shard_map(
        per_device, mesh=mesh, in_specs=in_specs, out_specs=out_specs, check_vma=False
    )
```

```python
import functools

import jax
import jax.numpy as jnp
import numpy as np
from jax import lax
from jax.experimental import pallas as pl
from jax.experimental.pallas import tpu as pltpu
from jax.sharding import PartitionSpec as P

NZ = 32
LANES = 128
near_weight = 4.0 / 3.0
far_weight = 1.0 / 12.0
LOG2E = 1.4426950408889634
GROUP = 4
PIECE = 64


VMEM = pltpu.VMEM
SMEM = pltpu.SMEM


def params(mib):
    return pltpu.CompilerParams(vmem_limit_bytes=mib << 20)


def odd_place(axis):
    return lax.rem(lax.axis_index(axis), 2)


def ahead_kernel(comps, planes, tiles, s_hbm, o_ref, sem):
    pair = odd_place("gx") * (planes // 2 - 1)
    total = comps * tiles
    parts = sem.shape[0]
    copies = []
    for i in range(parts):
        begin, end = total * i // parts, total * (i + 1) // parts
        where = pl.ds(begin, end - begin)
        copies.append(pltpu.make_async_copy(s_hbm.at[where, pair], o_ref.at[where], sem.at[i]))
        copies[-1].start()
    for copy in copies:
        copy.wait()


def pack_kernel(comps, planes, tiles, s_ref, b_ref, low_ref, high_ref):
    rows = planes * tiles
    lane = lax.broadcasted_iota(jnp.int32, (planes, LANES), 1)
    off_b = (1 - odd_place("gx")) * (planes - 2)
    for c in range(comps):
        for p in range(2):
            b_ref[c, p] = s_ref[pl.ds(c * rows + off_b + p, tiles, stride=planes), :]
    last = (tiles - 1) * planes
    for k in range(comps // 2):
        first, second = 2 * k * rows, (2 * k + 1) * rows
        low_a = s_ref[first : first + planes, :]
        low_b = s_ref[second : second + planes, :]
        high_a = s_ref[first + last : first + last + planes, :]
        high_b = s_ref[second + last : second + last + planes, :]
        low_ref[k] = jnp.where(lane < 64, low_a, pltpu.roll(low_b, 64, 1))
        high_ref[k] = jnp.where(lane < 64, pltpu.roll(high_a, 64, 1), high_b)


def split3(value):
    high = value.astype(jnp.bfloat16)
    rest = value - high.astype(jnp.float32)
    middle = rest.astype(jnp.bfloat16)
    low = (rest - middle.astype(jnp.float32)).astype(jnp.bfloat16)
    return high, middle, low


def shift_matrix():
    source = np.arange(LANES)[:, None]
    target = np.arange(LANES)[None, :]
    rows = LANES // NZ
    ys, yt = source // NZ, target // NZ
    turn = (target - source) % NZ
    same_z = turn == 0
    weights = {1: 16.0, 2: -1.0}
    own = np.where(source == target, -90.0, 0.0)
    cross = np.zeros_like(own)
    apart = np.where(target < LANES // 2, yt + rows - ys, ys + rows - yt)
    for distance, weight in weights.items():
        own += np.where((ys == yt) & (np.minimum(turn, NZ - turn) == distance), weight, 0.0)
        own += np.where(same_z & (abs(yt - ys) == distance), weight, 0.0)
        cross += np.where(same_z & (apart == distance), weight, 0.0)
    one = np.concatenate([own, cross], 1)
    return jnp.asarray(np.concatenate([one, one], 0), jnp.bfloat16)


def many_of(comps):
    return max(n for n in range(1, 4) if comps % n == 0)


def main_kernel(
    comps,
    planes,
    tiles,
    nreact,
    s_ref,
    shift_ref,
    d_hbm,
    sub_hbm,
    flame_hbm,
    lp_hbm,
    act_hbm,
    heat_hbm,
    rt_hbm,
    pr_hbm,
    o_ref,
    dv_ref,
    d_ref,
    sub_ref,
    flame_ref,
    lp_ref,
    act_ref,
    heat_ref,
    rt_ref,
    pr_ref,
    q_ref,
    p_ref,
    w1_ref,
    w2_ref,
    a_ref,
    old_ref,
    t_ref,
    st_ref,
    even_ref,
    odd_ref,
    third_ref,
    pos_ref,
    sem,
):
    rows = planes * tiles
    species = comps - 1
    block_rows = planes * tiles
    loads = [
        pltpu.make_async_copy(source, target, sem.at[i])
        for i, (source, target) in enumerate(
            (
                (d_hbm, d_ref),
                (sub_hbm, sub_ref),
                (flame_hbm, flame_ref),
                (lp_hbm, lp_ref),
                (act_hbm, act_ref),
                (heat_hbm, heat_ref),
                (rt_hbm, rt_ref),
                (pr_hbm, pr_ref),
            )
        )
    ]
    for load in loads:
        load.start()

    def scan_blocks():
        count = jnp.int32(0)
        for x in range(planes):
            for b in range(tiles):
                pos_ref[count] = b * planes + x
                count = count + flame_ref[x, b]
        for c in range(comps):
            dv_ref[c * planes : (c + 1) * planes, :] = jnp.full(
                (planes, LANES), d_ref[c], jnp.float32
            )
        return count

    padded = q_ref.shape[1]
    wide = w1_ref.shape[0]

    def tables():
        q_ref[...] = jnp.zeros_like(q_ref)
        p_ref[...] = jnp.zeros_like(p_ref)
        q_ref[0:species, 0:nreact] = rt_ref[:, 0:nreact] + rt_ref[:, nreact : 2 * nreact]
        p_ref[0:species, 0:nreact] = pr_ref[...]
        p_ref[PIECE : PIECE + species, 0:nreact] = q_ref[0:species, 0:nreact]
        for i, piece in enumerate(split3(act_ref[...].reshape(1, nreact) * (-LOG2E))):
            q_ref[species + i : species + i + 1, 0:nreact] = piece.astype(jnp.float32)
        for i, piece in enumerate(split3(lp_ref[...].reshape(1, nreact) * LOG2E)):
            q_ref[species + 3 + i : species + 4 + i, 0:nreact] = piece.astype(jnp.float32)
        for i, piece in enumerate(split3(heat_ref[...].reshape(1, nreact))):
            p_ref[species + i : species + i + 1, 0:nreact] = piece.astype(jnp.float32)
        q = q_ref[...]
        w1 = jnp.transpose(jnp.concatenate([q, q, q], 0))
        w1_ref[...] = w1[0:wide].astype(jnp.bfloat16)
        w = p_ref[...].astype(jnp.bfloat16)
        head, rest = w[:, :256], w[:, 256:padded]
        w2_ref[...] = jnp.concatenate([head, head, rest, rest], 1)
        a_ref[...] = jnp.ones_like(a_ref)

    many = many_of(comps)
    size = many * rows
    groups = comps // many
    shape = (many, tiles, planes, LANES)
    lane = lax.broadcasted_iota(jnp.int32, (1, 1, planes, LANES), 3)
    x = lax.broadcasted_iota(jnp.int32, (1, 1, planes, LANES), 2)
    zero = jnp.zeros((many, 1, planes, LANES), jnp.float32)
    near, far = near_weight * 12.0, -far_weight * 12.0
    weights = {
        -1: jnp.where(x > 0, near, 0.0),
        1: jnp.where(x < planes - 1, near, 0.0),
        -2: jnp.where(x > 1, far, 0.0),
        2: jnp.where(x < planes - 2, far, 0.0),
    }

    def product(i, buffer):
        flat = s_ref[pl.ds(pl.multiple_of(i * size, size), size), :]
        high = flat.astype(jnp.bfloat16)
        low = (flat - high.astype(jnp.float32)).astype(jnp.bfloat16)
        both = jnp.concatenate([high, low], 1)
        buffer[...] = jnp.dot(both, shift_ref[...], preferred_element_type=jnp.float32)

    def combine(i, buffer, inside):
        start = pl.multiple_of(i * size, size)
        v = s_ref[pl.ds(start, size), :].reshape(shape)
        own = buffer[:, :LANES].reshape(shape)
        cross = buffer[:, LANES:].reshape(shape)
        before = jnp.concatenate([zero, cross[:, :-1]], 1)
        after = jnp.concatenate([cross[:, 1:], zero], 1)
        own = own + jnp.where(lane < 64, before, after)
        for offset, weight in weights.items():
            if inside:
                moved = s_ref[pl.ds(start + offset, size), :].reshape(shape)
            else:
                moved = pltpu.roll(v, (-offset) % planes, 2)
            own = own + moved * weight
        for j in range(many):
            where = pl.ds(pl.multiple_of(start + j * rows, rows), rows)
            scale = d_ref[i * many + j] * (1.0 / 12.0)
            o_ref[where, :] = (v[j] + scale * own[j]).reshape(rows, LANES)

    buffers = (even_ref, odd_ref, third_ref)

    def make(i):
        if i < groups:
            product(i, buffers[i % 3])

    def use(i):
        combine(i, buffers[i % 3], 0 < i < groups - 1)

    make(0)
    make(1)
    for load in loads[:3]:
        load.wait()
    turn = groups // 2
    always = flame_ref[0, 0] >= 0

    @pl.when(always)
    def _():
        pos_ref[rows] = scan_blocks()
        for i in range(turn):
            make(i + 2)
            use(i)

    for load in loads[3:]:
        load.wait()

    @pl.when(always)
    def _():
        tables()
        for i in range(turn, groups):
            make(i + 2)
            use(i)

    count = pos_ref[rows]

    @pl.when(count > 0)
    def _():
        arow = lax.broadcasted_iota(jnp.int32, a_ref.shape, 0)

        def group(g, carry):
            most = jnp.int32(0)
            pieces = []
            for i in range(GROUP):
                slot = g * GROUP + i
                here = jnp.where(slot < count, slot, 0)
                at = pos_ref[here]
                n = jnp.where(
                    slot < count, sub_ref[lax.rem(at, planes), lax.div(at, planes)], 0
                )
                most = jnp.maximum(most, n)
                cols = slice(i * LANES, (i + 1) * LANES)
                mine = s_ref[pl.ds(block_rows + at, species, stride=rows), :]
                a_ref[0:species, cols] = mine
                old_ref[0:species, cols] = mine
                t_ref[:, cols] = s_ref[pl.ds(at, 1), :]
                pieces.append(jnp.full((1, LANES), n, jnp.int32))
            counts = jnp.concatenate(pieces, 1)
            st_ref[...] = 1.0 / jnp.maximum(counts, 1).astype(jnp.float32)

            def substep(k, inner):
                step = jnp.where(counts > k, st_ref[...], 0.0)
                amounts = a_ref[...]
                thermal = t_ref[...]
                inverse = 1.0 / thermal
                terms = jnp.where(
                    arow < species,
                    jnp.log2(amounts),
                    jnp.where(
                        arow < species + 3, inverse, jnp.where(arow < species + 6, 1.0, 0.0)
                    ),
                )
                rhs = jnp.concatenate(split3(terms), 0)
                exponent = jnp.dot(w1_ref[...], rhs, preferred_element_type=jnp.float32)
                progress = jnp.exp2(exponent)
                high = progress.astype(jnp.bfloat16)
                low = (progress - high.astype(jnp.float32)).astype(jnp.bfloat16)
                gap = 2 * LANES - wide + LANES
                rhs = jnp.concatenate(
                    [high[:256], low[:256], high[256:], high[:gap], low[256:], low[:gap]], 0
                )
                out = jnp.dot(w2_ref[...], rhs, preferred_element_type=jnp.float32)
                produced = out[:PIECE]
                loss = out[PIECE:]
                warm = out[species : species + 1] + (
                    out[species + 1 : species + 2] + out[species + 2 : species + 3]
                )
                a_ref[...] = (amounts + step * produced) * (amounts / (amounts + step * loss))
                t_ref[...] = thermal + step * warm
                return inner

            lax.fori_loop(0, most, substep, 0)

            for i in range(GROUP):
                slot = g * GROUP + i

                @pl.when(slot < count)
                def _(i=i, slot=slot):
                    at = pos_ref[slot]
                    cols = slice(i * LANES, (i + 1) * LANES)
                    where = pl.ds(block_rows + at, species, stride=rows)
                    change = a_ref[0:species, cols] - old_ref[0:species, cols]
                    o_ref[where, :] = o_ref[where, :] + change
                    top = pl.ds(at, 1)
                    o_ref[top, :] = o_ref[top, :] + (t_ref[:, cols] - s_ref[top, :])

            return carry

        lax.fori_loop(0, (count + (GROUP - 1)) // GROUP, group, 0)


def add_planes(planes, tiles, work, dv_ref, plane, begin, end, side):
    rows = planes * tiles
    for c in range(begin, end):
        near = plane(c, 1 - side)
        far = plane(c, side)
        weight = dv_ref[c * planes : (c + 1) * planes, :]
        first = pl.ds(c * rows + side * (planes - 1), tiles, stride=planes)
        second = pl.ds(c * rows + 1 + side * (planes - 3), tiles, stride=planes)
        one, two = work[first, :], work[second, :]
        work[first, :] = one + weight * (near_weight * near - far_weight * far)
        work[second, :] = two - (weight * far_weight) * near


def write_out(planes, tiles, work, out, sem, first, last, x, count):
    shape = (work.shape[0] // planes, planes, LANES)
    where = (pl.ds(first * tiles, (last - first) * tiles), pl.ds(x, count))
    return pltpu.make_async_copy(
        work.reshape(*shape).at[where], out.reshape(*shape).at[where], sem
    )


def inner_edges_kernel(
    comps, planes, tiles, part_ref, dv_ref, hb_ref, zl_ref, zh_ref, work, out, sem
):
    del part_ref
    rows = planes * tiles
    lane = lax.broadcasted_iota(jnp.int32, (planes, LANES), 1)
    last = (tiles - 1) * planes
    above = jnp.where(lane % 64 < NZ, near_weight, 0.0)
    below = jnp.where(lane % 64 >= NZ, near_weight, 0.0)
    lower = jnp.where(lane < 64, 1.0, 0.0)
    upper = jnp.where(lane < 64, 0.0, 1.0)

    def pair(k):
        low, high = zl_ref[k], zh_ref[k]
        low = pltpu.roll(low, LANES - NZ, 1) * above - far_weight * low
        high = pltpu.roll(high, NZ, 1) * below - far_weight * high
        lows = (low * lower, pltpu.roll(low * upper, 64, 1))
        highs = (pltpu.roll(high * lower, 64, 1), high * upper)
        for j in range(2):
            c = 2 * k + j
            weight = dv_ref[c * planes : (c + 1) * planes, :]
            top = slice(c * rows, c * rows + planes)
            end = slice(c * rows + last, c * rows + last + planes)
            work[top, :] = work[top, :] + weight * lows[j]
            work[end, :] = work[end, :] + weight * highs[j]

    half = comps // 2
    cuts = (0, 2 * (half // 5), 2 * (half // 2), 2 * (half * 7 // 9), comps)
    spans = list(zip(cuts, cuts[1:]))
    odd = odd_place("gx")
    for side in range(2):

        @pl.when(odd == 1 - side)
        def _(side=side):
            kept = (2 * side, planes - 2)
            for i, (first, end) in enumerate(spans):
                for k in range(first // 2, end // 2):
                    pair(k)
                add_planes(
                    planes, tiles, work, dv_ref, lambda c, p: hb_ref[c, p], first, end, side
                )
                write_out(planes, tiles, work, out, sem.at[i], first, end, *kept).start()
            for i, (first, end) in enumerate(spans):
                write_out(planes, tiles, work, out, sem.at[i], first, end, *kept).wait()


def outer_edges_kernel(comps, planes, tiles, part_ref, dv_ref, h_ref, prev, work, out, sem):
    del part_ref, prev
    odd = odd_place("gx")

    def plane(c, p):
        return h_ref[pl.ds(c * 2 * tiles + p, tiles, stride=2), :]

    bounds = [0, comps // 3, comps * 3 // 4, comps]
    spans = list(zip(bounds, bounds[1:]))
    for side in range(2):

        @pl.when(odd == side)
        def _(side=side):
            kept = (side * (planes - 2), 2)
            for i, (first, last) in enumerate(spans):
                add_planes(planes, tiles, work, dv_ref, plane, first, last, side)
                write_out(planes, tiles, work, out, sem.at[i], first, last, *kept).start()
            for i, (first, last) in enumerate(spans):
                write_out(planes, tiles, work, out, sem.at[i], first, last, *kept).wait()


def per_device(
    state, diffusivity, log_prefactor, activation, heat, reactants, products, substeps, flame
):
    comps, planes, cells = state.shape
    tiles = cells // LANES
    rows = planes * tiles
    nreact = log_prefactor.shape[0]
    gx, gy = lax.axis_size("gx"), lax.axis_size("gy")
    f32 = jnp.float32
    flat = (
        state.reshape(comps, planes, tiles, LANES)
        .transpose(0, 2, 1, 3)
        .reshape(comps * rows, LANES)
    )

    def stay(array):
        return pltpu.with_memory_space_constraint(array, pltpu.HBM)

    vmem = pl.BlockSpec(memory_space=VMEM)
    anywhere = pl.BlockSpec(memory_space=pl.ANY)

    hbm = pl.BlockSpec(memory_space=pltpu.HBM)
    sds = jax.ShapeDtypeStruct
    ahead = pl.pallas_call(
        functools.partial(ahead_kernel, comps, planes, tiles),
        out_shape=sds((comps * tiles, 2, LANES), f32),
        in_specs=[hbm],
        out_specs=vmem,
        scratch_shapes=[pltpu.SemaphoreType.DMA((1,))],
        compiler_params=params(8),
        name="ahead",
    )(stay(flat.reshape(comps * tiles, planes // 2, 2, LANES)))
    beside, low, high = pl.pallas_call(
        functools.partial(pack_kernel, comps, planes, tiles),
        out_shape=(
            sds((comps, 2, tiles, LANES), f32),
            sds((comps // 2, planes, LANES), f32),
            sds((comps // 2, planes, LANES), f32),
        ),
        in_specs=[vmem],
        out_specs=[vmem] * 3,
        compiler_params=params(16),
        name="pack",
    )(flat)

    outer = [(i, (i + 1) % gx) for i in range(1, gx, 2)]
    outer = outer + [(t, s) for s, t in outer]
    inner = [(i, i + 1) for i in range(0, gx, 2)]
    inner = inner + [(t, s) for s, t in inner]
    forward = [(i, (i + 1) % gy) for i in range(gy)]
    backward = [(t, s) for s, t in forward]
    ha = lax.ppermute(ahead, "gx", outer)
    hb = lax.ppermute(beside, "gx", inner)
    zl = lax.ppermute(high, "gy", forward)
    zh = lax.ppermute(low, "gy", backward)

    padded = pl.cdiv(nreact, LANES) * LANES
    wide = pl.cdiv(nreact, 16) * 16
    part, dv = pl.pallas_call(
        functools.partial(main_kernel, comps, planes, tiles, nreact),
        out_shape=(sds((comps * rows, LANES), f32), sds((comps * planes, LANES), f32)),
        in_specs=[vmem, vmem] + [hbm] * 8,
        out_specs=(vmem, vmem),
        scratch_shapes=[
            SMEM((comps,), f32),
            SMEM(substeps.shape, jnp.int32),
            SMEM(flame.shape, jnp.int32),
            VMEM((nreact,), f32),
            VMEM((nreact,), f32),
            VMEM((nreact,), f32),
            VMEM((comps - 1, 2 * nreact), f32),
            VMEM((comps - 1, nreact), f32),
            VMEM((PIECE, padded), f32),
            VMEM((2 * PIECE, padded), f32),
            VMEM((wide, 3 * PIECE), jnp.bfloat16),
            VMEM((2 * PIECE, 2 * padded), jnp.bfloat16),
            VMEM((PIECE, GROUP * LANES), f32),
            VMEM((PIECE, GROUP * LANES), f32),
            VMEM((1, GROUP * LANES), f32),
            VMEM((1, GROUP * LANES), f32),
            VMEM((many_of(comps) * rows, 2 * LANES), f32),
            VMEM((many_of(comps) * rows, 2 * LANES), f32),
            VMEM((many_of(comps) * rows, 2 * LANES), f32),
            SMEM((rows + 1,), jnp.int32),
            pltpu.SemaphoreType.DMA((8,)),
        ],
        compiler_params=params(24),
        cost_estimate=pl.CostEstimate(
            flops=2_000_000_000, bytes_accessed=16_000_000, transcendentals=1_000_000
        ),
        name="main",
    )(
        flat,
        shift_matrix(),
        *map(
            stay,
            (
                diffusivity,
                substeps,
                flame,
                log_prefactor,
                activation,
                heat,
                reactants.T,
                products,
            ),
        ),
    )

    whole = sds((comps * rows, LANES), f32)
    cost = pl.CostEstimate(flops=1_000_000, bytes_accessed=3_000_000, transcendentals=0)
    part, out = pl.pallas_call(
        functools.partial(inner_edges_kernel, comps, planes, tiles),
        out_shape=(whole, whole),
        in_specs=[vmem] * 5,
        out_specs=(vmem, anywhere),
        scratch_shapes=[pltpu.SemaphoreType.DMA((4,))],
        input_output_aliases={0: 0},
        compiler_params=params(16),
        cost_estimate=cost,
        name="inner_edges",
    )(part, dv, hb, zl, zh)
    _, out = pl.pallas_call(
        functools.partial(outer_edges_kernel, comps, planes, tiles),
        out_shape=(whole, whole),
        in_specs=[vmem] * 3 + [anywhere],
        out_specs=(vmem, anywhere),
        scratch_shapes=[pltpu.SemaphoreType.DMA((3,))],
        input_output_aliases={0: 0, 3: 1},
        compiler_params=params(16),
        cost_estimate=cost,
        name="outer_edges",
    )(part, dv, ha.reshape(comps * tiles * 2, LANES), out)
    return (
        out.reshape(comps, tiles, planes, LANES).transpose(0, 2, 1, 3).reshape(comps, planes, cells)
    )


def solution(mesh):
    in_specs = (P(None, "gx", "gy"), P(), P(), P(), P(), P(), P(), P("gx", "gy"), P("gx", "gy"))
    out_specs = P(None, "gx", "gy")

    return jax.shard_map(
        per_device, mesh=mesh, in_specs=in_specs, out_specs=out_specs, check_vma=False
    )
```
